32 devices in a mesh: req: 8 (over z, x), tp: 4 (over y, core).
Axes of the slice: x: 2, y: 2, z: 4, core: 2. Of those that a mesh axis runs over, the one named last changes fastest.
Arguments:
- tokens: bfloat16 [4096, 1024], P('req', 'tp'), may hold values from -17.5 to 17.5
- prompt_lengths: int32 [64, 4], P('req'), may hold values from 1 to 32, 64 in all within a row
- adapter_ids: int32 [64, 4], P('req'), may hold values from 0 to 15, as said below
- adapter_slot: int32 [16], replicated, may hold values from 0 to 15, as said below
- w_qkv: bfloat16 [3, 1024, 1024], P(None, None, 'tp'), may hold values from -0.1875 to 0.1875
- w_out: bfloat16 [1024, 1024], P('tp'), may hold values from -0.1875 to 0.1875
- w_fc1: bfloat16 [1024, 4096], P(None, 'tp'), may hold values from -0.1875 to 0.1875
- w_fc2: bfloat16 [4096, 1024], P('tp'), may hold values from -0.09375 to 0.09375
- qkv_down: bfloat16 [3, 1024, 256], P(None, None, 'req'), may hold values from -0.1875 to 0.1875
- qkv_up: bfloat16 [3, 256, 1024], P(None, 'req', 'tp'), may hold values from -0.75 to 0.75
- out_down: bfloat16 [1024, 256], P('tp', 'req'), may hold values from -0.1875 to 0.1875
- out_up: bfloat16 [256, 1024], P('req'), may hold values from -0.75 to 0.75
- fc1_down: bfloat16 [1024, 256], P(None, 'req'), may hold values from -0.1875 to 0.1875
- fc1_up: bfloat16 [256, 4096], P('req', 'tp'), may hold values from -0.75 to 0.75
- fc2_down: bfloat16 [4096, 256], P('tp', 'req'), may hold values from -0.09375 to 0.09375
- fc2_up: bfloat16 [256, 1024], P('req'), may hold values from -0.75 to 0.75
- norm1_gain: float32 [1024], replicated, may hold values from 0.5 to 1.5
- norm1_bias: float32 [1024], replicated, may hold values from -1.75 to 1.75
- norm2_gain: float32 [1024], replicated, may hold values from 0.5 to 1.5
- norm2_bias: float32 [1024], replicated, may hold values from -1.75 to 1.75
Outputs:
- layer_out: bfloat16 [4096, 1024], P('req', 'tp')
The draws below stay inside these ranges and needn't reach their ends.
Inputs may be any that keep to these rules, and one draw needn't show every extreme that they name: `prompt_lengths`: each row sums to 64, and its longest request has exactly 32 tokens. A permutation: adapter i is stored in slot adapter_slot[i] of the adapter arrays, and slot s lies on index s // 2 of req (its owner). `adapter_ids`: all requests of one block use adapters of one owner; the 8 blocks of one index of req use 8 different owners; the first block of every index of req uses one common owner.
All inputs are finite; a program needn't handle non-finite values.
Results may differ from the reference program's by a relative error of at most 0.015.
The reference program's roundings to bfloat16 on the way count: a program that leaves them out, or rounds other values in their place, can miss the bound.
Values may be sent and summed in bfloat16 or wider, within the bound.
No kernel may reach another device: no remote copies, remote signals or barrier semaphores. Data moves between devices by JAX's collectives and lax.ppermute only.
A program may use at most 64 MiB of HBM per device.

```python
import math
import jax
import jax.numpy as jnp
import numpy as np
from jax import lax

D = 1024
HEADS = 16
HEAD_DIM = 64
FF = 4096
RANK = 16
ADAPT_DEV = 2
CAP = 64
SEQ_G = 4
G_DEV = 8
MAXLEN = 32
BLOCKS = 64
TOKENS = 4096
ADAPTERS = 16
N_TP = 4


def joint_routes(key):
    owner_total = ADAPTERS // ADAPT_DEV
    slot_table = jax.random.permutation(jax.random.fold_in(key, 101), ADAPTERS).astype(jnp.int32)
    hot_owner = jax.random.randint(jax.random.fold_in(key, 102), (), 0, owner_total)
    rotation = jax.random.randint(jax.random.fold_in(key, 103), (owner_total, 1), 0, owner_total - 1)
    block_idx = jnp.arange(G_DEV, dtype=jnp.int32)[None, :]
    spread = (hot_owner + 1 + (block_idx - 1 + rotation) % (owner_total - 1)) % owner_total
    target = jnp.where(block_idx == 0, hot_owner, spread)
    local_pick = jax.random.randint(jax.random.fold_in(key, 104), (owner_total, G_DEV, SEQ_G), 0, ADAPT_DEV)
    slot_need = target[:, :, None] * ADAPT_DEV + local_pick
    inverse = jnp.argsort(slot_table, stable=True).astype(jnp.int32)
    chosen_ids = inverse[slot_need.reshape(-1)].reshape(owner_total * G_DEV, SEQ_G)
    return (slot_table, chosen_ids.astype(jnp.int32))


def draw_adapter_slot(key, part):
    return joint_routes(key)[0]


def draw_adapter_ids(key, part):
    return joint_routes(key)[1]


def draw_tokens(key, part):
    values = jnp.clip(jax.random.normal(key, (TOKENS, D), jnp.float32), -6.0, 6.0)
    return values.astype(jnp.bfloat16)


def block_levels(stream_key, shape, shards, smallest, high):
    def one(dim, shards_of):
        steps = jax.random.uniform(jax.random.fold_in(jax.random.fold_in(stream_key, 6), dim), (shards_of,), jnp.float32, smallest / len(shards), high / len(shards))
        return jnp.repeat(jnp.exp(steps), shape[dim] // shards_of).reshape((-1,) + (1,) * (len(shape) - dim - 1))

    gain = one(*shards[0])
    for cut in shards[1:]:
        gain = gain * one(*cut)
    return gain


def length_profile(number_of, total, reach, skew):
    weights = [(1 << 20) // math.isqrt(grade ** skew) + 1 for grade in range(2, number_of + 1)]
    spare, given = total - reach - (number_of - 1), [1] * (number_of - 1)
    while spare > 0:
        candidates = [i for i in range(number_of - 1) if given[i] < reach]
        pool, budget = sum([weights[i] for i in candidates]), spare
        for i in candidates:
            more = min(reach - given[i], max(1, budget * weights[i] // pool), spare)
            given[i] = given[i] + more
            spare = spare - more
    return np.array([reach] + given)


def ragged(stream_key, amount, total, most, slope):
    if amount == 2:
        one = jax.random.randint(stream_key, (), max(1, total - most), min(most, total - 1) + 1)
        return jnp.stack([one, total - one])
    lengths = jnp.asarray(length_profile(amount, total, most, slope), jnp.int32)
    pairs = (amount - 1) // 2
    giver, taker = lengths[1:1 + 2 * pairs:2], lengths[2:2 + 2 * pairs:2]
    margin = jnp.minimum(giver - 1, most - taker)
    moved = jax.random.randint(jax.random.fold_in(stream_key, 1), (pairs,), 0, 1 << 20) % (margin + 1)
    lengths = lengths.at[1:1 + 2 * pairs:2].set(giver - moved).at[2:2 + 2 * pairs:2].set(taker + moved)
    return lengths[jax.random.permutation(jax.random.fold_in(stream_key, 2), amount)]


def normal_values(own_key, extent, scale, limit, shards=(), kind=jnp.bfloat16):
    array = scale * jax.random.normal(own_key, extent, jnp.float32)
    if shards:
        array = array * block_levels(own_key, extent, shards, -0.22, 0.18)
    return jnp.clip(array, -limit, limit).astype(kind)


def setup_inputs(seed: int = 0) -> dict:
    arg_keys = jax.random.split(jax.random.key(seed), 21)
    tokens = draw_tokens(jax.random.fold_in(arg_keys[20], 71), 0)
    prompt_lengths = jax.vmap(lambda own: ragged(own, SEQ_G, CAP, MAXLEN, 1))(jax.random.split(arg_keys[1], BLOCKS)).reshape((BLOCKS, SEQ_G)).astype(jnp.int32)
    adapter_ids = draw_adapter_ids(jax.random.fold_in(arg_keys[20], 71), 0)
    adapter_slot = draw_adapter_slot(jax.random.fold_in(arg_keys[20], 71), 0)
    w_qkv = normal_values(arg_keys[4], (3, D, D), D ** -0.5, 0.1875, ((2, 4),))
    w_out = normal_values(arg_keys[5], (D, D), D ** -0.5, 0.1875, ((0, 4),))
    w_fc1 = normal_values(arg_keys[6], (D, FF), D ** -0.5, 0.1875, ((1, 4),))
    w_fc2 = normal_values(arg_keys[7], (FF, D), FF ** -0.5, 0.09375, ((0, 4),))
    qkv_down = normal_values(arg_keys[8], (3, D, ADAPTERS * RANK), D ** -0.5, 0.1875, ((2, 8),))
    qkv_up = normal_values(arg_keys[9], (3, ADAPTERS * RANK, D), (4 * RANK) ** -0.5, 0.75, ((1, 8), (2, 4)))
    out_down = normal_values(arg_keys[10], (D, ADAPTERS * RANK), D ** -0.5, 0.1875, ((0, 4), (1, 8)))
    out_up = normal_values(arg_keys[11], (ADAPTERS * RANK, D), (4 * RANK) ** -0.5, 0.75, ((0, 8),))
    fc1_down = normal_values(arg_keys[12], (D, ADAPTERS * RANK), D ** -0.5, 0.1875, ((1, 8),))
    fc1_up = normal_values(arg_keys[13], (ADAPTERS * RANK, FF), (4 * RANK) ** -0.5, 0.75, ((0, 8), (1, 4)))
    fc2_down = normal_values(arg_keys[14], (FF, ADAPTERS * RANK), FF ** -0.5, 0.09375, ((0, 4), (1, 8)))
    fc2_up = normal_values(arg_keys[15], (ADAPTERS * RANK, D), (4 * RANK) ** -0.5, 0.75, ((0, 8),))
    norm1_gain = jnp.clip(1.0 + 0.1 * jax.random.normal(arg_keys[16], (D,), jnp.float32), 0.5, 1.5)
    norm1_bias = normal_values(arg_keys[17], (D,), 0.3, 1.75, (), jnp.float32)
    norm2_gain = jnp.clip(1.0 + 0.1 * jax.random.normal(arg_keys[18], (D,), jnp.float32), 0.5, 1.5)
    norm2_bias = normal_values(arg_keys[19], (D,), 0.3, 1.75, (), jnp.float32)
    return {"tokens": tokens, "prompt_lengths": prompt_lengths, "adapter_ids": adapter_ids, "adapter_slot": adapter_slot, "w_qkv": w_qkv, "w_out": w_out, "w_fc1": w_fc1, "w_fc2": w_fc2, "qkv_down": qkv_down, "qkv_up": qkv_up, "out_down": out_down, "out_up": out_up, "fc1_down": fc1_down, "fc1_up": fc1_up, "fc2_down": fc2_down, "fc2_up": fc2_up, "norm1_gain": norm1_gain, "norm1_bias": norm1_bias, "norm2_gain": norm2_gain, "norm2_bias": norm2_bias}


norm_eps = 1e-05

def layer_norm(values, gain_vec, shift_vec):
    row_mean = lax.optimization_barrier(jnp.mean(values, axis=-1, keepdims=True))
    centred = values - row_mean
    variance = lax.optimization_barrier(jnp.mean(centred * centred, axis=-1, keepdims=True))
    return centred * lax.rsqrt(variance + norm_eps) * gain_vec + shift_vec

def rounded(values):
    return lax.optimization_barrier(values.astype(jnp.bfloat16)).astype(jnp.float32)

def block_codes(prompt_lengths, adapter_ids, adapter_slot):
    id_table = jnp.arange(adapter_slot.shape[0], dtype=jnp.int32)
    slot_of_req = lax.optimization_barrier(jnp.sum(jnp.where(adapter_ids[..., None] == id_table, adapter_slot, 0), axis=-1)).astype(jnp.int32)
    owner_of = (slot_of_req[..., 0] // ADAPT_DEV).astype(jnp.int32)
    local_pick = (slot_of_req % ADAPT_DEV).astype(jnp.int32)
    request_end = jnp.cumsum(prompt_lengths, axis=-1).astype(jnp.int32)
    position = jnp.arange(CAP, dtype=jnp.int32)
    segment = lax.optimization_barrier(jnp.sum((position[:, None] >= request_end[..., None, :]).astype(jnp.int32), axis=-1)).astype(jnp.int32)
    chosen = segment[..., None] == jnp.arange(SEQ_G, dtype=jnp.int32)
    row_local = lax.optimization_barrier(jnp.sum(jnp.where(chosen, local_pick[..., None, :], 0), axis=-1)).astype(jnp.int32)
    return (owner_of, (1 + segment * ADAPT_DEV + row_local).astype(jnp.int32))

def reference(tokens, prompt_lengths, adapter_ids, adapter_slot, w_qkv, w_out, w_fc1, w_fc2, qkv_down, qkv_up, out_down, out_up, fc1_down, fc1_up, fc2_down, fc2_up, norm1_gain, norm1_bias, norm2_gain, norm2_bias):
    highest = lax.Precision.HIGHEST
    owner_of, row_codes = block_codes(prompt_lengths, adapter_ids, adapter_slot)
    qkv_full = w_qkv.astype(jnp.float32)
    out_groups = w_out.astype(jnp.float32).reshape(N_TP, D // N_TP, D)
    fc1_full = w_fc1.astype(jnp.float32)
    fc2_groups = w_fc2.astype(jnp.float32).reshape(N_TP, FF // N_TP, D)
    span_cols = ADAPT_DEV * RANK
    column_adapter = jnp.arange(span_cols, dtype=jnp.int32) // RANK

    def per_block(block_item):
        x_rows, owner_one, codes_one = block_item
        first_col = (owner_one * span_cols).astype(jnp.int32)
        qkv_dn = lax.dynamic_slice_in_dim(qkv_down, first_col, span_cols, 2).astype(jnp.float32)
        qkv_upper = lax.dynamic_slice_in_dim(qkv_up, first_col, span_cols, 1).astype(jnp.float32)
        out_dn = lax.dynamic_slice_in_dim(out_down, first_col, span_cols, 1).astype(jnp.float32).reshape(N_TP, D // N_TP, span_cols)
        out_upper = lax.dynamic_slice_in_dim(out_up, first_col, span_cols, 0).astype(jnp.float32)
        fc1_dn = lax.dynamic_slice_in_dim(fc1_down, first_col, span_cols, 1).astype(jnp.float32)
        fc1_upper = lax.dynamic_slice_in_dim(fc1_up, first_col, span_cols, 0).astype(jnp.float32)
        fc2_dn = lax.dynamic_slice_in_dim(fc2_down, first_col, span_cols, 1).astype(jnp.float32).reshape(N_TP, FF // N_TP, span_cols)
        fc2_upper = lax.dynamic_slice_in_dim(fc2_up, first_col, span_cols, 0).astype(jnp.float32)
        selector = (column_adapter[None, :] == ((codes_one - 1) % ADAPT_DEV)[:, None]).astype(jnp.float32)
        x_float = x_rows.astype(jnp.float32)
        projected = jnp.einsum('cd,kdo->kco', x_float, qkv_full)
        reduced = jnp.einsum('cd,kdr->kcr', x_float, qkv_dn) * selector
        lifted = jnp.einsum('kcr,kro->kco', reduced, qkv_upper, precision=highest)
        qkv = rounded(projected + lifted).reshape(3, CAP, HEADS, HEAD_DIM)
        scores = jnp.einsum('chd,ehd->hce', qkv[0], qkv[1]) * HEAD_DIM ** (-0.5)
        same_request = codes_one[:, None] == codes_one[None, :]
        scores = jnp.where(same_request[None], scores, -1e+30)
        row_max = lax.optimization_barrier(jnp.max(scores, axis=-1, keepdims=True))
        expo = jnp.exp(scores - row_max)
        attn_weights = rounded(expo / lax.optimization_barrier(jnp.sum(expo, axis=-1, keepdims=True)))
        attended = rounded(jnp.einsum('hce,ehd->chd', attn_weights, qkv[2]).reshape(CAP, D))
        groups = attended.reshape(CAP, N_TP, D // N_TP)
        out_terms = jnp.einsum('cjf,jfo->jco', groups, out_groups)
        out_low = jnp.einsum('cjf,jfr->jcr', groups, out_dn) * selector[None]
        out_terms = out_terms + jnp.einsum('jcr,ro->jco', out_low, out_upper, precision=highest)
        attn_sum = lax.optimization_barrier(jnp.sum(rounded(out_terms), axis=0))
        h1 = rounded(layer_norm(x_float + attn_sum, norm1_gain, norm1_bias))
        gate_in = jnp.dot(h1, fc1_full)
        fc1_low = jnp.dot(h1, fc1_dn) * selector
        gate_in = gate_in + jnp.dot(fc1_low, fc1_upper, precision=highest)
        hidden = rounded(jax.nn.gelu(gate_in, approximate=False))
        hidden_groups = hidden.reshape(CAP, N_TP, FF // N_TP)
        ffn_terms = jnp.einsum('cjf,jfo->jco', hidden_groups, fc2_groups)
        ffn_low = jnp.einsum('cjf,jfr->jcr', hidden_groups, fc2_dn) * selector[None]
        ffn_terms = ffn_terms + jnp.einsum('jcr,ro->jco', ffn_low, fc2_upper, precision=highest)
        ffn_sum = lax.optimization_barrier(jnp.sum(rounded(ffn_terms), axis=0))
        return layer_norm(h1 + ffn_sum, norm2_gain, norm2_bias).astype(jnp.bfloat16)
    blocks_in = tokens.reshape(BLOCKS, CAP, D)
    finished = lax.map(per_block, (blocks_in, owner_of, row_codes))
    return finished.reshape(TOKENS, D)
```

```python
import functools

import jax
import jax.numpy as jnp
from jax import lax
from jax.experimental import pallas as pl
from jax.experimental.pallas import tpu as pltpu
from jax.sharding import PartitionSpec as P

HEAD_DIM = 64
RANK = 16
ADAPT_DEV = 2
CAP = 64
SEQ_G = 4
SPAN = ADAPT_DEV * RANK
PAD = 8
NORM_EPS = 1e-05
BF = jnp.bfloat16
F32 = jnp.float32
VMEM_LIMIT = 56 * 1024 * 1024


def dot(a, b):
    return lax.dot_general(a, b, (((1,), (0,)), ((), ())), preferred_element_type=F32)


def dot_t(a, b):
    return lax.dot_general(a, b, (((1,), (1,)), ((), ())), preferred_element_type=F32)


def layer_norm(values, gain, shift):
    mean = jnp.mean(values, axis=-1, keepdims=True)
    centred = values - mean
    variance = jnp.mean(centred * centred, axis=-1, keepdims=True)
    return centred * lax.rsqrt(variance + NORM_EPS) * gain + shift


def split_low(low, sel):
    low = low * sel
    high = low.astype(BF).astype(F32)
    lane = lax.broadcasted_iota(jnp.int32, low.shape, 1)
    return jnp.where((lane // SPAN) % 2 == 0, high, low - high).astype(BF)


def pack_kernel(lengths, ids, slots, tok, out):
    blocks = tok.shape[0]
    if out.shape[0] > blocks:
        out[...] = jnp.zeros(out.shape, out.dtype)
    width = out.shape[2]
    pos = lax.broadcasted_iota(jnp.int32, (PAD, width), 1) % CAP
    for g in range(blocks):
        slot = [slots[ids[g, k]] for k in range(SEQ_G)]
        owner = slot[0] // ADAPT_DEV
        code = jnp.full((PAD, width), 1 + slot[0] % ADAPT_DEV, jnp.int32)
        end = jnp.int32(0)
        for k in range(1, SEQ_G):
            end = end + lengths[g, k - 1]
            code = jnp.where(pos >= end, 1 + k * ADAPT_DEV + slot[k] % ADAPT_DEV, code)
        out[owner, :CAP, :] = tok[g]
        out[owner, CAP:, :] = code.astype(F32).astype(BF)


def attn_kernel(n_tp, me, *refs):
    parts, (w, down, up, att, sel_out, x_full) = refs[:n_tp], refs[n_tp:]
    blocks = parts[0].shape[0]
    width = parts[0].shape[2]
    rows = blocks * CAP
    tp = me[0]
    for r in range(n_tp):
        start = pl.multiple_of((tp ^ r) * width, width)
        x_full[:, pl.ds(start, width)] = parts[r][:, :CAP, :].reshape(rows, width)
    x = x_full[...]
    pair_lane = lax.broadcasted_iota(jnp.int32, (2 * CAP, 2 * CAP), 1)
    pair_row = lax.broadcasted_iota(jnp.int32, (2 * CAP, 2 * CAP), 0)
    eye = pair_lane == pair_row
    lane_sel = lax.broadcasted_iota(jnp.int32, (2 * CAP, sel_out.shape[1]), 1)
    lane_sel = ((lane_sel // RANK) % ADAPT_DEV).astype(F32)
    masks, sels = [], []
    for p in range(blocks // 2):
        c0 = parts[0][2 * p, CAP : CAP + 1, : 2 * CAP].astype(F32)
        c1 = parts[0][2 * p + 1, CAP : CAP + 1, : 2 * CAP].astype(F32) + 64.0
        idr = jnp.where(pair_lane < CAP, c0, c1)
        idc = jnp.sum(jnp.where(eye, idr, 0.0), axis=1, keepdims=True)
        masks.append(idr == idc)
        pick = idc - 1.0
        pick = pick - 2.0 * jnp.floor(pick * 0.5)
        sels.append((lane_sel == pick).astype(F32))
    sel = jnp.concatenate(sels, axis=0)
    sel_out[...] = sel.astype(BF)
    low = split_low(dot(x, down[...]), jnp.concatenate([sel, sel], axis=1)[:, : 6 * SPAN])
    qkv = []
    for k in range(3):
        full = dot(x, w[k]) + dot(low[:, 2 * k * SPAN : 2 * (k + 1) * SPAN], up[k])
        qkv.append(full.astype(BF))
    q, k_, v = qkv
    q = (q.astype(F32) * HEAD_DIM**-0.5).astype(BF)
    first = pair_lane < HEAD_DIM
    zero = jnp.zeros((), BF)
    for p in range(blocks // 2):
        r0 = p * 2 * CAP
        for h in range(width // (2 * HEAD_DIM)):
            c0 = h * 2 * HEAD_DIM
            qq = q[r0 : r0 + 2 * CAP, c0 : c0 + 2 * HEAD_DIM]
            kk = k_[r0 : r0 + 2 * CAP, c0 : c0 + 2 * HEAD_DIM]
            vv = v[r0 : r0 + 2 * CAP, c0 : c0 + 2 * HEAD_DIM]
            both = []
            for half in (first, ~first):
                s = dot_t(jnp.where(half, qq, zero), kk)
                s = jnp.where(masks[p], s, -1e30)
                e = jnp.exp(s - jnp.max(s, axis=-1, keepdims=True))
                prob = (e / jnp.sum(e, axis=-1, keepdims=True)).astype(BF)
                both.append(dot(prob, vv))
            att[r0 : r0 + 2 * CAP, c0 : c0 + 2 * HEAD_DIM] = jnp.where(first, *both).astype(BF)


def ffn_kernel(n_tp, me, *refs):
    atts, wouts, odowns = refs[:n_tp], refs[n_tp : 2 * n_tp], refs[2 * n_tp : 3 * n_tp]
    (x, sel_in, oup, w1, d1, u1, w2, d2, u2, g1, b1, even, odd, h_own, h_scr) = refs[3 * n_tp :]
    rows, feat = x.shape
    blocks = rows // CAP
    share = CAP // n_tp
    tp = me[0]
    step = min(rows, 256)
    for r0 in range(0, rows, step):
        rs = slice(r0, r0 + step)
        nb = step // CAP
        sel = sel_in[rs].astype(F32)[:, : 2 * SPAN]
        total = x[rs].astype(F32)
        low = None
        for r in range(n_tp):
            a = atts[r][rs]
            total = total + dot(a, wouts[r][...])
            part = dot(a, odowns[r][...])
            low = part if low is None else low + part
        total = total + dot(split_low(low, sel), oup[...])
        h1 = layer_norm(total, g1[...], b1[...]).astype(BF)
        h_scr[r0 // CAP : r0 // CAP + nb] = h1.reshape(nb, n_tp, share, feat)
        gate = dot(h1, w1[...]) + dot(split_low(dot(h1, d1[...]), sel), u1[...])
        hidden = (0.5 * gate * (1.0 + lax.erf(gate * 0.7071067811865476))).astype(BF)
        term = dot(hidden, w2[...]) + dot(split_low(dot(hidden, d2[...]), sel), u2[...])
        term = term.reshape(nb, n_tp, share, feat)
        own_rows = slice(r0 // n_tp, (r0 + step) // n_tp)
        for j in range(n_tp):
            rel = tp ^ j
            piece = term[:, j].reshape(nb * share, feat)

            @pl.when(rel % 2 == 0)
            def _():
                even[rel // 2, own_rows, :] = piece

            @pl.when(rel % 2 == 1)
            def _():
                odd[rel // 2, own_rows, :] = piece.astype(BF)

    h_own[...] = h_scr[:, tp].reshape(blocks * share, feat)


def last_kernel(n_tp, even, got, *refs):
    arrived, (h_own, g2, b2, out) = refs[: n_tp // 2 - 1], refs[n_tp // 2 - 1 :]
    total = h_own[...].astype(F32) + (even[0] + got[0].astype(F32))
    for a in arrived:
        total = total + a[...].astype(F32)
    done = layer_norm(total, g2[...], b2[...]).astype(BF)
    n, _, share, width = out.shape
    for f in range(n_tp):
        out[:, f] = done[:, f * width : (f + 1) * width].reshape(n, share, width)


def unpack_kernel(ids, slots, arrived, out):
    for g in range(out.shape[0]):
        out[g] = arrived[slots[ids[g, 0]] // ADAPT_DEV]


def whole(shape):
    zeros = (0,) * len(shape)
    return pl.BlockSpec(tuple(shape), lambda *_: zeros)


SMEM = pl.BlockSpec(memory_space=pltpu.SMEM)


def params():
    return pltpu.CompilerParams(vmem_limit_bytes=VMEM_LIMIT)


def body(
    tokens,
    prompt_lengths,
    adapter_ids,
    adapter_slot,
    w_qkv,
    w_out,
    w_fc1,
    w_fc2,
    qkv_down,
    qkv_up,
    out_down,
    out_up,
    fc1_down,
    fc1_up,
    fc2_down,
    fc2_up,
    norm1_gain,
    norm1_bias,
    norm2_gain,
    norm2_bias,
):
    n_req = lax.axis_size("req")
    n_tp = lax.axis_size("tp")
    feat = w_qkv.shape[1]
    width = tokens.shape[1]
    blocks = tokens.shape[0] // CAP
    share = CAP // n_tp
    me = jnp.reshape(lax.axis_index("tp"), (1,)).astype(jnp.int32)

    def swap(value, r):
        return lax.ppermute(value, "tp", [(i, i ^ r) for i in range(n_tp)])

    def gather(value):
        far = [value] + [swap(value, 2 * y) for y in range(1, n_tp // 2)]
        found = []
        for piece in far:
            found += [piece, swap(piece, 1)]
        return found

    def twice(value, axis):
        return jnp.concatenate([value, value], axis=axis)

    packed = pl.pallas_call(
        pack_kernel,
        out_shape=jax.ShapeDtypeStruct((n_req, CAP + PAD, width), BF),
        in_specs=[SMEM, SMEM, SMEM, pl.BlockSpec(memory_space=pltpu.VMEM)],
        out_specs=pl.BlockSpec(memory_space=pltpu.VMEM),
        name="pack",
    )(prompt_lengths, adapter_ids, adapter_slot, tokens.reshape(blocks, CAP, width))
    arrived = lax.all_to_all(packed, "req", split_axis=0, concat_axis=0, tiled=True)
    parts = gather(arrived)
    wouts = gather(w_out)
    odowns = gather(twice(out_down, 1))

    step_blocks = min(n_req, 8)
    steps = n_req // step_blocks
    step_rows = step_blocks * CAP
    rows = n_req * CAP

    def by_rows(cols):
        return pl.BlockSpec((step_rows, cols), lambda i: (i, 0))

    down = jnp.transpose(twice(qkv_down, 2), (1, 0, 2)).reshape(feat, 6 * SPAN)
    up = twice(qkv_up, 1)
    attended, sel, x_full = pl.pallas_call(
        functools.partial(attn_kernel, n_tp),
        grid=(steps,),
        out_shape=(
            jax.ShapeDtypeStruct((rows, width), BF),
            jax.ShapeDtypeStruct((rows, 4 * SPAN), BF),
            jax.ShapeDtypeStruct((rows, feat), BF),
        ),
        in_specs=[SMEM]
        + [pl.BlockSpec((step_blocks, CAP + PAD, width), lambda i: (i, 0, 0))] * n_tp
        + [whole(w_qkv.shape), whole(down.shape), whole(up.shape)],
        out_specs=(by_rows(width), by_rows(4 * SPAN), by_rows(feat)),
        compiler_params=params(),
        name="attend",
    )(me, *parts, w_qkv, down, up)

    atts = gather(attended)
    oup, u1, u2 = twice(out_up, 0), twice(fc1_up, 0), twice(fc2_up, 0)
    d1, d2 = twice(fc1_down, 1), twice(fc2_down, 1)
    g1, b1 = norm1_gain[None], norm1_bias[None]
    half = n_tp // 2
    own = rows // n_tp
    step_own = step_rows // n_tp
    consts = [oup, w_fc1, d1, u1, w_fc2, d2, u2, g1, b1]
    even, odd, h_own = pl.pallas_call(
        functools.partial(ffn_kernel, n_tp),
        grid=(steps,),
        out_shape=(
            jax.ShapeDtypeStruct((half, own, feat), F32),
            jax.ShapeDtypeStruct((half, own, feat), BF),
            jax.ShapeDtypeStruct((own, feat), BF),
        ),
        in_specs=[SMEM]
        + [by_rows(width)] * n_tp
        + [whole(w.shape) for w in wouts + odowns]
        + [by_rows(feat), by_rows(4 * SPAN)]
        + [whole(c.shape) for c in consts],
        out_specs=(
            pl.BlockSpec((half, step_own, feat), lambda i: (0, i, 0)),
            pl.BlockSpec((half, step_own, feat), lambda i: (0, i, 0)),
            pl.BlockSpec((step_own, feat), lambda i: (i, 0)),
        ),
        scratch_shapes=[pltpu.VMEM((step_blocks, n_tp, share, feat), BF)],
        compiler_params=params(),
        name="feed",
    )(me, *atts, *wouts, *odowns, x_full, sel, *consts)

    got = swap(odd, 1)
    sums = [
        swap((even[y] + got[y].astype(F32)).astype(BF), 2 * y) for y in range(1, half)
    ]
    vm = pl.BlockSpec(memory_space=pltpu.VMEM)
    done = pl.pallas_call(
        functools.partial(last_kernel, n_tp),
        out_shape=jax.ShapeDtypeStruct((n_req, n_tp, share, width), BF),
        in_specs=[vm] * (5 + len(sums)),
        out_specs=vm,
        compiler_params=params(),
        name="finish",
    )(even, got, *sums, h_own, norm2_gain[None], norm2_bias[None])
    back = lax.all_to_all(
        done.reshape(n_req * n_tp, share, width),
        ("req", "tp"),
        split_axis=0,
        concat_axis=0,
        tiled=True,
    )
    result = pl.pallas_call(
        unpack_kernel,
        out_shape=jax.ShapeDtypeStruct((blocks, CAP, width), BF),
        in_specs=[SMEM, SMEM, vm],
        out_specs=vm,
        name="unpack",
    )(adapter_ids, adapter_slot, back.reshape(n_req, CAP, width))
    return result.reshape(blocks * CAP, width)


def solution(mesh):
    placed = (
        P("req", "tp"),
        P("req", None),
        P("req", None),
        P(),
        P(None, None, "tp"),
        P("tp", None),
        P(None, "tp"),
        P("tp", None),
        P(None, None, "req"),
        P(None, "req", "tp"),
        P("tp", "req"),
        P("req", None),
        P(None, "req"),
        P("req", "tp"),
        P("tp", "req"),
        P("req", None),
        P(),
        P(),
        P(),
        P(),
    )
    return jax.shard_map(
        body, mesh=mesh, in_specs=placed, out_specs=P("req", "tp"), check_vma=False
    )
```

```python
import functools

import jax
import jax.numpy as jnp
from jax import lax
from jax.experimental import pallas as pl
from jax.experimental.pallas import tpu as pltpu
from jax.sharding import PartitionSpec as P

HEAD_DIM = 64
RANK = 16
ADAPT_DEV = 2
CAP = 64
SEQ_G = 4
SPAN = ADAPT_DEV * RANK
PAD = 8
NORM_EPS = 1e-05
BF = jnp.bfloat16
F32 = jnp.float32
VMEM_LIMIT = 56 * 1024 * 1024


def dot(a, b):
    return lax.dot_general(a, b, (((1,), (0,)), ((), ())), preferred_element_type=F32)


def dot_t(a, b):
    return lax.dot_general(a, b, (((1,), (1,)), ((), ())), preferred_element_type=F32)


def layer_norm(values, gain, shift):
    mean = jnp.mean(values, axis=-1, keepdims=True)
    centred = values - mean
    variance = jnp.mean(centred * centred, axis=-1, keepdims=True)
    return centred * lax.rsqrt(variance + NORM_EPS) * gain + shift


def split_low(low, sel):
    low = low * sel
    high = low.astype(BF).astype(F32)
    return jnp.concatenate([high, low - high], axis=1).astype(BF)


def pack_kernel(n_y, lengths_in, ids_in, slots, tok, out, owners, lengths, ids, sems):
    copies = [
        pltpu.make_async_copy(lengths_in, lengths, sems.at[0]),
        pltpu.make_async_copy(ids_in, ids, sems.at[1]),
    ]
    for c in copies:
        c.start()
    blocks = tok.shape[0]
    if out.shape[0] > blocks:
        out[...] = jnp.zeros(out.shape, out.dtype)
    width = out.shape[3]
    pos = lax.broadcasted_iota(jnp.int32, (PAD, width), 1) % CAP
    for c in copies:
        c.wait()
    for g in range(blocks):
        slot = [slots[ids[g, k]] for k in range(SEQ_G)]
        owner = slot[0] // ADAPT_DEV
        owners[g] = owner
        code = jnp.full((PAD, width), 1 + slot[0] % ADAPT_DEV, jnp.int32)
        end = jnp.int32(0)
        for k in range(1, SEQ_G):
            end = end + lengths[g, k - 1]
            code = jnp.where(pos >= end, 1 + k * ADAPT_DEV + slot[k] % ADAPT_DEV, code)
        code = code.astype(F32).astype(BF)
        for y in range(n_y):
            out[owner, y, :CAP, :] = tok[g]
            out[owner, y, CAP:, :] = code


def attn_kernel(n_y, me, mine, other, w, down, up, att, sel_out, x_full, up_all):
    blocks = mine.shape[0]
    width = mine.shape[3]
    rows = blocks * CAP
    core = me[0] % 2
    for y in range(n_y):
        for piece, c in ((mine, core), (other, 1 - core)):
            start = pl.multiple_of((2 * y + c) * width, width)
            x_full[:, pl.ds(start, width)] = piece[:, y, :CAP, :].reshape(rows, width)
    up_all[...] = jnp.zeros(up_all.shape, BF)
    for k in range(3):
        for part in range(2):
            first_row = (3 * part + k) * SPAN
            up_all[first_row : first_row + SPAN, k * width : (k + 1) * width] = up[k]
    downs = jnp.concatenate([down[0], down[1], down[2]], axis=1)
    pair_lane = lax.broadcasted_iota(jnp.int32, (2 * CAP, 2 * CAP), 1)
    pair_row = lax.broadcasted_iota(jnp.int32, (2 * CAP, 2 * CAP), 0)
    eye = pair_lane == pair_row
    lane_sel = ((pair_lane // RANK) % ADAPT_DEV).astype(F32)
    first = pair_lane < HEAD_DIM
    zero = jnp.zeros((), BF)
    tile = min(4, blocks)
    for t in range(blocks // tile):
        base = t * tile * CAP
        masks, sels = [], []
        for p in range(t * tile // 2, (t + 1) * tile // 2):
            c0 = mine[2 * p, 0, CAP : CAP + 1, : 2 * CAP].astype(F32)
            c1 = mine[2 * p + 1, 0, CAP : CAP + 1, : 2 * CAP].astype(F32) + 64.0
            idr = jnp.where(pair_lane < CAP, c0, c1)
            idc = jnp.sum(jnp.where(eye, idr, 0.0), axis=1, keepdims=True)
            masks.append(idr == idc)
            pick = idc - 1.0
            pick = pick - 2.0 * jnp.floor(pick * 0.5)
            sels.append((lane_sel == pick).astype(F32))
        sel = jnp.concatenate(sels, axis=0)
        rs = slice(base, base + tile * CAP)
        sel_out[rs] = sel.astype(BF)
        x = x_full[rs]
        low = split_low(dot(x, downs), sel[:, : 3 * SPAN])
        q, k_, v = [
            dot(x, w[k]) + dot(low, up_all[:, k * width : (k + 1) * width]) for k in range(3)
        ]
        q = (q.astype(BF).astype(F32) * HEAD_DIM**-0.5).astype(BF)
        k_, v = k_.astype(BF), v.astype(BF)
        for p in range(tile // 2):
            prs = slice(p * 2 * CAP, (p + 1) * 2 * CAP)
            out_rows = slice(base + p * 2 * CAP, base + (p + 1) * 2 * CAP)
            for h in range(width // (2 * HEAD_DIM)):
                cs = slice(h * 2 * HEAD_DIM, (h + 1) * 2 * HEAD_DIM)
                both = []
                for half in (first, ~first):
                    s = dot_t(jnp.where(half, q[prs, cs], zero), k_[prs, cs])
                    s = jnp.where(masks[p], s, -1e30)
                    e = jnp.exp(s - jnp.max(s, axis=-1, keepdims=True))
                    inv = 1.0 / jnp.sum(e, axis=-1, keepdims=True)
                    both.append(dot((e * inv).astype(BF), v[prs, cs]))
                att[out_rows, cs] = jnp.where(first, *both).astype(BF)


def ffn_kernel(n_tp, me, *refs):
    atts, wouts, odowns = refs[:n_tp], refs[n_tp : 2 * n_tp], refs[2 * n_tp : 3 * n_tp]
    (x, sel_in, oup, w1, d1, u1, w2, d2, u2, g1, b1, even, odd, h_own, h_scr) = refs[3 * n_tp :]
    rows, feat = x.shape
    blocks = rows // CAP
    share = CAP // n_tp
    tp = me[0]
    step = min(rows, 256)
    ups = [jnp.concatenate([u[...], u[...]], axis=0) for u in (oup, u1, u2)]
    for r0 in range(0, rows, step):
        rs = slice(r0, r0 + step)
        nb = step // CAP
        sel = sel_in[rs].astype(F32)[:, :SPAN]
        total = x[rs].astype(F32)
        low = None
        for r in range(n_tp):
            a = atts[r][rs]
            total = total + dot(a, wouts[r][...])
            part = dot(a, odowns[r][...])
            low = part if low is None else low + part
        total = total + dot(split_low(low, sel), ups[0])
        h1 = layer_norm(total, g1[...], b1[...]).astype(BF)
        h_scr[r0 // CAP : r0 // CAP + nb] = h1.reshape(nb, n_tp, share, feat)
        gate = dot(h1, w1[...]) + dot(split_low(dot(h1, d1[...]), sel), ups[1])
        hidden = (0.5 * gate * (1.0 + lax.erf(gate * 0.7071067811865476))).astype(BF)
        term = dot(hidden, w2[...]) + dot(split_low(dot(hidden, d2[...]), sel), ups[2])
        term = term.reshape(nb, n_tp, share, feat)
        own_rows = slice(r0 // n_tp, (r0 + step) // n_tp)
        for j in range(n_tp):
            rel = tp ^ j
            piece = term[:, j].reshape(nb * share, feat)

            @pl.when(rel % 2 == 0)
            def _():
                even[rel // 2, own_rows, :] = piece

            @pl.when(rel % 2 == 1)
            def _():
                odd[rel // 2, own_rows, :] = piece.astype(BF)

    h_own[...] = h_scr[:, tp].reshape(blocks * share, feat)


def last_kernel(n_tp, even, got, *refs):
    arrived, (h_own, g2, b2, out) = refs[: n_tp // 2 - 1], refs[n_tp // 2 - 1 :]
    total = h_own[...].astype(F32) + (even[0] + got[0].astype(F32))
    for a in arrived:
        total = total + a[...].astype(F32)
    done = layer_norm(total, g2[...], b2[...]).astype(BF)
    n, _, share, width = out.shape
    for f in range(n_tp):
        out[:, f] = done[:, f * width : (f + 1) * width].reshape(n, share, width)


def unpack_kernel(owners, arrived, out, sems):
    copies = [
        pltpu.make_async_copy(arrived.at[owners[g]], out.at[g], sems.at[g])
        for g in range(out.shape[0])
    ]
    for c in copies:
        c.start()
    for c in copies:
        c.wait()


def whole(shape):
    zeros = (0,) * len(shape)
    return pl.BlockSpec(tuple(shape), lambda *_: zeros)


vm = pl.BlockSpec(memory_space=pltpu.VMEM)
ANY = pl.BlockSpec(memory_space=pl.ANY)
SMEM = pl.BlockSpec(memory_space=pltpu.SMEM)


def params():
    return pltpu.CompilerParams(vmem_limit_bytes=VMEM_LIMIT)


def body(
    tokens,
    prompt_lengths,
    adapter_ids,
    adapter_slot,
    w_qkv,
    w_out,
    w_fc1,
    w_fc2,
    qkv_down,
    qkv_up,
    out_down,
    out_up,
    fc1_down,
    fc1_up,
    fc2_down,
    fc2_up,
    norm1_gain,
    norm1_bias,
    norm2_gain,
    norm2_bias,
):
    n_req = lax.axis_size("req")
    n_tp = lax.axis_size("tp")
    feat = w_qkv.shape[1]
    width = tokens.shape[1]
    blocks = tokens.shape[0] // CAP
    share = CAP // n_tp
    half = n_tp // 2
    me = jnp.reshape(lax.axis_index("tp"), (1,)).astype(jnp.int32)

    def swap(value, r):
        return lax.ppermute(value, "tp", [(i, i ^ r) for i in range(n_tp)])

    def gather(value):
        far = [value] + [swap(value, 2 * y) for y in range(1, n_tp // 2)]
        found = []
        for piece in far:
            found += [piece, swap(piece, 1)]
        return found

    groups = [
        [(r * half + y) * 2 + c for r in range(n_req) for y in range(half)] for c in range(2)
    ]
    packed, owners = pl.pallas_call(
        functools.partial(pack_kernel, half),
        out_shape=(
            jax.ShapeDtypeStruct((n_req, half, CAP + PAD, width), BF),
            jax.ShapeDtypeStruct((blocks,), jnp.int32),
        ),
        in_specs=[ANY, ANY, SMEM, vm],
        out_specs=(vm, SMEM),
        scratch_shapes=[
            pltpu.SMEM(prompt_lengths.shape, jnp.int32),
            pltpu.SMEM(adapter_ids.shape, jnp.int32),
            pltpu.SemaphoreType.DMA((2,)),
        ],
        name="pack",
    )(prompt_lengths, adapter_ids, adapter_slot, tokens.reshape(blocks, CAP, width))
    mine = lax.all_to_all(
        packed.reshape(n_req * half, CAP + PAD, width),
        ("req", "tp"),
        split_axis=0,
        concat_axis=0,
        tiled=True,
        axis_index_groups=groups,
    ).reshape(n_req, half, CAP + PAD, width)
    other = swap(mine, 1)
    wouts = gather(w_out)
    odowns = gather(out_down)

    step_blocks = min(n_req, 8)
    steps = n_req // step_blocks
    step_rows = step_blocks * CAP
    rows = n_req * CAP

    def by_rows(cols):
        return pl.BlockSpec((step_rows, cols), lambda i: (i, 0))

    by_block = pl.BlockSpec((step_blocks, half, CAP + PAD, width), lambda i: (i, 0, 0, 0))
    attended, sel, x_full = pl.pallas_call(
        functools.partial(attn_kernel, half),
        grid=(steps,),
        out_shape=(
            jax.ShapeDtypeStruct((rows, width), BF),
            jax.ShapeDtypeStruct((rows, 4 * SPAN), BF),
            jax.ShapeDtypeStruct((rows, feat), BF),
        ),
        in_specs=[SMEM, by_block, by_block]
        + [whole(w_qkv.shape), whole(qkv_down.shape), whole(qkv_up.shape)],
        out_specs=(by_rows(width), by_rows(4 * SPAN), by_rows(feat)),
        scratch_shapes=[pltpu.VMEM((6 * SPAN, 3 * width), BF)],
        compiler_params=params(),
        name="attend",
    )(me, mine, other, w_qkv, qkv_down, qkv_up)

    atts = gather(attended)
    g1, b1 = norm1_gain[None], norm1_bias[None]
    own = rows // n_tp
    step_own = step_rows // n_tp
    consts = [out_up, w_fc1, fc1_down, fc1_up, w_fc2, fc2_down, fc2_up, g1, b1]
    even, odd, h_own = pl.pallas_call(
        functools.partial(ffn_kernel, n_tp),
        grid=(steps,),
        out_shape=(
            jax.ShapeDtypeStruct((half, own, feat), F32),
            jax.ShapeDtypeStruct((half, own, feat), BF),
            jax.ShapeDtypeStruct((own, feat), BF),
        ),
        in_specs=[SMEM]
        + [by_rows(width)] * n_tp
        + [whole(w.shape) for w in wouts + odowns]
        + [by_rows(feat), by_rows(4 * SPAN)]
        + [whole(c.shape) for c in consts],
        out_specs=(
            pl.BlockSpec((half, step_own, feat), lambda i: (0, i, 0)),
            pl.BlockSpec((half, step_own, feat), lambda i: (0, i, 0)),
            pl.BlockSpec((step_own, feat), lambda i: (i, 0)),
        ),
        scratch_shapes=[pltpu.VMEM((step_blocks, n_tp, share, feat), BF)],
        compiler_params=params(),
        name="feed",
    )(me, *atts, *wouts, *odowns, x_full, sel, *consts)

    got = swap(odd, 1)
    sums = [
        swap((even[y] + got[y].astype(F32)).astype(BF), 2 * y) for y in range(1, half)
    ]
    done = pl.pallas_call(
        functools.partial(last_kernel, n_tp),
        out_shape=jax.ShapeDtypeStruct((n_req, n_tp, share, width), BF),
        grid=(1,),
        in_specs=[whole((1, own, feat)), whole((1, own, feat))]
        + [whole((own, feat))] * (1 + len(sums))
        + [whole((1, feat))] * 2,
        out_specs=whole((n_req, n_tp, share, width)),
        compiler_params=params(),
        name="finish",
    )(even, got, *sums, h_own, norm2_gain[None], norm2_bias[None])
    back = lax.all_to_all(
        done.reshape(n_req * n_tp, share, width),
        ("req", "tp"),
        split_axis=0,
        concat_axis=0,
        tiled=True,
    )
    result = pl.pallas_call(
        unpack_kernel,
        out_shape=jax.ShapeDtypeStruct((blocks, CAP, width), BF),
        in_specs=[SMEM, ANY],
        out_specs=ANY,
        scratch_shapes=[pltpu.SemaphoreType.DMA((blocks,))],
        name="unpack",
    )(owners, back.reshape(n_req, CAP, width))
    return result.reshape(blocks * CAP, width)


def solution(mesh):
    placed = (
        P("req", "tp"),
        P("req", None),
        P("req", None),
        P(),
        P(None, None, "tp"),
        P("tp", None),
        P(None, "tp"),
        P("tp", None),
        P(None, None, "req"),
        P(None, "req", "tp"),
        P("tp", "req"),
        P("req", None),
        P(None, "req"),
        P("req", "tp"),
        P("tp", "req"),
        P("req", None),
        P(),
        P(),
        P(),
        P(),
    )
    return jax.shard_map(
        body, mesh=mesh, in_specs=placed, out_specs=P("req", "tp"), check_vma=False
    )
```

```python
import functools

import jax
import jax.numpy as jnp
from jax import lax
from jax.experimental import pallas as pl
from jax.experimental.pallas import tpu as pltpu
from jax.sharding import PartitionSpec as P

HEAD_DIM = 64
RANK = 16
ADAPT_DEV = 2
CAP = 64
SEQ_G = 4
SPAN = ADAPT_DEV * RANK
PAD = 8
NORM_EPS = 1e-05
BF = jnp.bfloat16
F32 = jnp.float32


def dot(a, b):
    return lax.dot_general(a, b, (((1,), (0,)), ((), ())), preferred_element_type=F32)


def dot_t(a, b):
    return lax.dot_general(a, b, (((1,), (1,)), ((), ())), preferred_element_type=F32)


def layer_norm(values, gain, shift):
    mean = jnp.mean(values, axis=-1, keepdims=True)
    centred = values - mean
    variance = jnp.mean(centred * centred, axis=-1, keepdims=True)
    return centred * lax.rsqrt(variance + NORM_EPS) * gain + shift


def split_low(low, sel):
    low = low * sel
    high = low.astype(BF).astype(F32)
    return jnp.concatenate([high, low - high], axis=1).astype(BF)


def pack_kernel(lengths_in, ids_in, slots, tok, out, owners, lengths, ids, sems):
    copies = [
        pltpu.make_async_copy(lengths_in, lengths, sems.at[0]),
        pltpu.make_async_copy(ids_in, ids, sems.at[1]),
    ]
    for c in copies:
        c.start()
    blocks = tok.shape[0]
    if out.shape[0] > blocks:
        out[...] = jnp.zeros(out.shape, out.dtype)
    width = out.shape[2]
    pos = lax.broadcasted_iota(jnp.int32, (PAD, width), 1) % CAP
    for c in copies:
        c.wait()
    for g in range(blocks):
        slot = [slots[ids[k, g]] for k in range(SEQ_G)]
        owner = slot[0] // ADAPT_DEV
        owners[g] = owner
        code = jnp.full((PAD, width), 1 + slot[0] % ADAPT_DEV, jnp.int32)
        end = jnp.int32(0)
        for k in range(1, SEQ_G):
            end = end + lengths[k - 1, g]
            code = jnp.where(pos >= end, 1 + k * ADAPT_DEV + slot[k] % ADAPT_DEV, code)
        out[owner, :CAP, :] = tok[g]
        out[owner, CAP:, :] = code.astype(F32).astype(BF)


def tiles(count, step):
    if count <= 2:
        for t in range(count):
            step(t)
    else:
        lax.fori_loop(0, count, lambda t, c: (step(t), c)[1], 0)


def span(start, size):
    return pl.ds(start if isinstance(start, int) else pl.multiple_of(start, size), size)


def attn_kernel(n_tp, me, *refs):
    parts, (w, down, up, att, sel_out, x_full, up_all) = refs[:n_tp], refs[n_tp:]
    blocks = parts[0].shape[0]
    width = parts[0].shape[2]
    rows = blocks * CAP
    tp = me[0]
    for r in range(n_tp):
        x_full[:, span((tp ^ r) * width, width)] = parts[r][:, :CAP, :].reshape(rows, width)
    up_all[...] = jnp.zeros(up_all.shape, BF)
    for k in range(3):
        for part in range(2):
            first_row = (3 * part + k) * SPAN
            up_all[first_row : first_row + SPAN, k * width : (k + 1) * width] = up[k]
    pair_lane = lax.broadcasted_iota(jnp.int32, (2 * CAP, 2 * CAP), 1)
    pair_row = lax.broadcasted_iota(jnp.int32, (2 * CAP, 2 * CAP), 0)
    eye = pair_lane == pair_row
    lane_sel = ((pair_lane // RANK) % ADAPT_DEV).astype(F32)
    first = pair_lane < HEAD_DIM
    zero = jnp.zeros((), BF)
    tile = min(4, blocks)

    def step(t):
        rs = span(t * (tile * CAP), tile * CAP)
        masks, sels = [], []
        for p in range(tile // 2):
            b0 = t * tile + 2 * p
            c0 = parts[0][b0, CAP : CAP + 1, : 2 * CAP].astype(F32)
            c1 = parts[0][b0 + 1, CAP : CAP + 1, : 2 * CAP].astype(F32) + 64.0
            idr = jnp.where(pair_lane < CAP, c0, c1)
            idc = jnp.sum(jnp.where(eye, idr, 0.0), axis=1, keepdims=True)
            masks.append(idr == idc)
            pick = idc - 1.0
            pick = pick - 2.0 * jnp.floor(pick * 0.5)
            sels.append((lane_sel == pick).astype(F32))
        sel = jnp.concatenate(sels, axis=0)
        sel_out[rs] = sel.astype(BF)
        x = x_full[rs]
        low = split_low(dot_t(x, down[...]), sel[:, : 3 * SPAN])
        q, k_, v = [
            dot(x, w[k]) + dot(low, up_all[:, k * width : (k + 1) * width]) for k in range(3)
        ]
        q = (q.astype(BF).astype(F32) * HEAD_DIM**-0.5).astype(BF)
        k_, v = k_.astype(BF), v.astype(BF)
        for p in range(tile // 2):
            prs = slice(p * 2 * CAP, (p + 1) * 2 * CAP)
            out_rows = span(t * (tile * CAP) + p * 2 * CAP, 2 * CAP)
            for h in range(width // (2 * HEAD_DIM)):
                cs = slice(h * 2 * HEAD_DIM, (h + 1) * 2 * HEAD_DIM)
                both = []
                for half in (first, ~first):
                    s = dot_t(jnp.where(half, q[prs, cs], zero), k_[prs, cs])
                    s = jnp.where(masks[p], s, -1e30)
                    e = jnp.exp(s - jnp.max(s, axis=-1, keepdims=True))
                    inv = 1.0 / jnp.sum(e, axis=-1, keepdims=True)
                    both.append(dot((e * inv).astype(BF), v[prs, cs]))
                att[out_rows, cs] = jnp.where(first, *both).astype(BF)

    tiles(blocks // tile, step)


def ffn_kernel(n_tp, me, *refs):
    atts, wouts, odowns = refs[:n_tp], refs[n_tp : 2 * n_tp], refs[2 * n_tp : 3 * n_tp]
    (x, sel_in, oup, w1, d1, u1, w2, d2, u2, g1, b1, even, odd, h_own, h_scr) = refs[3 * n_tp :]
    rows, feat = x.shape
    blocks = rows // CAP
    share = CAP // n_tp
    tp = me[0]
    size = min(rows, 256)
    nb = size // CAP
    ups = [jnp.concatenate([u[...], u[...]], axis=0) for u in (oup, u1, u2)]

    def step(t):
        rs = span(t * size, size)
        sel = sel_in[rs].astype(F32)[:, :SPAN]
        total = x[rs].astype(F32)
        low = None
        for r in range(n_tp):
            a = atts[r][rs]
            total = total + dot(a, wouts[r][...])
            part = dot_t(a, odowns[r][...])
            low = part if low is None else low + part
        total = total + dot(split_low(low, sel), ups[0])
        h1 = layer_norm(total, g1[...], b1[...]).astype(BF)
        h_scr[span(t * nb, nb)] = h1.reshape(nb, n_tp, share, feat)
        gate = dot(h1, w1[...]) + dot(split_low(dot_t(h1, d1[...]), sel), ups[1])
        hidden = (0.5 * gate * (1.0 + lax.erf(gate * 0.7071067811865476))).astype(BF)
        term = dot(hidden, w2[...]) + dot(split_low(dot_t(hidden, d2[...]), sel), ups[2])
        term = term.reshape(nb, n_tp, share, feat)
        own_rows = span(t * (size // n_tp), size // n_tp)
        for j in range(n_tp):
            rel = tp ^ j
            piece = term[:, j].reshape(nb * share, feat)

            @pl.when(rel % 2 == 0)
            def _():
                even[rel // 2, own_rows, :] = piece

            @pl.when(rel % 2 == 1)
            def _():
                odd[rel // 2, own_rows, :] = piece.astype(BF)

    tiles(rows // size, step)
    h_own[...] = h_scr[:, tp].reshape(blocks * share, feat)


def last_kernel(n_tp, even, got, *refs):
    arrived, (h_own, g2, b2, out) = refs[: n_tp // 2 - 1], refs[n_tp // 2 - 1 :]
    total = h_own[...].astype(F32) + (even[0] + got[0].astype(F32))
    for a in arrived:
        total = total + a[...].astype(F32)
    done = layer_norm(total, g2[...], b2[...]).astype(BF)
    n, _, share, width = out.shape
    for f in range(n_tp):
        out[:, f] = done[:, f * width : (f + 1) * width].reshape(n, share, width)


def unpack_kernel(owners, arrived, out):
    for g in range(out.shape[0]):
        out[g] = arrived[owners[g]]


VM = pl.BlockSpec(memory_space=pltpu.VMEM)
ANY = pl.BlockSpec(memory_space=pl.ANY)
SMEM = pl.BlockSpec(memory_space=pltpu.SMEM)


def near(*arrays):
    return [pltpu.with_memory_space_constraint(a, pltpu.VMEM) for a in arrays]


def params(mib=20):
    return pltpu.CompilerParams(vmem_limit_bytes=mib * 1024 * 1024)


def body(
    tokens,
    prompt_lengths,
    adapter_ids,
    adapter_slot,
    w_qkv,
    w_out,
    w_fc1,
    w_fc2,
    qkv_down,
    qkv_up,
    out_down,
    out_up,
    fc1_down,
    fc1_up,
    fc2_down,
    fc2_up,
    norm1_gain,
    norm1_bias,
    norm2_gain,
    norm2_bias,
):
    n_req = lax.axis_size("req")
    n_tp = lax.axis_size("tp")
    feat = w_qkv.shape[1]
    width = tokens.shape[1]
    blocks = tokens.shape[0] // CAP
    share = CAP // n_tp
    half = n_tp // 2
    me = jnp.reshape(lax.axis_index("tp"), (1,)).astype(jnp.int32)

    def swap(value, r):
        return lax.ppermute(value, "tp", [(i, i ^ r) for i in range(n_tp)])

    def gather(value):
        far = [value] + [swap(value, 2 * y) for y in range(1, n_tp // 2)]
        found = []
        for piece in far:
            found += [piece, swap(piece, 1)]
        return found

    packed, owners = pl.pallas_call(
        pack_kernel,
        out_shape=(
            pltpu.VMEM((n_req, CAP + PAD, width), BF),
            jax.ShapeDtypeStruct((blocks,), jnp.int32),
        ),
        in_specs=[ANY, ANY, SMEM, VM],
        out_specs=(VM, SMEM),
        scratch_shapes=[
            pltpu.SMEM((SEQ_G, blocks), jnp.int32),
            pltpu.SMEM((SEQ_G, blocks), jnp.int32),
            pltpu.SemaphoreType.DMA((2,)),
        ],
        compiler_params=params(4),
        name="pack",
    )(prompt_lengths.T, adapter_ids.T, adapter_slot, tokens.reshape(blocks, CAP, width))
    arrived = lax.all_to_all(packed, "req", split_axis=0, concat_axis=0, tiled=True)
    w_far = [swap(w_out, 2 * y) for y in range(1, half)]
    o_own = out_down.T
    o_far = [swap(o_own, 2 * y) for y in range(1, half)]
    arrived, w_far, o_far = lax.optimization_barrier((arrived, w_far, o_far))
    parts = gather(arrived)

    rows = n_req * CAP
    attended, sel, x_full = pl.pallas_call(
        functools.partial(attn_kernel, n_tp),
        out_shape=(
            pltpu.VMEM((rows, width), BF),
            pltpu.VMEM((rows, 4 * SPAN), BF),
            pltpu.VMEM((rows, feat), BF),
        ),
        in_specs=[SMEM] + [VM] * (n_tp + 3),
        out_specs=(VM,) * 3,
        scratch_shapes=[pltpu.VMEM((6 * SPAN, 3 * width), BF)],
        compiler_params=params(),
        name="attend",
    )(
        me,
        *near(
            *parts,
            w_qkv,
            jnp.swapaxes(qkv_down, 1, 2).reshape(3 * SPAN, feat),
            qkv_up,
        ),
    )

    atts = gather(attended)
    wouts, odowns = [], []
    for w_piece, o_piece in zip([w_out] + w_far, [o_own] + o_far):
        wouts += [w_piece, swap(w_piece, 1)]
        odowns += [o_piece, swap(o_piece, 1)]
    own = rows // n_tp
    consts = [out_up, w_fc1, fc1_down.T, fc1_up, w_fc2, fc2_down.T, fc2_up]
    consts += [norm1_gain[None], norm1_bias[None]]
    even, odd, h_own = pl.pallas_call(
        functools.partial(ffn_kernel, n_tp),
        out_shape=(
            pltpu.VMEM((half, own, feat), F32),
            pltpu.VMEM((half, own, feat), BF),
            pltpu.VMEM((own, feat), BF),
        ),
        in_specs=[SMEM] + [VM] * (3 * n_tp + 2 + len(consts)),
        out_specs=(VM,) * 3,
        scratch_shapes=[pltpu.VMEM((n_req, n_tp, share, feat), BF)],
        compiler_params=params(),
        name="feed",
    )(me, *near(*atts, *wouts, *odowns, x_full, sel, *consts))

    got = swap(odd, 1)
    sums = [
        swap((even[y] + got[y].astype(F32)).astype(BF), 2 * y) for y in range(1, half)
    ]
    done = pl.pallas_call(
        functools.partial(last_kernel, n_tp),
        out_shape=pltpu.VMEM((n_req, n_tp, share, width), BF),
        in_specs=[VM] * (5 + len(sums)),
        out_specs=VM,
        compiler_params=params(),
        name="finish",
    )(*near(even, got, *sums, h_own, norm2_gain[None], norm2_bias[None]))
    back = lax.all_to_all(
        done.reshape(n_req * n_tp, share, width),
        ("req", "tp"),
        split_axis=0,
        concat_axis=0,
        tiled=True,
    )
    result = pl.pallas_call(
        unpack_kernel,
        out_shape=jax.ShapeDtypeStruct((blocks, CAP, width), BF),
        in_specs=[SMEM, VM],
        out_specs=VM,
        compiler_params=params(4),
        name="unpack",
    )(owners, *near(back.reshape(n_req, CAP, width)))
    return result.reshape(blocks * CAP, width)


def solution(mesh):
    placed = (
        P("req", "tp"),
        P("req", None),
        P("req", None),
        P(),
        P(None, None, "tp"),
        P("tp", None),
        P(None, "tp"),
        P("tp", None),
        P(None, None, "req"),
        P(None, "req", "tp"),
        P("tp", "req"),
        P("req", None),
        P(None, "req"),
        P("req", "tp"),
        P("tp", "req"),
        P("req", None),
        P(),
        P(),
        P(),
        P(),
    )
    return jax.shard_map(
        body, mesh=mesh, in_specs=placed, out_specs=P("req", "tp"), check_vma=False
    )
```

```python
import functools

import jax
import jax.numpy as jnp
from jax import lax
from jax.experimental import pallas as pl
from jax.experimental.pallas import tpu as pltpu
from jax.sharding import PartitionSpec as P

HEAD_DIM = 64
RANK = 16
ADAPT_DEV = 2
CAP = 64
SEQ_G = 4
SPAN = ADAPT_DEV * RANK
PAD = 8
NORM_EPS = 1e-05
BF = jnp.bfloat16
F32 = jnp.float32


def dot(a, b):
    return lax.dot_general(a, b, (((1,), (0,)), ((), ())), preferred_element_type=F32)


def dot_t(a, b):
    return lax.dot_general(a, b, (((1,), (1,)), ((), ())), preferred_element_type=F32)


def layer_norm(values, gain, shift):
    mean = jnp.mean(values, axis=-1, keepdims=True)
    centred = values - mean
    variance = jnp.mean(centred * centred, axis=-1, keepdims=True)
    return centred * lax.rsqrt(variance + NORM_EPS) * gain + shift


def split_low(low, sel):
    low = low * sel
    high = low.astype(BF).astype(F32)
    return jnp.concatenate([high, low - high], axis=1).astype(BF)


def fetch(pairs, sems):
    copies = [
        pltpu.make_async_copy(src, dst, sems.at[i]) for i, (src, dst) in enumerate(pairs)
    ]
    for c in copies:
        c.start()
    return copies


def pack_kernel(
    lengths_in, ids_in, slots_in, tok_in, out, owners, lengths, ids, slots, tok, sems
):
    copies = fetch(
        [(lengths_in, lengths), (ids_in, ids), (slots_in, slots), (tok_in, tok)], sems
    )
    blocks = tok.shape[0]
    if out.shape[0] > blocks:
        out[...] = jnp.zeros(out.shape, out.dtype)
    width = out.shape[2]
    pos = lax.broadcasted_iota(jnp.int32, (PAD, width), 1) % CAP
    for c in copies:
        c.wait()
    for g in range(blocks):
        slot = [slots[ids[k, g]] for k in range(SEQ_G)]
        owner = slot[0] // ADAPT_DEV
        owners[g] = owner
        code = jnp.full((PAD, width), 1 + slot[0] % ADAPT_DEV, jnp.int32)
        end = jnp.int32(0)
        for k in range(1, SEQ_G):
            end = end + lengths[k - 1, g]
            code = jnp.where(pos >= end, 1 + k * ADAPT_DEV + slot[k] % ADAPT_DEV, code)
        out[owner, :CAP, :] = tok[g]
        out[owner, CAP:, :] = code.astype(F32).astype(BF)


def tiles(count, step):
    step(0)
    if count == 2:
        step(1)
    elif count > 2:
        lax.fori_loop(1, count, lambda t, c: (step(t), c)[1], 0)


def span(start, size):
    return pl.ds(start if isinstance(start, int) else pl.multiple_of(start, size), size)


def attn_kernel(n_tp, me, *refs):
    parts = refs[:n_tp]
    w_in, down_in, up_in, att, sel_out, x_full, up_all, w, down, up, sems = refs[n_tp:]
    copies = fetch(
        [(down_in, down), (up_in, up)] + [(w_in.at[k], w.at[k]) for k in range(3)], sems
    )
    blocks = parts[0].shape[0]
    width = parts[0].shape[2]
    rows = blocks * CAP
    tp = me[0]
    for r in range(n_tp):
        x_full[:, span((tp ^ r) * width, width)] = parts[r][:, :CAP, :].reshape(rows, width)
    up_all[...] = jnp.zeros(up_all.shape, BF)
    copies[0].wait()
    copies[1].wait()
    for k in range(3):
        for part in range(2):
            first_row = (3 * part + k) * SPAN
            up_all[first_row : first_row + SPAN, k * width : (k + 1) * width] = up[k]
    pair_lane = lax.broadcasted_iota(jnp.int32, (2 * CAP, 2 * CAP), 1)
    pair_row = lax.broadcasted_iota(jnp.int32, (2 * CAP, 2 * CAP), 0)
    eye = pair_lane == pair_row
    lane_sel = ((pair_lane // RANK) % ADAPT_DEV).astype(F32)
    first = pair_lane < HEAD_DIM
    zero = jnp.zeros((), BF)
    tile = min(4, blocks)

    def step(t):
        rs = span(t * (tile * CAP), tile * CAP)
        masks, sels = [], []
        for p in range(tile // 2):
            b0 = t * tile + 2 * p
            c0 = parts[0][b0, CAP : CAP + 1, : 2 * CAP].astype(F32)
            c1 = parts[0][b0 + 1, CAP : CAP + 1, : 2 * CAP].astype(F32) + 64.0
            idr = jnp.where(pair_lane < CAP, c0, c1)
            idc = jnp.sum(jnp.where(eye, idr, 0.0), axis=1, keepdims=True)
            masks.append(idr == idc)
            pick = idc - 1.0
            pick = pick - 2.0 * jnp.floor(pick * 0.5)
            sels.append((lane_sel == pick).astype(F32))
        sel = jnp.concatenate(sels, axis=0)
        sel_out[rs] = sel.astype(BF)
        x = x_full[rs]
        low = split_low(dot_t(x, down[...]), sel[:, : 3 * SPAN])
        qkv = []
        for k in range(3):
            if isinstance(t, int) and t == 0:
                copies[2 + k].wait()
            qkv.append(dot(x, w[k]) + dot(low, up_all[:, k * width : (k + 1) * width]))
        q, k_, v = qkv
        q = (q.astype(BF).astype(F32) * HEAD_DIM**-0.5).astype(BF)
        k_, v = k_.astype(BF), v.astype(BF)
        for p in range(tile // 2):
            prs = slice(p * 2 * CAP, (p + 1) * 2 * CAP)
            out_rows = span(t * (tile * CAP) + p * 2 * CAP, 2 * CAP)
            for h in range(width // (2 * HEAD_DIM)):
                cs = slice(h * 2 * HEAD_DIM, (h + 1) * 2 * HEAD_DIM)
                both = []
                for half in (first, ~first):
                    s = dot_t(jnp.where(half, q[prs, cs], zero), k_[prs, cs])
                    s = jnp.where(masks[p], s, -1e30)
                    e = jnp.exp(s - jnp.max(s, axis=-1, keepdims=True))
                    inv = 1.0 / jnp.sum(e, axis=-1, keepdims=True)
                    both.append(dot((e * inv).astype(BF), v[prs, cs]))
                att[out_rows, cs] = jnp.where(first, *both).astype(BF)

    tiles(blocks // tile, step)


def ffn_kernel(n_tp, me, *refs):
    atts, wouts, odowns = refs[:n_tp], refs[n_tp : 2 * n_tp], refs[2 * n_tp : 3 * n_tp]
    (x, sel_in, w1_in, w2_in, oup, d1, u1, d2, u2, g1, b1) = refs[3 * n_tp : 3 * n_tp + 11]
    even, odd, h_own, h_scr, w1, w2, sems = refs[3 * n_tp + 11 :]
    copies = fetch([(w1_in, w1), (w2_in, w2)], sems)
    rows, feat = x.shape
    blocks = rows // CAP
    share = CAP // n_tp
    tp = me[0]
    size = min(rows, 256)
    nb = size // CAP
    ups = [jnp.concatenate([u[...], u[...]], axis=0) for u in (oup, u1, u2)]

    def step(t):
        rs = span(t * size, size)
        sel = sel_in[rs].astype(F32)[:, :SPAN]
        total = x[rs].astype(F32)
        low = None
        for r in range(n_tp):
            a = atts[r][rs]
            total = total + dot(a, wouts[r][...])
            part = dot_t(a, odowns[r][...])
            low = part if low is None else low + part
        total = total + dot(split_low(low, sel), ups[0])
        h1 = layer_norm(total, g1[...], b1[...]).astype(BF)
        h_scr[span(t * nb, nb)] = h1.reshape(nb, n_tp, share, feat)
        if isinstance(t, int) and t == 0:
            copies[0].wait()
        gate = dot(h1, w1[...]) + dot(split_low(dot_t(h1, d1[...]), sel), ups[1])
        hidden = (0.5 * gate * (1.0 + lax.erf(gate * 0.7071067811865476))).astype(BF)
        if isinstance(t, int) and t == 0:
            copies[1].wait()
        term = dot(hidden, w2[...]) + dot(split_low(dot_t(hidden, d2[...]), sel), ups[2])
        term = term.reshape(nb, n_tp, share, feat)
        own_rows = span(t * (size // n_tp), size // n_tp)
        for j in range(n_tp):
            rel = tp ^ j
            piece = term[:, j].reshape(nb * share, feat)

            @pl.when(rel % 2 == 0)
            def _():
                even[rel // 2, own_rows, :] = piece

            @pl.when(rel % 2 == 1)
            def _():
                odd[rel // 2, own_rows, :] = piece.astype(BF)

    tiles(rows // size, step)
    h_own[...] = h_scr[:, tp].reshape(blocks * share, feat)


def last_kernel(n_tp, even, got, *refs):
    arrived, (h_own, g2, b2, out) = refs[: n_tp // 2 - 1], refs[n_tp // 2 - 1 :]
    total = h_own[...].astype(F32) + (even[0] + got[0].astype(F32))
    for a in arrived:
        total = total + a[...].astype(F32)
    done = layer_norm(total, g2[...], b2[...]).astype(BF)
    n, _, share, width = out.shape
    for f in range(n_tp):
        out[:, f] = done[:, f * width : (f + 1) * width].reshape(n, share, width)


def unpack_kernel(owners, arrived, out):
    for g in range(out.shape[0]):
        out[g] = arrived[owners[g]]


VM = pl.BlockSpec(memory_space=pltpu.VMEM)
HBM = pl.BlockSpec(memory_space=pltpu.HBM)
SMEM = pl.BlockSpec(memory_space=pltpu.SMEM)


def near(*arrays):
    return [pltpu.with_memory_space_constraint(a, pltpu.VMEM) for a in arrays]


def far(*arrays):
    return [pltpu.with_memory_space_constraint(a, pltpu.HBM) for a in arrays]


def params(mib=20):
    return pltpu.CompilerParams(vmem_limit_bytes=mib * 1024 * 1024)


def body(
    tokens,
    prompt_lengths,
    adapter_ids,
    adapter_slot,
    w_qkv,
    w_out,
    w_fc1,
    w_fc2,
    qkv_down,
    qkv_up,
    out_down,
    out_up,
    fc1_down,
    fc1_up,
    fc2_down,
    fc2_up,
    norm1_gain,
    norm1_bias,
    norm2_gain,
    norm2_bias,
):
    n_req = lax.axis_size("req")
    n_tp = lax.axis_size("tp")
    feat = w_qkv.shape[1]
    width = tokens.shape[1]
    blocks = tokens.shape[0] // CAP
    share = CAP // n_tp
    half = n_tp // 2
    me = jnp.reshape(lax.axis_index("tp"), (1,)).astype(jnp.int32)

    def swap(value, r):
        return lax.ppermute(value, "tp", [(i, i ^ r) for i in range(n_tp)])

    def gather(value):
        far = [value] + [swap(value, 2 * y) for y in range(1, n_tp // 2)]
        found = []
        for piece in far:
            found += [piece, swap(piece, 1)]
        return found

    packed, owners = pl.pallas_call(
        pack_kernel,
        out_shape=(
            pltpu.VMEM((n_req, CAP + PAD, width), BF),
            jax.ShapeDtypeStruct((blocks,), jnp.int32),
        ),
        in_specs=[HBM] * 4,
        out_specs=(VM, SMEM),
        scratch_shapes=[
            pltpu.SMEM((SEQ_G, blocks), jnp.int32),
            pltpu.SMEM((SEQ_G, blocks), jnp.int32),
            pltpu.SMEM(adapter_slot.shape, jnp.int32),
            pltpu.VMEM((blocks, CAP, width), BF),
            pltpu.SemaphoreType.DMA((4,)),
        ],
        compiler_params=params(4),
        name="pack",
    )(
        *far(
            prompt_lengths.T,
            adapter_ids.T,
            adapter_slot,
            tokens.reshape(blocks, CAP, width),
        )
    )
    arrived = lax.all_to_all(packed, "req", split_axis=0, concat_axis=0, tiled=True)
    w_far = [swap(w_out, 2 * y) for y in range(1, half)]
    o_own = out_down.T
    o_far = [swap(o_own, 2 * y) for y in range(1, half)]
    arrived, w_far, o_far = lax.optimization_barrier((arrived, w_far, o_far))
    parts = gather(arrived)
    wouts, odowns = [], []
    for w_piece, o_piece in zip([w_out] + w_far, [o_own] + o_far):
        wouts += [w_piece, swap(w_piece, 1)]
        odowns += [o_piece, swap(o_piece, 1)]
    parts, wouts, odowns = lax.optimization_barrier((parts, wouts, odowns))

    rows = n_req * CAP
    attended, sel, x_full = pl.pallas_call(
        functools.partial(attn_kernel, n_tp),
        out_shape=(
            pltpu.VMEM((rows, width), BF),
            pltpu.VMEM((rows, 4 * SPAN), BF),
            pltpu.VMEM((rows, feat), BF),
        ),
        in_specs=[SMEM] + [VM] * n_tp + [HBM] * 3,
        out_specs=(VM,) * 3,
        scratch_shapes=[
            pltpu.VMEM((6 * SPAN, 3 * width), BF),
            pltpu.VMEM((3, feat, width), BF),
            pltpu.VMEM((3 * SPAN, feat), BF),
            pltpu.VMEM((3, SPAN, width), BF),
            pltpu.SemaphoreType.DMA((5,)),
        ],
        compiler_params=params(),
        name="attend",
    )(
        me,
        *near(*parts),
        *far(
            w_qkv,
            jnp.swapaxes(qkv_down, 1, 2).reshape(3 * SPAN, feat),
            qkv_up,
        ),
    )

    atts = gather(attended)
    own = rows // n_tp
    consts = [out_up, fc1_down.T, fc1_up, fc2_down.T, fc2_up]
    consts += [norm1_gain[None], norm1_bias[None]]
    even, odd, h_own = pl.pallas_call(
        functools.partial(ffn_kernel, n_tp),
        out_shape=(
            pltpu.VMEM((half, own, feat), F32),
            pltpu.VMEM((half, own, feat), BF),
            pltpu.VMEM((own, feat), BF),
        ),
        in_specs=[SMEM]
        + [VM] * (3 * n_tp + 2)
        + [HBM] * 2
        + [VM] * len(consts),
        out_specs=(VM,) * 3,
        scratch_shapes=[
            pltpu.VMEM((n_req, n_tp, share, feat), BF),
            pltpu.VMEM(w_fc1.shape, BF),
            pltpu.VMEM(w_fc2.shape, BF),
            pltpu.SemaphoreType.DMA((2,)),
        ],
        compiler_params=params(),
        name="feed",
    )(
        me,
        *near(*atts, *wouts, *odowns, x_full, sel),
        *far(w_fc1, w_fc2),
        *near(*consts),
    )

    got = swap(odd, 1)
    sums = [
        swap((even[y] + got[y].astype(F32)).astype(BF), 2 * y) for y in range(1, half)
    ]
    done = pl.pallas_call(
        functools.partial(last_kernel, n_tp),
        out_shape=pltpu.VMEM((n_req, n_tp, share, width), BF),
        in_specs=[VM] * (5 + len(sums)),
        out_specs=VM,
        compiler_params=params(),
        name="finish",
    )(*near(even, got, *sums, h_own, norm2_gain[None], norm2_bias[None]))
    back = lax.all_to_all(
        done.reshape(n_req * n_tp, share, width),
        ("req", "tp"),
        split_axis=0,
        concat_axis=0,
        tiled=True,
    )
    result = pl.pallas_call(
        unpack_kernel,
        out_shape=jax.ShapeDtypeStruct((blocks, CAP, width), BF),
        in_specs=[SMEM, VM],
        out_specs=VM,
        compiler_params=params(4),
        name="unpack",
    )(owners, *near(back.reshape(n_req, CAP, width)))
    return result.reshape(blocks * CAP, width)


def solution(mesh):
    placed = (
        P("req", "tp"),
        P("req", None),
        P("req", None),
        P(),
        P(None, None, "tp"),
        P("tp", None),
        P(None, "tp"),
        P("tp", None),
        P(None, None, "req"),
        P(None, "req", "tp"),
        P("tp", "req"),
        P("req", None),
        P(None, "req"),
        P("req", "tp"),
        P("tp", "req"),
        P("req", None),
        P(),
        P(),
        P(),
        P(),
    )
    return jax.shard_map(
        body, mesh=mesh, in_specs=placed, out_specs=P("req", "tp"), check_vma=False
    )
```

```python
import functools

import jax
import jax.numpy as jnp
from jax import lax
from jax.experimental import pallas as pl
from jax.experimental.pallas import tpu as pltpu
from jax.sharding import PartitionSpec as P

HEAD_DIM = 64
RANK = 16
ADAPT_DEV = 2
CAP = 64
SEQ_G = 4
SPAN = ADAPT_DEV * RANK
PAD = 8
NORM_EPS = 1e-05
BF = jnp.bfloat16
F32 = jnp.float32


def dot(a, b):
    return lax.dot_general(a, b, (((1,), (0,)), ((), ())), preferred_element_type=F32)


def dot_t(a, b):
    return lax.dot_general(a, b, (((1,), (1,)), ((), ())), preferred_element_type=F32)


def layer_norm(values, gain, shift):
    mean = jnp.mean(values, axis=-1, keepdims=True)
    centred = values - mean
    variance = jnp.mean(centred * centred, axis=-1, keepdims=True)
    return centred * lax.rsqrt(variance + NORM_EPS) * gain + shift


def split_low(low, sel):
    low = low * sel
    high = low.astype(BF).astype(F32)
    return jnp.concatenate([high, low - high], axis=1).astype(BF)


def fetch(pairs, sems):
    copies = [
        pltpu.make_async_copy(src, dst, sems.at[i]) for i, (src, dst) in enumerate(pairs)
    ]
    for c in copies:
        c.start()
    return copies


def pack_kernel(
    lengths_in, ids_in, slots_in, tok_in, out, owners, lengths, ids, slots, tok, sems
):
    copies = fetch(
        [(lengths_in, lengths), (ids_in, ids), (slots_in, slots), (tok_in, tok)], sems
    )
    blocks = tok.shape[0]
    if out.shape[0] > blocks:
        out[...] = jnp.zeros(out.shape, out.dtype)
    width = out.shape[2]
    pos = lax.broadcasted_iota(jnp.int32, (PAD, width), 1) % CAP
    for c in copies:
        c.wait()
    for g in range(blocks):
        slot = [slots[ids[k, g]] for k in range(SEQ_G)]
        owner = slot[0] // ADAPT_DEV
        owners[g] = owner
        code = jnp.full((PAD, width), 1 + slot[0] % ADAPT_DEV, jnp.int32)
        end = jnp.int32(0)
        for k in range(1, SEQ_G):
            end = end + lengths[k - 1, g]
            code = jnp.where(pos >= end, 1 + k * ADAPT_DEV + slot[k] % ADAPT_DEV, code)
        out[owner, :CAP, :] = tok[g]
        out[owner, CAP:, :] = code.astype(F32).astype(BF)


def tiles(count, step):
    step(0)
    if count == 2:
        step(1)
    elif count > 2:
        lax.fori_loop(1, count, lambda t, c: (step(t), c)[1], 0)


def span(start, size):
    return pl.ds(start if isinstance(start, int) else pl.multiple_of(start, size), size)


def attn_kernel(n_tp, chunk, me, *refs):
    parts = refs[:n_tp]
    copies = None
    if chunk == 0:
        w_in, down_in, up_in, att, sel_out, x_full, w, down, up_all, up, sems = refs[n_tp:]
        copies = fetch(
            [(down_in, down), (up_in, up)] + [(w_in.at[k], w.at[k]) for k in range(3)], sems
        )
    else:
        w, down, up_all, att, sel_out, x_full = refs[n_tp:]
    blocks = att.shape[0] // CAP
    width = parts[0].shape[2]
    rows = blocks * CAP
    tp = me[0]
    offsets = [chunk * blocks if part.shape[0] > blocks else 0 for part in parts]
    for r in range(n_tp):
        x_full[:, span((tp ^ r) * width, width)] = parts[r][
            offsets[r] : offsets[r] + blocks, :CAP, :
        ].reshape(rows, width)
    if chunk == 0:
        up_all[...] = jnp.zeros(up_all.shape, BF)
        copies[0].wait()
        copies[1].wait()
        for k in range(3):
            for part in range(2):
                first_row = (3 * part + k) * SPAN
                up_all[first_row : first_row + SPAN, k * width : (k + 1) * width] = up[k]
    pair_lane = lax.broadcasted_iota(jnp.int32, (2 * CAP, 2 * CAP), 1)
    pair_row = lax.broadcasted_iota(jnp.int32, (2 * CAP, 2 * CAP), 0)
    eye = pair_lane == pair_row
    lane_sel = ((pair_lane // RANK) % ADAPT_DEV).astype(F32)
    first = pair_lane < HEAD_DIM
    zero = jnp.zeros((), BF)
    tile = min(4, blocks)

    def step(t):
        rs = span(t * (tile * CAP), tile * CAP)
        masks, sels = [], []
        for p in range(tile // 2):
            b0 = offsets[0] + t * tile + 2 * p
            c0 = parts[0][b0, CAP : CAP + 1, : 2 * CAP].astype(F32)
            c1 = parts[0][b0 + 1, CAP : CAP + 1, : 2 * CAP].astype(F32) + 64.0
            idr = jnp.where(pair_lane < CAP, c0, c1)
            idc = jnp.sum(jnp.where(eye, idr, 0.0), axis=1, keepdims=True)
            masks.append(idr == idc)
            pick = idc - 1.0
            pick = pick - 2.0 * jnp.floor(pick * 0.5)
            sels.append((lane_sel == pick).astype(F32))
        sel = jnp.concatenate(sels, axis=0)
        sel_out[rs] = sel.astype(BF)
        x = x_full[rs]
        low = split_low(dot_t(x, down[...]), sel[:, : 3 * SPAN])
        qkv = []
        for k in range(3):
            if copies and isinstance(t, int):
                copies[2 + k].wait()
            qkv.append(dot(x, w[k]) + dot(low, up_all[:, k * width : (k + 1) * width]))
        q, k_, v = qkv
        q = (q.astype(BF).astype(F32) * HEAD_DIM**-0.5).astype(BF)
        k_, v = k_.astype(BF), v.astype(BF)
        for p in range(tile // 2):
            prs = slice(p * 2 * CAP, (p + 1) * 2 * CAP)
            out_rows = span(t * (tile * CAP) + p * 2 * CAP, 2 * CAP)
            for h in range(width // (2 * HEAD_DIM)):
                cs = slice(h * 2 * HEAD_DIM, (h + 1) * 2 * HEAD_DIM)
                both = []
                for half in (first, ~first):
                    s = dot_t(jnp.where(half, q[prs, cs], zero), k_[prs, cs])
                    s = jnp.where(masks[p], s, -1e30)
                    e = jnp.exp(s - jnp.max(s, axis=-1, keepdims=True))
                    inv = 1.0 / jnp.sum(e, axis=-1, keepdims=True)
                    both.append(dot((e * inv).astype(BF), v[prs, cs]))
                att[out_rows, cs] = jnp.where(first, *both).astype(BF)

    tiles(blocks // tile, step)


def ffn_kernel(n_tp, chunk, me, *refs):
    atts, wouts, odowns = refs[:n_tp], refs[n_tp : 2 * n_tp], refs[2 * n_tp : 3 * n_tp]
    x, sel_in, oup, d1, u1, d2, u2, g1, b1 = refs[3 * n_tp : 3 * n_tp + 9]
    copies = None
    if chunk == 0:
        w1_in, w2_in, even, odd, odds, h_own, w1, w2, h_scr, sems = refs[3 * n_tp + 9 :]
        copies = fetch([(w1_in, w1), (w2_in, w2)], sems)
    else:
        w1, w2, even, odd, odds, h_own, h_scr = refs[3 * n_tp + 9 :]
    rows, feat = x.shape
    blocks = rows // CAP
    share = CAP // n_tp
    tp = me[0]
    size = min(rows, 256)
    nb = size // CAP
    ups = [jnp.concatenate([u[...], u[...]], axis=0) for u in (oup, u1, u2)]

    def step(t):
        rs = span(t * size, size)
        sel = sel_in[rs].astype(F32)[:, :SPAN]
        total = x[rs].astype(F32)
        low = None
        for r in range(n_tp):
            a = atts[r][rs]
            total = total + dot(a, wouts[r][...])
            part = dot_t(a, odowns[r][...])
            low = part if low is None else low + part
        total = total + dot(split_low(low, sel), ups[0])
        h1 = layer_norm(total, g1[...], b1[...]).astype(BF)
        h_scr[span(t * nb, nb)] = h1.reshape(nb, n_tp, share, feat)
        if copies and isinstance(t, int):
            copies[0].wait()
        gate = dot(h1, w1[...]) + dot(split_low(dot_t(h1, d1[...]), sel), ups[1])
        hidden = (0.5 * gate * (1.0 + lax.erf(gate * 0.7071067811865476))).astype(BF)
        if copies and isinstance(t, int):
            copies[1].wait()
        term = dot(hidden, w2[...]) + dot(split_low(dot_t(hidden, d2[...]), sel), ups[2])
        term = term.reshape(nb, n_tp, share, feat)
        own_rows = span(t * (size // n_tp), size // n_tp)
        for j in range(n_tp):
            rel = tp ^ j
            piece = term[:, j].reshape(nb * share, feat)

            @pl.when(rel % 2 == 0)
            def _():
                even[rel // 2, own_rows, :] = piece

            @pl.when(rel == 1)
            def _():
                odd[own_rows, :] = piece.astype(BF)

            @pl.when((rel % 2 == 1) & (rel > 1))
            def _():
                odds[rel // 2 - 1, own_rows, :] = piece.astype(BF)

    tiles(rows // size, step)
    h_own[...] = h_scr[:, tp].reshape(blocks * share, feat)


def last_kernel(n_tp, earlier, *refs):
    g2, b2, out = refs[-3:]
    even, got, h_own = refs[earlier : earlier + 3]
    _, share, width = out.shape[1:]
    step = h_own.shape[0] // share
    total = h_own[...].astype(F32) + (even[0] + got[...].astype(F32))
    for arrived in refs[earlier + 3 : -3]:
        total = total + arrived[...].astype(F32)
    done = layer_norm(total, g2[...], b2[...]).astype(BF)
    if earlier:
        out[: refs[0].shape[0]] = refs[0][...]
    for f in range(n_tp):
        piece = done[:, f * width : (f + 1) * width].reshape(step, share, width)
        out[out.shape[0] - step :, f] = piece


def unpack_kernel(owners, arrived, out):
    for g in range(out.shape[0]):
        out[g] = arrived[owners[g]]


VM = pl.BlockSpec(memory_space=pltpu.VMEM)
HBM = pl.BlockSpec(memory_space=pltpu.HBM)
SMEM = pl.BlockSpec(memory_space=pltpu.SMEM)


def near(*arrays):
    return [pltpu.with_memory_space_constraint(a, pltpu.VMEM) for a in arrays]


def far(*arrays):
    return [pltpu.with_memory_space_constraint(a, pltpu.HBM) for a in arrays]


def work(flops, rows):
    return pl.CostEstimate(flops=5 * flops, transcendentals=rows * 1024, bytes_accessed=rows * 8192)


def params(mib=20):
    return pltpu.CompilerParams(vmem_limit_bytes=mib * 1024 * 1024)


def body(
    tokens,
    prompt_lengths,
    adapter_ids,
    adapter_slot,
    w_qkv,
    w_out,
    w_fc1,
    w_fc2,
    qkv_down,
    qkv_up,
    out_down,
    out_up,
    fc1_down,
    fc1_up,
    fc2_down,
    fc2_up,
    norm1_gain,
    norm1_bias,
    norm2_gain,
    norm2_bias,
):
    n_req = lax.axis_size("req")
    n_tp = lax.axis_size("tp")
    feat = w_qkv.shape[1]
    width = tokens.shape[1]
    blocks = tokens.shape[0] // CAP
    share = CAP // n_tp
    half = n_tp // 2
    me = jnp.reshape(lax.axis_index("tp"), (1,)).astype(jnp.int32)

    def swap(value, r):
        return lax.ppermute(value, "tp", [(i, i ^ r) for i in range(n_tp)])

    def second_hop(pieces):
        return [hop for piece in pieces for hop in (piece, swap(piece, 1))]

    packed, owners = pl.pallas_call(
        pack_kernel,
        out_shape=(
            pltpu.VMEM((n_req, CAP + PAD, width), BF),
            jax.ShapeDtypeStruct((blocks,), jnp.int32),
        ),
        in_specs=[HBM] * 4,
        out_specs=(VM, SMEM),
        scratch_shapes=[
            pltpu.SMEM((SEQ_G, blocks), jnp.int32),
            pltpu.SMEM((SEQ_G, blocks), jnp.int32),
            pltpu.SMEM(adapter_slot.shape, jnp.int32),
            pltpu.VMEM((blocks, CAP, width), BF),
            pltpu.SemaphoreType.DMA((4,)),
        ],
        compiler_params=params(4),
        name="pack",
    )(
        *far(
            prompt_lengths.T,
            adapter_ids.T,
            adapter_slot,
            tokens.reshape(blocks, CAP, width),
        )
    )
    arrived = lax.all_to_all(packed, "req", split_axis=0, concat_axis=0, tiled=True)
    w_far = [swap(w_out, 2 * y) for y in range(1, half)]
    w_near = swap(w_out, 1)
    odowns = [out_down.T] + [swap(out_down.T, r) for r in range(1, n_tp)]
    arrived, w_far, w_near, odowns = lax.optimization_barrier((arrived, w_far, w_near, odowns))
    count = 2
    step_blocks = n_req // count
    rows = step_blocks * CAP
    own = rows // n_tp
    beside = swap(arrived, 1)
    x_far = []
    for c in range(count):
        piece = arrived[c * step_blocks : (c + 1) * step_blocks]
        x_far.append([swap(piece, 2 * y) for y in range(1, half)])
    wouts = [w_out, w_near] + second_hop(w_far)
    x_far[0] = second_hop(x_far[0])
    x_far[0], wouts = lax.optimization_barrier((x_far[0], wouts))

    qkv_weights = far(
        w_qkv, jnp.swapaxes(qkv_down, 1, 2).reshape(3 * SPAN, feat), qkv_up
    )
    ffn_weights = far(w_fc1, w_fc2)
    consts = near(
        out_up, fc1_down.T, fc1_up, fc2_down.T, fc2_up, norm1_gain[None], norm1_bias[None]
    )
    steps = []
    for c in range(count):
        if c:
            x_far[c], steps[0][0] = lax.optimization_barrier((x_far[c], steps[0][0]))
            x_far[c] = second_hop(x_far[c])
        keep = [] if c else [
            pltpu.VMEM((3, feat, width), BF),
            pltpu.VMEM((3 * SPAN, feat), BF),
            pltpu.VMEM((6 * SPAN, 3 * width), BF),
        ]
        attended, sel, x_full, *kept = pl.pallas_call(
            functools.partial(attn_kernel, n_tp, c),
            out_shape=[
                pltpu.VMEM((rows, width), BF),
                pltpu.VMEM((rows, 4 * SPAN), BF),
                pltpu.VMEM((rows, feat), BF),
            ]
            + keep,
            in_specs=[SMEM] + [VM] * n_tp + [VM if c else HBM] * 3,
            out_specs=[VM] * (3 + len(keep)),
            scratch_shapes=[] if c else [
                pltpu.VMEM((3, SPAN, width), BF),
                pltpu.SemaphoreType.DMA((5,)),
            ],
            compiler_params=params(12),
            cost_estimate=work(2 * rows * feat * 3 * width + 4 * rows * width * 2 * CAP, rows),
            name="attend",
        )(me, *near(arrived, beside, *x_far[c]), *qkv_weights)
        if c == 0:
            qkv_weights = near(*kept)
        y_got = [swap(attended, 2 * y) for y in range(1, half)]
        if c:
            steps[0][1], attended = lax.optimization_barrier((steps[0][1], attended))
        steps.append([attended, y_got, sel, x_full])

    def finish(earlier, *values):
        blocks_done = step_blocks + sum(e.shape[0] for e in earlier)
        values = near(*earlier, *values, norm2_gain[None], norm2_bias[None])
        return pl.pallas_call(
            functools.partial(last_kernel, n_tp, len(earlier)),
            out_shape=pltpu.VMEM((blocks_done, n_tp, share, width), BF),
            in_specs=[VM] * len(values),
            out_specs=VM,
            compiler_params=params(8),
            name="finish",
        )(*values)

    for c in range(count):
        attended, y_got, sel, x_full = steps[c]
        atts = second_hop([attended] + y_got)
        if c:
            atts, firsts = lax.optimization_barrier((atts, firsts))
            firsts = [swap(piece, 2 * (y + 1)) for y, piece in enumerate(firsts)]
        keep = [] if c else [pltpu.VMEM(w_fc1.shape, BF), pltpu.VMEM(w_fc2.shape, BF)]
        even, odd, odds, h_own, *kept = pl.pallas_call(
            functools.partial(ffn_kernel, n_tp, c),
            out_shape=[
                pltpu.VMEM((half, own, feat), F32),
                pltpu.VMEM((own, feat), BF),
                pltpu.VMEM((half - 1, own, feat), BF),
                pltpu.VMEM((own, feat), BF),
            ]
            + keep,
            in_specs=[SMEM]
            + [VM] * (3 * n_tp + 2 + len(consts))
            + [VM if c else HBM] * 2,
            out_specs=[VM] * (4 + len(keep)),
            scratch_shapes=[pltpu.VMEM((step_blocks, n_tp, share, feat), BF)]
            + ([] if c else [pltpu.SemaphoreType.DMA((2,))]),
            compiler_params=params(16),
            cost_estimate=work(2 * rows * feat * (2 * w_fc1.shape[1] + feat), rows),
            name="feed",
        )(
            me,
            *near(*atts, *wouts, *odowns, x_full, sel),
            *consts,
            *ffn_weights,
        )
        if c == 0:
            ffn_weights = near(*kept)
        gots = swap(odds, 1)
        if c:
            earlier = finish([], *first_ends, *firsts)
            gots, earlier = lax.optimization_barrier((gots, earlier))
        sends = [(even[y] + gots[y - 1].astype(F32)).astype(BF) for y in range(1, half)]
        ends = [even, swap(odd, 1), h_own]
        if c == 0:
            firsts, first_ends = sends, ends
        else:
            sends = [swap(piece, 2 * (y + 1)) for y, piece in enumerate(sends)]
            done = finish([earlier], *ends, *sends)
    back = lax.all_to_all(
        done.reshape(n_req * n_tp, share, width),
        ("req", "tp"),
        split_axis=0,
        concat_axis=0,
        tiled=True,
    )
    result = pl.pallas_call(
        unpack_kernel,
        out_shape=jax.ShapeDtypeStruct((blocks, CAP, width), BF),
        in_specs=[SMEM, VM],
        out_specs=VM,
        compiler_params=params(4),
        name="unpack",
    )(owners, *near(back.reshape(n_req, CAP, width)))
    return result.reshape(blocks * CAP, width)


def solution(mesh):
    placed = (
        P("req", "tp"),
        P("req", None),
        P("req", None),
        P(),
        P(None, None, "tp"),
        P("tp", None),
        P(None, "tp"),
        P("tp", None),
        P(None, None, "req"),
        P(None, "req", "tp"),
        P("tp", "req"),
        P("req", None),
        P(None, "req"),
        P("req", "tp"),
        P("tp", "req"),
        P("req", None),
        P(),
        P(),
        P(),
        P(),
    )
    return jax.shard_map(
        body, mesh=mesh, in_specs=placed, out_specs=P("req", "tp"), check_vma=False
    )
```

```python
import functools

import jax
import jax.numpy as jnp
from jax import lax
from jax.experimental import pallas as pl
from jax.experimental.pallas import tpu as pltpu
from jax.sharding import PartitionSpec as P

HEAD_DIM = 64
RANK = 16
ADAPT_DEV = 2
CAP = 64
SEQ_G = 4
SPAN = ADAPT_DEV * RANK
PAD = 8
NORM_EPS = 1e-05
BF = jnp.bfloat16
F32 = jnp.float32


def dot(a, b):
    return lax.dot_general(a, b, (((1,), (0,)), ((), ())), preferred_element_type=F32)


def dot_t(a, b):
    return lax.dot_general(a, b, (((1,), (1,)), ((), ())), preferred_element_type=F32)


def layer_norm(values, gain, shift):
    mean = jnp.mean(values, axis=-1, keepdims=True)
    centred = values - mean
    variance = jnp.mean(centred * centred, axis=-1, keepdims=True)
    return centred * lax.rsqrt(variance + NORM_EPS) * gain + shift


def split_low(low, sel):
    low = low * sel
    high = low.astype(BF).astype(F32)
    return jnp.concatenate([high, low - high], axis=1).astype(BF)


def fetch(pairs, sems):
    copies = [
        pltpu.make_async_copy(src, dst, sems.at[i]) for i, (src, dst) in enumerate(pairs)
    ]
    for c in copies:
        c.start()
    return copies


def pack_kernel(
    lengths_in, ids_in, slots_in, tok_in, out, owners, lengths, ids, slots, tok, sems
):
    copies = fetch(
        [(lengths_in, lengths), (ids_in, ids), (slots_in, slots), (tok_in, tok)], sems
    )
    blocks = tok.shape[0]
    if out.shape[0] > blocks:
        out[...] = jnp.zeros(out.shape, out.dtype)
    width = out.shape[2]
    pos = lax.broadcasted_iota(jnp.int32, (PAD, width), 1) % CAP
    for c in copies:
        c.wait()
    for g in range(blocks):
        slot = [slots[ids[k, g]] for k in range(SEQ_G)]
        owner = slot[0] // ADAPT_DEV
        owners[g] = owner
        code = jnp.full((PAD, width), 1 + slot[0] % ADAPT_DEV, jnp.int32)
        end = jnp.int32(0)
        for k in range(1, SEQ_G):
            end = end + lengths[k - 1, g]
            code = jnp.where(pos >= end, 1 + k * ADAPT_DEV + slot[k] % ADAPT_DEV, code)
        out[owner, :CAP, :] = tok[g]
        out[owner, CAP:, :] = code.astype(F32).astype(BF)


def tiles(count, step):
    step(0)
    if count == 2:
        step(1)
    elif count > 2:
        lax.fori_loop(1, count, lambda t, c: (step(t), c)[1], 0)


def span(start, size):
    return pl.ds(start if isinstance(start, int) else pl.multiple_of(start, size), size)


def begin_kernel(
    me, own, beside, w_in, w1_in, w2_in, down_in, up_in, *refs
):
    acc, low, sel_out, bias_out, w, w1, w2, down, up_all, up, sems = refs
    pairs = [(up_in, up), (down_in, down)] + [(w_in.at[k], w.at[k]) for k in range(3)]
    for src, dst in ((w1_in, w1), (w2_in, w2)):
        half = src.shape[0] // 2
        pairs += [(src.at[:half], dst.at[:half]), (src.at[half:], dst.at[half:])]
    copies = fetch(pairs, sems)
    up_all[...] = jnp.zeros(up_all.shape, BF)
    copies[0].wait()
    for k in range(3):
        for part in range(2):
            first_row = (3 * part + k) * SPAN
            up_all[first_row : first_row + SPAN, k * up.shape[2] : (k + 1) * up.shape[2]] = up[k]
    for c in copies[1:5]:
        c.wait()
    blocks = own.shape[0]
    width = own.shape[2]
    tp = me[0]
    spans = [span(tp * width, width), span((tp ^ 1) * width, width)]
    pair_lane = lax.broadcasted_iota(jnp.int32, (2 * CAP, 2 * CAP), 1)
    pair_row = lax.broadcasted_iota(jnp.int32, (2 * CAP, 2 * CAP), 0)
    eye = pair_lane == pair_row
    lane_sel = ((pair_lane // RANK) % ADAPT_DEV).astype(F32)
    tile = min(4, blocks)

    def step(t):
        rs = span(t * (tile * CAP), tile * CAP)
        bs = pl.ds(t * tile, tile)
        xs = [part[bs, :CAP, :].reshape(tile * CAP, width) for part in (own, beside)]
        for k in range(3):
            acc[k, rs] = dot(xs[0], w[k, spans[0]]) + dot(xs[1], w[k, spans[1]])
        low[rs] = dot_t(xs[0], down[:, spans[0]]) + dot_t(xs[1], down[:, spans[1]])
        for p in range(tile // 2):
            b0 = t * tile + 2 * p
            c0 = own[b0, CAP : CAP + 1, : 2 * CAP].astype(F32)
            c1 = own[b0 + 1, CAP : CAP + 1, : 2 * CAP].astype(F32) + 64.0
            idr = jnp.where(pair_lane < CAP, c0, c1)
            idc = jnp.sum(jnp.where(eye, idr, 0.0), axis=1, keepdims=True)
            ps = span(t * (tile * CAP) + p * 2 * CAP, 2 * CAP)
            bias_out[ps] = jnp.where(idr == idc, 0.0, -1e30)
            pick = idc - 1.0
            pick = pick - 2.0 * jnp.floor(pick * 0.5)
            sel_out[ps] = (lane_sel == pick).astype(BF)

    tiles(blocks // tile, step)
    for c in copies[5:]:
        c.wait()


def attn_kernel(n_tp, chunk, me, *refs):
    parts = refs[:n_tp]
    acc, low_in, sel_in, bias, w, down, up_all, att, x_full = refs[n_tp:]
    blocks = att.shape[0] // CAP
    width = parts[0].shape[2]
    rows = blocks * CAP
    tp = me[0]
    spans = [span((tp ^ r) * width, width) for r in range(n_tp)]
    for r in range(n_tp):
        offset = chunk * blocks if part_of(parts[r], blocks) else 0
        x_full[:, spans[r]] = parts[r][offset : offset + blocks, :CAP, :].reshape(rows, width)
    first = lax.broadcasted_iota(jnp.int32, (2 * CAP, 2 * CAP), 1) < HEAD_DIM
    zero = jnp.zeros((), BF)
    tile = min(4, blocks)

    def step(t):
        start = t * (tile * CAP)
        rs = span(start, tile * CAP)
        whole = span(chunk * rows + start, tile * CAP)
        bs = pl.ds(t * tile, tile)
        xs = [parts[r][bs, :CAP, :].reshape(tile * CAP, width) for r in range(2, n_tp)]
        low = low_in[whole]
        for r in range(2, n_tp):
            low = low + dot_t(xs[r - 2], down[:, spans[r]])
        low = split_low(low, sel_in[whole].astype(F32)[:, : 3 * SPAN])
        qkv = []
        for k in range(3):
            total = acc[k, whole] + dot(low, up_all[:, k * width : (k + 1) * width])
            for r in range(2, n_tp):
                total = total + dot(xs[r - 2], w[k, spans[r]])
            qkv.append(total.astype(BF))
        q, k_, v = qkv
        q = (q.astype(F32) * HEAD_DIM**-0.5).astype(BF)
        for p in range(tile // 2):
            prs = slice(p * 2 * CAP, (p + 1) * 2 * CAP)
            out_rows = span(start + p * 2 * CAP, 2 * CAP)
            mask = bias[span(chunk * rows + start + p * 2 * CAP, 2 * CAP)]
            for h in range(width // (2 * HEAD_DIM)):
                cs = slice(h * 2 * HEAD_DIM, (h + 1) * 2 * HEAD_DIM)
                both = []
                for half in (first, ~first):
                    s = dot_t(jnp.where(half, q[prs, cs], zero), k_[prs, cs]) + mask
                    e = jnp.exp(s - jnp.max(s, axis=-1, keepdims=True))
                    inv = 1.0 / jnp.sum(e, axis=-1, keepdims=True)
                    both.append(dot((e * inv).astype(BF), v[prs, cs]))
                att[out_rows, cs] = jnp.where(first, *both).astype(BF)

    tiles(blocks // tile, step)


def part_of(array, blocks):
    return array.shape[0] > blocks


def ffn_kernel(n_tp, chunk, me, *refs):
    atts, wouts, odowns = refs[:n_tp], refs[n_tp : 2 * n_tp], refs[2 * n_tp : 3 * n_tp]
    x, sel_in, oup, d1, u1, d2, u2, g1, b1, w1, w2 = refs[3 * n_tp : 3 * n_tp + 11]
    even, odd, odds, h_own, h_scr = refs[3 * n_tp + 11 :]
    rows, feat = x.shape
    blocks = rows // CAP
    share = CAP // n_tp
    tp = me[0]
    size = min(rows, 256)
    nb = size // CAP
    ups = [jnp.concatenate([u[...], u[...]], axis=0) for u in (oup, u1, u2)]

    def step(t):
        rs = span(t * size, size)
        sel = sel_in[span(chunk * rows + t * size, size)].astype(F32)[:, :SPAN]
        total = x[rs].astype(F32)
        low = None
        for r in range(n_tp):
            a = atts[r][rs]
            total = total + dot(a, wouts[r][...])
            part = dot_t(a, odowns[r][...])
            low = part if low is None else low + part
        total = total + dot(split_low(low, sel), ups[0])
        h1 = layer_norm(total, g1[...], b1[...]).astype(BF)
        h_scr[span(t * nb, nb)] = h1.reshape(nb, n_tp, share, feat)
        gate = dot(h1, w1[...]) + dot(split_low(dot_t(h1, d1[...]), sel), ups[1])
        hidden = (0.5 * gate * (1.0 + lax.erf(gate * 0.7071067811865476))).astype(BF)
        term = dot(hidden, w2[...]) + dot(split_low(dot_t(hidden, d2[...]), sel), ups[2])
        term = term.reshape(nb, n_tp, share, feat)
        own_rows = span(t * (size // n_tp), size // n_tp)
        for j in range(n_tp):
            rel = tp ^ j
            piece = term[:, j].reshape(nb * share, feat)

            @pl.when(rel % 2 == 0)
            def _():
                even[rel // 2, own_rows, :] = piece

            @pl.when(rel == 1)
            def _():
                odd[own_rows, :] = piece.astype(BF)

            @pl.when((rel % 2 == 1) & (rel > 1))
            def _():
                odds[rel // 2 - 1, own_rows, :] = piece.astype(BF)

    tiles(rows // size, step)
    h_own[...] = h_scr[:, tp].reshape(blocks * share, feat)


def last_kernel(n_tp, earlier, *refs):
    g2, b2, out = refs[-3:]
    even, got, h_own = refs[earlier : earlier + 3]
    _, share, width = out.shape[1:]
    step = h_own.shape[0] // share
    total = h_own[...].astype(F32) + (even[0] + got[...].astype(F32))
    for arrived in refs[earlier + 3 : -3]:
        total = total + arrived[...].astype(F32)
    done = layer_norm(total, g2[...], b2[...]).astype(BF)
    if earlier:
        out[: refs[0].shape[0]] = refs[0][...]
    for f in range(n_tp):
        piece = done[:, f * width : (f + 1) * width].reshape(step, share, width)
        out[out.shape[0] - step :, f] = piece


def unpack_kernel(owners, arrived, out):
    for g in range(out.shape[0]):
        out[g] = arrived[owners[g]]


VM = pl.BlockSpec(memory_space=pltpu.VMEM)
HBM = pl.BlockSpec(memory_space=pltpu.HBM)
SMEM = pl.BlockSpec(memory_space=pltpu.SMEM)


def near(*arrays):
    return [pltpu.with_memory_space_constraint(a, pltpu.VMEM) for a in arrays]


def far(*arrays):
    return [pltpu.with_memory_space_constraint(a, pltpu.HBM) for a in arrays]


def work(flops, rows):
    return pl.CostEstimate(flops=5 * flops, transcendentals=rows * 1024, bytes_accessed=rows * 8192)


def params(mib=20):
    return pltpu.CompilerParams(vmem_limit_bytes=mib * 1024 * 1024)


def body(
    tokens,
    prompt_lengths,
    adapter_ids,
    adapter_slot,
    w_qkv,
    w_out,
    w_fc1,
    w_fc2,
    qkv_down,
    qkv_up,
    out_down,
    out_up,
    fc1_down,
    fc1_up,
    fc2_down,
    fc2_up,
    norm1_gain,
    norm1_bias,
    norm2_gain,
    norm2_bias,
):
    n_req = lax.axis_size("req")
    n_tp = lax.axis_size("tp")
    feat = w_qkv.shape[1]
    width = tokens.shape[1]
    blocks = tokens.shape[0] // CAP
    share = CAP // n_tp
    half = n_tp // 2
    me = jnp.reshape(lax.axis_index("tp"), (1,)).astype(jnp.int32)

    def swap(value, r):
        return lax.ppermute(value, "tp", [(i, i ^ r) for i in range(n_tp)])

    def second_hop(pieces):
        return [hop for piece in pieces for hop in (piece, swap(piece, 1))]

    packed, owners = pl.pallas_call(
        pack_kernel,
        out_shape=(
            pltpu.VMEM((n_req, CAP + PAD, width), BF),
            jax.ShapeDtypeStruct((blocks,), jnp.int32),
        ),
        in_specs=[HBM] * 4,
        out_specs=(VM, SMEM),
        scratch_shapes=[
            pltpu.SMEM((SEQ_G, blocks), jnp.int32),
            pltpu.SMEM((SEQ_G, blocks), jnp.int32),
            pltpu.SMEM(adapter_slot.shape, jnp.int32),
            pltpu.VMEM((blocks, CAP, width), BF),
            pltpu.SemaphoreType.DMA((4,)),
        ],
        compiler_params=params(4),
        name="pack",
    )(
        *far(
            prompt_lengths.T,
            adapter_ids.T,
            adapter_slot,
            tokens.reshape(blocks, CAP, width),
        )
    )
    packed, me, w_first, o_first = lax.optimization_barrier(
        (packed, me, w_out, out_down.T)
    )
    arrived = lax.all_to_all(packed, "req", split_axis=0, concat_axis=0, tiled=True)
    w_far = [swap(w_first, 2 * y) for y in range(1, half)]
    w_near = swap(w_first, 1)
    odowns = [out_down.T] + [swap(o_first, r) for r in range(1, n_tp)]
    arrived, w_far, w_near, odowns = lax.optimization_barrier((arrived, w_far, w_near, odowns))
    count = 2
    step_blocks = n_req // count
    rows = step_blocks * CAP
    own = rows // n_tp
    beside = swap(arrived, 1)
    x_far = []
    for c in range(count):
        piece = arrived[c * step_blocks : (c + 1) * step_blocks]
        x_far.append([swap(piece, 2 * y) for y in range(1, half)])
    *begun, w_all, w1, w2, downs, up_all = pl.pallas_call(
        begin_kernel,
        out_shape=[
            pltpu.VMEM((3, count * rows, width), F32),
            pltpu.VMEM((count * rows, 3 * SPAN), F32),
            pltpu.VMEM((count * rows, 4 * SPAN), BF),
            pltpu.VMEM((count * rows, 2 * CAP), F32),
            pltpu.VMEM((3, feat, width), BF),
            pltpu.VMEM(w_fc1.shape, BF),
            pltpu.VMEM(w_fc2.shape, BF),
            pltpu.VMEM((3 * SPAN, feat), BF),
            pltpu.VMEM((6 * SPAN, 3 * width), BF),
        ],
        in_specs=[SMEM] + [VM] * 2 + [HBM] * 5,
        out_specs=[VM] * 9,
        scratch_shapes=[
            pltpu.VMEM((3, SPAN, width), BF),
            pltpu.SemaphoreType.DMA((9,)),
        ],
        compiler_params=params(8),
        cost_estimate=work(rows * feat * 3 * width, rows),
        name="begin",
    )(
        me,
        *near(arrived, beside),
        *far(
            w_qkv,
            w_fc1,
            w_fc2,
            jnp.swapaxes(qkv_down, 1, 2).reshape(3 * SPAN, feat),
            qkv_up,
        ),
    )
    w_all, w1, w2, downs, up_all = near(w_all, w1, w2, downs, up_all)
    x_far[0], begun = lax.optimization_barrier((x_far[0], begun))
    x_far[0] = second_hop(x_far[0])

    consts = near(
        out_up, fc1_down.T, fc1_up, fc2_down.T, fc2_up, norm1_gain[None], norm1_bias[None]
    )
    sel = begun[2]
    steps = []
    for c in range(count):
        if c:
            x_far[c], w_far, steps[0][0] = lax.optimization_barrier(
                (x_far[c], w_far, steps[0][0])
            )
            x_far[c] = second_hop(x_far[c])
        attended, x_full = pl.pallas_call(
            functools.partial(attn_kernel, n_tp, c),
            out_shape=[pltpu.VMEM((rows, width), BF), pltpu.VMEM((rows, feat), BF)],
            in_specs=[SMEM] + [VM] * (n_tp + 7),
            out_specs=[VM] * 2,
            compiler_params=params(12),
            cost_estimate=work(2 * rows * feat * 3 * width + 4 * rows * width * 2 * CAP, rows),
            name="attend",
        )(me, *near(arrived, beside, *x_far[c], *begun), w_all, downs, up_all)
        y_got = [swap(attended, 2 * y) for y in range(1, half)]
        if c:
            steps[0][1], attended = lax.optimization_barrier((steps[0][1], attended))
        steps.append([attended, y_got, x_full])
    wouts = [w_out, w_near] + second_hop(w_far)

    def finish(earlier, *values):
        blocks_done = step_blocks + sum(e.shape[0] for e in earlier)
        values = near(*earlier, *values, norm2_gain[None], norm2_bias[None])
        return pl.pallas_call(
            functools.partial(last_kernel, n_tp, len(earlier)),
            out_shape=pltpu.VMEM((blocks_done, n_tp, share, width), BF),
            in_specs=[VM] * len(values),
            out_specs=VM,
            compiler_params=params(8),
            name="finish",
        )(*values)

    for c in range(count):
        attended, y_got, x_full = steps[c]
        atts = second_hop([attended] + y_got)
        if c:
            atts, firsts = lax.optimization_barrier((atts, firsts))
            firsts = [swap(piece, 2 * (y + 1)) for y, piece in enumerate(firsts)]
        even, odd, odds, h_own = pl.pallas_call(
            functools.partial(ffn_kernel, n_tp, c),
            out_shape=[
                pltpu.VMEM((half, own, feat), F32),
                pltpu.VMEM((own, feat), BF),
                pltpu.VMEM((half - 1, own, feat), BF),
                pltpu.VMEM((own, feat), BF),
            ],
            in_specs=[SMEM] + [VM] * (3 * n_tp + 4 + len(consts)),
            out_specs=[VM] * 4,
            scratch_shapes=[pltpu.VMEM((step_blocks, n_tp, share, feat), BF)],
            compiler_params=params(16),
            cost_estimate=work(2 * rows * feat * (2 * w_fc1.shape[1] + feat), rows),
            name="feed",
        )(me, *near(*atts, *wouts, *odowns, x_full, sel), *consts, w1, w2)
        gots = swap(odds, 1)
        if c:
            earlier = finish([], *first_ends, *firsts)
            gots, earlier = lax.optimization_barrier((gots, earlier))
        sends = [(even[y] + gots[y - 1].astype(F32)).astype(BF) for y in range(1, half)]
        ends = [even, swap(odd, 1), h_own]
        if c == 0:
            firsts, first_ends = sends, ends
        else:
            sends = [swap(piece, 2 * (y + 1)) for y, piece in enumerate(sends)]
            done = finish([earlier], *ends, *sends)
    back = lax.all_to_all(
        done.reshape(n_req * n_tp, share, width),
        ("req", "tp"),
        split_axis=0,
        concat_axis=0,
        tiled=True,
    )
    result = pl.pallas_call(
        unpack_kernel,
        out_shape=jax.ShapeDtypeStruct((blocks, CAP, width), BF),
        in_specs=[SMEM, VM],
        out_specs=VM,
        compiler_params=params(4),
        name="unpack",
    )(owners, *near(back.reshape(n_req, CAP, width)))
    return result.reshape(blocks * CAP, width)


def solution(mesh):
    placed = (
        P("req", "tp"),
        P("req", None),
        P("req", None),
        P(),
        P(None, None, "tp"),
        P("tp", None),
        P(None, "tp"),
        P("tp", None),
        P(None, None, "req"),
        P(None, "req", "tp"),
        P("tp", "req"),
        P("req", None),
        P(None, "req"),
        P("req", "tp"),
        P("tp", "req"),
        P("req", None),
        P(),
        P(),
        P(),
        P(),
    )
    return jax.shard_map(
        body, mesh=mesh, in_specs=placed, out_specs=P("req", "tp"), check_vma=False
    )
```

```python
import functools

import jax
import jax.numpy as jnp
from jax import lax
from jax.experimental import pallas as pl
from jax.experimental.pallas import tpu as pltpu
from jax.sharding import PartitionSpec as P

HEAD_DIM = 64
RANK = 16
ADAPT_DEV = 2
CAP = 64
SEQ_G = 4
SPAN = ADAPT_DEV * RANK
PAD = 8
NORM_EPS = 1e-05
BF = jnp.bfloat16
F32 = jnp.float32


def dot(a, b):
    return lax.dot_general(a, b, (((1,), (0,)), ((), ())), preferred_element_type=F32)


def dot_t(a, b):
    return lax.dot_general(a, b, (((1,), (1,)), ((), ())), preferred_element_type=F32)


def layer_norm(values, gain, shift):
    mean = jnp.mean(values, axis=-1, keepdims=True)
    centred = values - mean
    variance = jnp.mean(centred * centred, axis=-1, keepdims=True)
    return centred * lax.rsqrt(variance + NORM_EPS) * gain + shift


def split_low(low, sel):
    low = low * sel
    high = low.astype(BF).astype(F32)
    return jnp.concatenate([high, low - high], axis=1).astype(BF)


def fetch(pairs, sems):
    copies = [
        pltpu.make_async_copy(src, dst, sems.at[i]) for i, (src, dst) in enumerate(pairs)
    ]
    for c in copies:
        c.start()
    return copies


def pack_kernel(
    lengths_in, ids_in, slots_in, tok_in, out, owners, lengths, ids, slots, tok, sems
):
    copies = fetch(
        [(lengths_in, lengths), (ids_in, ids), (slots_in, slots), (tok_in, tok)], sems
    )
    blocks = tok.shape[0]
    if out.shape[0] > blocks:
        out[...] = jnp.zeros(out.shape, out.dtype)
    width = out.shape[2]
    pos = lax.broadcasted_iota(jnp.int32, (PAD, width), 1) % CAP
    for c in copies:
        c.wait()
    for g in range(blocks):
        slot = [slots[ids[k, g]] for k in range(SEQ_G)]
        owner = slot[0] // ADAPT_DEV
        owners[g] = owner
        code = jnp.full((PAD, width), 1 + slot[0] % ADAPT_DEV, jnp.int32)
        end = jnp.int32(0)
        for k in range(1, SEQ_G):
            end = end + lengths[k - 1, g]
            code = jnp.where(pos >= end, 1 + k * ADAPT_DEV + slot[k] % ADAPT_DEV, code)
        out[owner, :CAP, :] = tok[g]
        out[owner, CAP:, :] = code.astype(F32).astype(BF)


def tiles(count, step):
    step(0)
    if count == 2:
        step(1)
    elif count > 2:
        lax.fori_loop(1, count, lambda t, c: (step(t), c)[1], 0)


def span(start, size):
    return pl.ds(start if isinstance(start, int) else pl.multiple_of(start, size), size)


def begin_kernel(
    me, own, beside, w_in, w1_in, w2_in, down_in, up_in, *refs
):
    acc, low, sel_out, bias_out, w, w1, w2, down, up_all, up, sems = refs
    pairs = [(up_in, up), (down_in, down)] + [(w_in.at[k], w.at[k]) for k in range(3)]
    for src, dst in ((w1_in, w1), (w2_in, w2)):
        half = src.shape[0] // 2
        pairs += [(src.at[:half], dst.at[:half]), (src.at[half:], dst.at[half:])]
    copies = fetch(pairs, sems)
    up_all[...] = jnp.zeros(up_all.shape, BF)
    copies[0].wait()
    for k in range(3):
        for part in range(2):
            first_row = (3 * part + k) * SPAN
            up_all[first_row : first_row + SPAN, k * up.shape[2] : (k + 1) * up.shape[2]] = up[k]
    for c in copies[1:5]:
        c.wait()
    blocks = own.shape[0]
    width = own.shape[2]
    tp = me[0]
    spans = [span(tp * width, width), span((tp ^ 1) * width, width)]
    pair_lane = lax.broadcasted_iota(jnp.int32, (2 * CAP, 2 * CAP), 1)
    pair_row = lax.broadcasted_iota(jnp.int32, (2 * CAP, 2 * CAP), 0)
    eye = pair_lane == pair_row
    lane_sel = ((pair_lane // RANK) % ADAPT_DEV).astype(F32)
    tile = min(4, blocks)

    def step(t):
        rs = span(t * (tile * CAP), tile * CAP)
        bs = pl.ds(t * tile, tile)
        xs = [part[bs, :CAP, :].reshape(tile * CAP, width) for part in (own, beside)]
        for k in range(3):
            acc[k, rs] = dot(xs[0], w[k, spans[0]]) + dot(xs[1], w[k, spans[1]])
        low[rs] = dot_t(xs[0], down[:, spans[0]]) + dot_t(xs[1], down[:, spans[1]])
        for p in range(tile // 2):
            b0 = t * tile + 2 * p
            c0 = own[b0, CAP : CAP + 1, : 2 * CAP].astype(F32)
            c1 = own[b0 + 1, CAP : CAP + 1, : 2 * CAP].astype(F32) + 64.0
            idr = jnp.where(pair_lane < CAP, c0, c1)
            idc = jnp.sum(jnp.where(eye, idr, 0.0), axis=1, keepdims=True)
            ps = span(t * (tile * CAP) + p * 2 * CAP, 2 * CAP)
            bias_out[ps] = jnp.where(idr == idc, 0.0, -1e30)
            pick = idc - 1.0
            pick = pick - 2.0 * jnp.floor(pick * 0.5)
            sel_out[ps] = (lane_sel == pick).astype(BF)

    tiles(blocks // tile, step)
    for c in copies[5:]:
        c.wait()


def attn_kernel(n_tp, chunk, me, *refs):
    parts = refs[:n_tp]
    acc, low_in, sel_in, bias, w, down, up_all, att, x_full = refs[n_tp:]
    blocks = att.shape[0] // CAP
    width = parts[0].shape[2]
    rows = blocks * CAP
    tp = me[0]
    spans = [span((tp ^ r) * width, width) for r in range(n_tp)]
    for r in range(n_tp):
        chunk_part = parts[r][chunk * blocks : (chunk + 1) * blocks, :CAP, :]
        x_full[:, spans[r]] = chunk_part.reshape(rows, width)
    first = lax.broadcasted_iota(jnp.int32, (2 * CAP, 2 * CAP), 1) < HEAD_DIM
    zero = jnp.zeros((), BF)
    tile = min(4, blocks)

    def step(t):
        start = t * (tile * CAP)
        rs = span(start, tile * CAP)
        whole = span(chunk * rows + start, tile * CAP)
        bs = pl.ds(chunk * blocks + t * tile, tile)
        xs = [parts[r][bs, :CAP, :].reshape(tile * CAP, width) for r in range(2, n_tp)]
        low = low_in[whole]
        for r in range(2, n_tp):
            low = low + dot_t(xs[r - 2], down[:, spans[r]])
        low = split_low(low, sel_in[whole].astype(F32)[:, : 3 * SPAN])
        qkv = []
        for k in range(3):
            total = acc[k, whole] + dot(low, up_all[:, k * width : (k + 1) * width])
            for r in range(2, n_tp):
                total = total + dot(xs[r - 2], w[k, spans[r]])
            qkv.append(total.astype(BF))
        q, k_, v = qkv
        q = (q.astype(F32) * HEAD_DIM**-0.5).astype(BF)
        for p in range(tile // 2):
            prs = slice(p * 2 * CAP, (p + 1) * 2 * CAP)
            out_rows = span(start + p * 2 * CAP, 2 * CAP)
            mask = bias[span(chunk * rows + start + p * 2 * CAP, 2 * CAP)]
            for h in range(width // (2 * HEAD_DIM)):
                cs = slice(h * 2 * HEAD_DIM, (h + 1) * 2 * HEAD_DIM)
                both = []
                for half in (first, ~first):
                    s = dot_t(jnp.where(half, q[prs, cs], zero), k_[prs, cs]) + mask
                    e = jnp.exp(s - jnp.max(s, axis=-1, keepdims=True))
                    inv = 1.0 / jnp.sum(e, axis=-1, keepdims=True)
                    both.append(dot((e * inv).astype(BF), v[prs, cs]))
                att[out_rows, cs] = jnp.where(first, *both).astype(BF)

    tiles(blocks // tile, step)


def ffn_kernel(n_tp, chunk, me, *refs):
    atts, wouts, odowns = refs[:n_tp], refs[n_tp : 2 * n_tp], refs[2 * n_tp : 3 * n_tp]
    x, sel_in, oup, d1, u1, d2, u2, g1, b1, w1, w2 = refs[3 * n_tp : 3 * n_tp + 11]
    even, odd, odds, h_own, h_scr = refs[3 * n_tp + 11 :]
    rows, feat = x.shape
    blocks = rows // CAP
    share = CAP // n_tp
    tp = me[0]
    size = min(rows, 256)
    nb = size // CAP
    ups = [jnp.concatenate([u[...], u[...]], axis=0) for u in (oup, u1, u2)]

    def step(t):
        rs = span(t * size, size)
        sel = sel_in[span(chunk * rows + t * size, size)].astype(F32)[:, :SPAN]
        total = x[rs].astype(F32)
        low = None
        for r in range(n_tp):
            a = atts[r][rs]
            total = total + dot(a, wouts[r][...])
            part = dot_t(a, odowns[r][...])
            low = part if low is None else low + part
        total = total + dot(split_low(low, sel), ups[0])
        h1 = layer_norm(total, g1[...], b1[...]).astype(BF)
        h_scr[span(t * nb, nb)] = h1.reshape(nb, n_tp, share, feat)
        gate = dot(h1, w1[...]) + dot(split_low(dot_t(h1, d1[...]), sel), ups[1])
        hidden = (0.5 * gate * (1.0 + lax.erf(gate * 0.7071067811865476))).astype(BF)
        term = dot(hidden, w2[...]) + dot(split_low(dot_t(hidden, d2[...]), sel), ups[2])
        term = term.reshape(nb, n_tp, share, feat)
        own_rows = span(t * (size // n_tp), size // n_tp)
        for j in range(n_tp):
            rel = tp ^ j
            piece = term[:, j].reshape(nb * share, feat)

            @pl.when(rel % 2 == 0)
            def _():
                even[rel // 2, own_rows, :] = piece

            @pl.when(rel == 1)
            def _():
                odd[own_rows, :] = piece.astype(BF)

            @pl.when((rel % 2 == 1) & (rel > 1))
            def _():
                odds[rel // 2 - 1, own_rows, :] = piece.astype(BF)

    tiles(rows // size, step)
    h_own[...] = h_scr[:, tp].reshape(blocks * share, feat)


def last_kernel(n_tp, earlier, *refs):
    g2, b2, out = refs[-3:]
    even, got, h_own = refs[earlier : earlier + 3]
    _, share, width = out.shape[1:]
    step = h_own.shape[0] // share
    total = h_own[...].astype(F32) + (even[0] + got[...].astype(F32))
    for arrived in refs[earlier + 3 : -3]:
        total = total + arrived[...].astype(F32)
    done = layer_norm(total, g2[...], b2[...]).astype(BF)
    if earlier:
        out[: refs[0].shape[0]] = refs[0][...]
    for f in range(n_tp):
        piece = done[:, f * width : (f + 1) * width].reshape(step, share, width)
        out[out.shape[0] - step :, f] = piece


def unpack_kernel(owners, arrived, out):
    for g in range(out.shape[0]):
        out[g] = arrived[owners[g]]


VM = pl.BlockSpec(memory_space=pltpu.VMEM)
HBM = pl.BlockSpec(memory_space=pltpu.HBM)
SMEM = pl.BlockSpec(memory_space=pltpu.SMEM)


def near(*arrays):
    return [pltpu.with_memory_space_constraint(a, pltpu.VMEM) for a in arrays]


def far(*arrays):
    return [pltpu.with_memory_space_constraint(a, pltpu.HBM) for a in arrays]


def work(flops, rows):
    return pl.CostEstimate(flops=5 * flops, transcendentals=rows * 1024, bytes_accessed=rows * 8192)


def params(mib=20):
    return pltpu.CompilerParams(vmem_limit_bytes=mib * 1024 * 1024)


def body(
    tokens,
    prompt_lengths,
    adapter_ids,
    adapter_slot,
    w_qkv,
    w_out,
    w_fc1,
    w_fc2,
    qkv_down,
    qkv_up,
    out_down,
    out_up,
    fc1_down,
    fc1_up,
    fc2_down,
    fc2_up,
    norm1_gain,
    norm1_bias,
    norm2_gain,
    norm2_bias,
):
    n_req = lax.axis_size("req")
    n_tp = lax.axis_size("tp")
    feat = w_qkv.shape[1]
    width = tokens.shape[1]
    blocks = tokens.shape[0] // CAP
    share = CAP // n_tp
    half = n_tp // 2
    me = jnp.reshape(lax.axis_index("tp"), (1,)).astype(jnp.int32)

    def swap(value, r):
        return lax.ppermute(value, "tp", [(i, i ^ r) for i in range(n_tp)])

    def second_hop(pieces):
        return [hop for piece in pieces for hop in (piece, swap(piece, 1))]

    packed, owners = pl.pallas_call(
        pack_kernel,
        out_shape=(
            pltpu.VMEM((n_req, CAP + PAD, width), BF),
            jax.ShapeDtypeStruct((blocks,), jnp.int32),
        ),
        in_specs=[HBM] * 4,
        out_specs=(VM, SMEM),
        scratch_shapes=[
            pltpu.SMEM((SEQ_G, blocks), jnp.int32),
            pltpu.SMEM((SEQ_G, blocks), jnp.int32),
            pltpu.SMEM(adapter_slot.shape, jnp.int32),
            pltpu.VMEM((blocks, CAP, width), BF),
            pltpu.SemaphoreType.DMA((4,)),
        ],
        compiler_params=params(4),
        name="pack",
    )(
        *far(
            prompt_lengths.T,
            adapter_ids.T,
            adapter_slot,
            tokens.reshape(blocks, CAP, width),
        )
    )
    packed, me, w_first, o_first = lax.optimization_barrier(
        (packed, me, w_out, out_down.T)
    )
    arrived = lax.all_to_all(packed, "req", split_axis=0, concat_axis=0, tiled=True)
    w_far = [swap(w_first, 2 * y) for y in range(1, half)]
    w_near = swap(w_first, 1)
    odowns = [out_down.T] + [swap(o_first, r) for r in range(1, n_tp)]
    arrived, w_far, w_near, odowns = lax.optimization_barrier((arrived, w_far, w_near, odowns))
    count = 2
    step_blocks = n_req // count
    rows = step_blocks * CAP
    own = rows // n_tp
    beside = swap(arrived, 1)
    x_far = [swap(arrived, 2 * y) for y in range(1, half)]
    *begun, w_all, w1, w2, downs, up_all = pl.pallas_call(
        begin_kernel,
        out_shape=[
            pltpu.VMEM((3, count * rows, width), F32),
            pltpu.VMEM((count * rows, 3 * SPAN), F32),
            pltpu.VMEM((count * rows, 4 * SPAN), BF),
            pltpu.VMEM((count * rows, 2 * CAP), F32),
            pltpu.VMEM((3, feat, width), BF),
            pltpu.VMEM(w_fc1.shape, BF),
            pltpu.VMEM(w_fc2.shape, BF),
            pltpu.VMEM((3 * SPAN, feat), BF),
            pltpu.VMEM((6 * SPAN, 3 * width), BF),
        ],
        in_specs=[SMEM] + [VM] * 2 + [HBM] * 5,
        out_specs=[VM] * 9,
        scratch_shapes=[
            pltpu.VMEM((3, SPAN, width), BF),
            pltpu.SemaphoreType.DMA((9,)),
        ],
        compiler_params=params(8),
        cost_estimate=work(rows * feat * 3 * width, rows),
        name="begin",
    )(
        me,
        *near(arrived, beside),
        *far(
            w_qkv,
            w_fc1,
            w_fc2,
            jnp.swapaxes(qkv_down, 1, 2).reshape(3 * SPAN, feat),
            qkv_up,
        ),
    )
    w_all, w1, w2, downs, up_all = near(w_all, w1, w2, downs, up_all)
    x_far, begun = lax.optimization_barrier((x_far, begun))
    x_far = second_hop(x_far)

    consts = near(
        out_up, fc1_down.T, fc1_up, fc2_down.T, fc2_up, norm1_gain[None], norm1_bias[None]
    )
    sel = begun[2]
    steps = []
    for c in range(count):
        attended, x_full = pl.pallas_call(
            functools.partial(attn_kernel, n_tp, c),
            out_shape=[pltpu.VMEM((rows, width), BF), pltpu.VMEM((rows, feat), BF)],
            in_specs=[SMEM] + [VM] * (n_tp + 7),
            out_specs=[VM] * 2,
            compiler_params=params(12),
            cost_estimate=work(2 * rows * feat * 3 * width + 4 * rows * width * 2 * CAP, rows),
            name="attend",
        )(me, *near(arrived, beside, *x_far, *begun), w_all, downs, up_all)
        y_got = [swap(attended, 2 * y) for y in range(1, half)]
        if c:
            steps[0][1], attended, w_far = lax.optimization_barrier(
                (steps[0][1], attended, w_far)
            )
        steps.append([attended, y_got, x_full])
    wouts = [w_out, w_near] + second_hop(w_far)

    def finish(earlier, *values):
        blocks_done = step_blocks + sum(e.shape[0] for e in earlier)
        values = near(*earlier, *values, norm2_gain[None], norm2_bias[None])
        return pl.pallas_call(
            functools.partial(last_kernel, n_tp, len(earlier)),
            out_shape=pltpu.VMEM((blocks_done, n_tp, share, width), BF),
            in_specs=[VM] * len(values),
            out_specs=VM,
            compiler_params=params(8),
            name="finish",
        )(*values)

    for c in range(count):
        attended, y_got, x_full = steps[c]
        atts = second_hop([attended] + y_got)
        if c:
            atts, firsts = lax.optimization_barrier((atts, firsts))
            firsts = [swap(piece, 2 * (y + 1)) for y, piece in enumerate(firsts)]
        even, odd, odds, h_own = pl.pallas_call(
            functools.partial(ffn_kernel, n_tp, c),
            out_shape=[
                pltpu.VMEM((half, own, feat), F32),
                pltpu.VMEM((own, feat), BF),
                pltpu.VMEM((half - 1, own, feat), BF),
                pltpu.VMEM((own, feat), BF),
            ],
            in_specs=[SMEM] + [VM] * (3 * n_tp + 4 + len(consts)),
            out_specs=[VM] * 4,
            scratch_shapes=[pltpu.VMEM((step_blocks, n_tp, share, feat), BF)],
            compiler_params=params(16),
            cost_estimate=work(2 * rows * feat * (2 * w_fc1.shape[1] + feat), rows),
            name="feed",
        )(me, *near(*atts, *wouts, *odowns, x_full, sel), *consts, w1, w2)
        gots = swap(odds, 1)
        if c:
            earlier = finish([], *first_ends, *firsts)
            gots, earlier = lax.optimization_barrier((gots, earlier))
        sends = [(even[y] + gots[y - 1].astype(F32)).astype(BF) for y in range(1, half)]
        odd, sends = lax.optimization_barrier((odd, sends))
        ends = [even, swap(odd, 1), h_own]
        if c == 0:
            firsts, first_ends = sends, ends
        else:
            sends = [swap(piece, 2 * (y + 1)) for y, piece in enumerate(sends)]
            done = finish([earlier], *ends, *sends)
    back = lax.all_to_all(
        done.reshape(n_req * n_tp, share, width),
        ("req", "tp"),
        split_axis=0,
        concat_axis=0,
        tiled=True,
    )
    result = pl.pallas_call(
        unpack_kernel,
        out_shape=jax.ShapeDtypeStruct((blocks, CAP, width), BF),
        in_specs=[SMEM, VM],
        out_specs=VM,
        compiler_params=params(4),
        name="unpack",
    )(owners, *near(back.reshape(n_req, CAP, width)))
    return result.reshape(blocks * CAP, width)


def solution(mesh):
    placed = (
        P("req", "tp"),
        P("req", None),
        P("req", None),
        P(),
        P(None, None, "tp"),
        P("tp", None),
        P(None, "tp"),
        P("tp", None),
        P(None, None, "req"),
        P(None, "req", "tp"),
        P("tp", "req"),
        P("req", None),
        P(None, "req"),
        P("req", "tp"),
        P("tp", "req"),
        P("req", None),
        P(),
        P(),
        P(),
        P(),
    )
    return jax.shard_map(
        body, mesh=mesh, in_specs=placed, out_specs=P("req", "tp"), check_vma=False
    )
```

```python
import functools

import jax
import jax.numpy as jnp
from jax import lax
from jax.experimental import pallas as pl
from jax.experimental.pallas import tpu as pltpu
from jax.sharding import PartitionSpec as P

HEAD_DIM = 64
RANK = 16
ADAPT_DEV = 2
CAP = 64
SEQ_G = 4
SPAN = ADAPT_DEV * RANK
PAD = 8
NORM_EPS = 1e-05
BF = jnp.bfloat16
F32 = jnp.float32


def dot(a, b):
    return lax.dot_general(a, b, (((1,), (0,)), ((), ())), preferred_element_type=F32)


def dot_t(a, b):
    return lax.dot_general(a, b, (((1,), (1,)), ((), ())), preferred_element_type=F32)


def layer_norm(values, gain, shift):
    mean = jnp.mean(values, axis=-1, keepdims=True)
    centred = values - mean
    variance = jnp.mean(centred * centred, axis=-1, keepdims=True)
    return centred * lax.rsqrt(variance + NORM_EPS) * gain + shift


def split_low(low, sel):
    low = low * sel
    high = low.astype(BF).astype(F32)
    return jnp.concatenate([high, low - high], axis=1).astype(BF)


def fetch(pairs, sems):
    copies = [
        pltpu.make_async_copy(src, dst, sems.at[i]) for i, (src, dst) in enumerate(pairs)
    ]
    for c in copies:
        c.start()
    return copies


def twice(ref):
    return jnp.concatenate([ref[...], ref[...]], axis=0)


def split_two(low, sel):
    low = low * sel
    high = low.astype(BF).astype(F32)
    lane = lax.broadcasted_iota(jnp.int32, low.shape, 1)
    return jnp.where(lane < low.shape[1] // 2, high, low - high).astype(BF)


def pack_kernel(
    lengths_in, ids_in, slots_in, tok_in, out, owners, lengths, ids, slots, tok, sems
):
    copies = fetch(
        [(lengths_in, lengths), (ids_in, ids), (slots_in, slots), (tok_in, tok)], sems
    )
    blocks = tok.shape[0]
    if out.shape[0] > blocks:
        out[...] = jnp.zeros(out.shape, out.dtype)
    width = out.shape[2]
    pos = lax.broadcasted_iota(jnp.int32, (PAD, width), 1) % CAP
    for c in copies:
        c.wait()
    for g in range(blocks):
        slot = [slots[ids[k, g]] for k in range(SEQ_G)]
        owner = slot[0] // ADAPT_DEV
        owners[g] = owner
        code = jnp.full((PAD, width), 1 + slot[0] % ADAPT_DEV, jnp.int32)
        end = jnp.int32(0)
        for k in range(1, SEQ_G):
            end = end + lengths[k - 1, g]
            code = jnp.where(pos >= end, 1 + k * ADAPT_DEV + slot[k] % ADAPT_DEV, code)
        out[owner, :CAP, :] = tok[g]
        out[owner, CAP:, :] = code.astype(F32).astype(BF)


def tiles(count, step):
    step(0)
    if count == 2:
        step(1)
    elif count > 2:
        lax.fori_loop(1, count, lambda t, c: (step(t), c)[1], 0)


def span(start, size):
    return pl.ds(start if isinstance(start, int) else pl.multiple_of(start, size), size)


def begin_kernel(
    me, own, beside, w_in, w1_in, w2_in, down_in, up_in, *refs
):
    acc, low, sel_out, bias_out, w, w1, w2, down, up_all, up, sems = refs
    pairs = [(up_in, up), (down_in, down)] + [(w_in.at[k], w.at[k]) for k in range(3)]
    for src, dst in ((w1_in, w1), (w2_in, w2)):
        half = src.shape[0] // 2
        pairs += [(src.at[:half], dst.at[:half]), (src.at[half:], dst.at[half:])]
    copies = fetch(pairs, sems)
    up_all[...] = jnp.zeros(up_all.shape, BF)
    copies[0].wait()
    for k in range(3):
        for part in range(2):
            first_row = (3 * part + k) * SPAN
            up_all[first_row : first_row + SPAN, k * up.shape[2] : (k + 1) * up.shape[2]] = up[k]
    for c in copies[1:5]:
        c.wait()
    blocks = own.shape[0]
    width = own.shape[2]
    tp = me[0]
    spans = [span(tp * width, width), span((tp ^ 1) * width, width)]
    pair_lane = lax.broadcasted_iota(jnp.int32, (2 * CAP, 2 * CAP), 1)
    pair_row = lax.broadcasted_iota(jnp.int32, (2 * CAP, 2 * CAP), 0)
    eye = pair_lane == pair_row
    lane_sel = ((pair_lane // RANK) % ADAPT_DEV).astype(F32)
    tile = min(4, blocks)

    def step(t):
        rs = span(t * (tile * CAP), tile * CAP)
        bs = pl.ds(t * tile, tile)
        xs = [part[bs, :CAP, :].reshape(tile * CAP, width) for part in (own, beside)]
        for k in range(3):
            acc[k, rs] = dot(xs[0], w[k, spans[0]]) + dot(xs[1], w[k, spans[1]])
        low[rs] = dot_t(xs[0], down[:, spans[0]]) + dot_t(xs[1], down[:, spans[1]])
        for p in range(tile // 2):
            b0 = t * tile + 2 * p
            c0 = own[b0, CAP : CAP + 1, : 2 * CAP].astype(F32)
            c1 = own[b0 + 1, CAP : CAP + 1, : 2 * CAP].astype(F32) + 64.0
            idr = jnp.where(pair_lane < CAP, c0, c1)
            idc = jnp.sum(jnp.where(eye, idr, 0.0), axis=1, keepdims=True)
            ps = span(t * (tile * CAP) + p * 2 * CAP, 2 * CAP)
            bias_out[ps] = jnp.where(idr == idc, 0.0, -1e30)
            pick = idc - 1.0
            pick = pick - 2.0 * jnp.floor(pick * 0.5)
            sel_out[ps] = (lane_sel == pick).astype(BF)

    tiles(blocks // tile, step)
    for c in copies[5:]:
        c.wait()


def attn_kernel(n_tp, chunk, me, *refs):
    parts = refs[:n_tp]
    acc, low_in, sel_in, bias, w, down, up_all, att, x_full = refs[n_tp:]
    blocks = att.shape[0] // CAP
    width = parts[0].shape[2]
    rows = blocks * CAP
    tp = me[0]
    spans = [span((tp ^ r) * width, width) for r in range(n_tp)]
    for r in range(n_tp):
        offset = chunk * blocks if part_of(parts[r], blocks) else 0
        x_full[:, spans[r]] = parts[r][offset : offset + blocks, :CAP, :].reshape(rows, width)
    first = lax.broadcasted_iota(jnp.int32, (2 * CAP, 2 * CAP), 1) < HEAD_DIM
    zero = jnp.zeros((), BF)
    tile = min(4, blocks)

    def step(t):
        start = t * (tile * CAP)
        rs = span(start, tile * CAP)
        whole = span(chunk * rows + start, tile * CAP)
        bs = pl.ds(t * tile, tile)
        xs = [parts[r][bs, :CAP, :].reshape(tile * CAP, width) for r in range(2, n_tp)]
        low = low_in[whole]
        for r in range(2, n_tp):
            low = low + dot_t(xs[r - 2], down[:, spans[r]])
        low = split_low(low, sel_in[whole].astype(F32)[:, : 3 * SPAN])
        qkv = []
        for k in range(3):
            total = acc[k, whole] + dot(low, up_all[:, k * width : (k + 1) * width])
            for r in range(2, n_tp):
                total = total + dot(xs[r - 2], w[k, spans[r]])
            qkv.append(total.astype(BF))
        q, k_, v = qkv
        q = (q.astype(F32) * HEAD_DIM**-0.5).astype(BF)
        for p in range(tile // 2):
            prs = slice(p * 2 * CAP, (p + 1) * 2 * CAP)
            out_rows = span(start + p * 2 * CAP, 2 * CAP)
            mask = bias[span(chunk * rows + start + p * 2 * CAP, 2 * CAP)]
            for h in range(width // (2 * HEAD_DIM)):
                cs = slice(h * 2 * HEAD_DIM, (h + 1) * 2 * HEAD_DIM)
                both = []
                for half in (first, ~first):
                    s = dot_t(jnp.where(half, q[prs, cs], zero), k_[prs, cs]) + mask
                    e = jnp.exp(s - jnp.max(s, axis=-1, keepdims=True))
                    inv = 1.0 / jnp.sum(e, axis=-1, keepdims=True)
                    both.append(dot((e * inv).astype(BF), v[prs, cs]))
                att[out_rows, cs] = jnp.where(first, *both).astype(BF)

    tiles(blocks // tile, step)


def part_of(array, blocks):
    return array.shape[0] > blocks


def ffn_kernel(n_tp, chunk, me, *refs):
    atts, wouts, odowns = refs[:n_tp], refs[n_tp : 2 * n_tp], refs[2 * n_tp : 3 * n_tp]
    x, sel_in, oup, d1, u1, d2, u2, g1, b1, w1, w2 = refs[3 * n_tp : 3 * n_tp + 11]
    even, odd, odds, h_own, h_scr = refs[3 * n_tp + 11 :]
    rows, feat = x.shape
    blocks = rows // CAP
    share = CAP // n_tp
    tp = me[0]
    size = min(rows, 256)
    nb = size // CAP
    ups = [jnp.concatenate([u[...], u[...]], axis=0) for u in (oup, u1, u2)]

    def step(t):
        rs = span(t * size, size)
        sel = sel_in[span(chunk * rows + t * size, size)].astype(F32)[:, : 2 * SPAN]
        low = None
        for r in range(n_tp):
            part = dot_t(atts[r][rs], twice(odowns[r]))
            low = part if low is None else low + part
        low = split_two(low, sel)
        total = x[rs].astype(F32)
        for r in range(n_tp):
            total = total + dot(atts[r][rs], wouts[r][...])
        total = total + dot(low, ups[0])
        h1 = layer_norm(total, g1[...], b1[...]).astype(BF)
        h_scr[span(t * nb, nb)] = h1.reshape(nb, n_tp, share, feat)
        low = split_two(dot_t(h1, twice(d1)), sel)
        pieces = []
        for n in range(4):
            ns = slice(n * w1.shape[1] // 4, (n + 1) * w1.shape[1] // 4)
            gate = dot(h1, w1[:, ns]) + dot(low, ups[1][:, ns])
            pieces.append((0.5 * gate * (1.0 + lax.erf(gate * 0.7071067811865476))).astype(BF))
        hidden = jnp.concatenate(pieces, axis=1)
        low = split_two(dot_t(hidden, twice(d2)), sel)
        term = dot(hidden, w2[...]) + dot(low, ups[2])
        term = term.reshape(nb, n_tp, share, feat)
        own_rows = span(t * (size // n_tp), size // n_tp)
        for j in range(n_tp):
            rel = tp ^ j
            piece = term[:, j].reshape(nb * share, feat)

            @pl.when(rel % 2 == 0)
            def _():
                even[rel // 2, own_rows, :] = piece

            @pl.when(rel == 1)
            def _():
                odd[own_rows, :] = piece.astype(BF)

            @pl.when((rel % 2 == 1) & (rel > 1))
            def _():
                odds[rel // 2 - 1, own_rows, :] = piece.astype(BF)

    tiles(rows // size, step)
    h_own[...] = h_scr[:, tp].reshape(blocks * share, feat)


def last_kernel(n_tp, earlier, *refs):
    g2, b2, out = refs[-3:]
    even, got, h_own = refs[earlier : earlier + 3]
    _, share, width = out.shape[1:]
    step = h_own.shape[0] // share
    total = h_own[...].astype(F32) + (even[0] + got[...].astype(F32))
    for arrived in refs[earlier + 3 : -3]:
        total = total + arrived[...].astype(F32)
    done = layer_norm(total, g2[...], b2[...]).astype(BF)
    if earlier:
        out[: refs[0].shape[0]] = refs[0][...]
    for f in range(n_tp):
        piece = done[:, f * width : (f + 1) * width].reshape(step, share, width)
        out[out.shape[0] - step :, f] = piece


def unpack_kernel(owners, arrived, out):
    for g in range(out.shape[0]):
        out[g] = arrived[owners[g]]


VM = pl.BlockSpec(memory_space=pltpu.VMEM)
HBM = pl.BlockSpec(memory_space=pltpu.HBM)
SMEM = pl.BlockSpec(memory_space=pltpu.SMEM)


def near(*arrays):
    return [pltpu.with_memory_space_constraint(a, pltpu.VMEM) for a in arrays]


def far(*arrays):
    return [pltpu.with_memory_space_constraint(a, pltpu.HBM) for a in arrays]


def work(flops, rows):
    return pl.CostEstimate(flops=5 * flops, transcendentals=rows * 1024, bytes_accessed=rows * 8192)


def params(mib=20):
    return pltpu.CompilerParams(vmem_limit_bytes=mib * 1024 * 1024)


def body(
    tokens,
    prompt_lengths,
    adapter_ids,
    adapter_slot,
    w_qkv,
    w_out,
    w_fc1,
    w_fc2,
    qkv_down,
    qkv_up,
    out_down,
    out_up,
    fc1_down,
    fc1_up,
    fc2_down,
    fc2_up,
    norm1_gain,
    norm1_bias,
    norm2_gain,
    norm2_bias,
):
    n_req = lax.axis_size("req")
    n_tp = lax.axis_size("tp")
    feat = w_qkv.shape[1]
    width = tokens.shape[1]
    blocks = tokens.shape[0] // CAP
    share = CAP // n_tp
    half = n_tp // 2
    me = jnp.reshape(lax.axis_index("tp"), (1,)).astype(jnp.int32)

    def swap(value, r):
        return lax.ppermute(value, "tp", [(i, i ^ r) for i in range(n_tp)])

    def second_hop(pieces):
        return [hop for piece in pieces for hop in (piece, swap(piece, 1))]

    packed, owners = pl.pallas_call(
        pack_kernel,
        out_shape=(
            pltpu.VMEM((n_req, CAP + PAD, width), BF),
            jax.ShapeDtypeStruct((blocks,), jnp.int32),
        ),
        in_specs=[HBM] * 4,
        out_specs=(VM, SMEM),
        scratch_shapes=[
            pltpu.SMEM((SEQ_G, blocks), jnp.int32),
            pltpu.SMEM((SEQ_G, blocks), jnp.int32),
            pltpu.SMEM(adapter_slot.shape, jnp.int32),
            pltpu.VMEM((blocks, CAP, width), BF),
            pltpu.SemaphoreType.DMA((4,)),
        ],
        compiler_params=params(4),
        name="pack",
    )(
        *far(
            prompt_lengths.T,
            adapter_ids.T,
            adapter_slot,
            tokens.reshape(blocks, CAP, width),
        )
    )
    packed, me, w_first, o_first = lax.optimization_barrier(
        (packed, me, w_out, out_down.T)
    )
    arrived = lax.all_to_all(packed, "req", split_axis=0, concat_axis=0, tiled=True)
    w_far = [swap(w_first, 2 * y) for y in range(1, half)]
    w_near = swap(w_first, 1)
    odowns = [out_down.T] + [swap(o_first, r) for r in range(1, n_tp)]
    arrived, w_far, w_near, odowns = lax.optimization_barrier((arrived, w_far, w_near, odowns))
    count = 2
    step_blocks = n_req // count
    rows = step_blocks * CAP
    own = rows // n_tp
    beside = swap(arrived, 1)
    x_far = []
    for c in range(count):
        piece = arrived[c * step_blocks : (c + 1) * step_blocks]
        x_far.append([swap(piece, 2 * y) for y in range(1, half)])
    *begun, w_all, w1, w2, downs, up_all = pl.pallas_call(
        begin_kernel,
        out_shape=[
            pltpu.VMEM((3, count * rows, width), F32),
            pltpu.VMEM((count * rows, 3 * SPAN), F32),
            pltpu.VMEM((count * rows, 4 * SPAN), BF),
            pltpu.VMEM((count * rows, 2 * CAP), F32),
            pltpu.VMEM((3, feat, width), BF),
            pltpu.VMEM(w_fc1.shape, BF),
            pltpu.VMEM(w_fc2.shape, BF),
            pltpu.VMEM((3 * SPAN, feat), BF),
            pltpu.VMEM((6 * SPAN, 3 * width), BF),
        ],
        in_specs=[SMEM] + [VM] * 2 + [HBM] * 5,
        out_specs=[VM] * 9,
        scratch_shapes=[
            pltpu.VMEM((3, SPAN, width), BF),
            pltpu.SemaphoreType.DMA((9,)),
        ],
        compiler_params=params(8),
        cost_estimate=work(rows * feat * 3 * width, rows),
        name="begin",
    )(
        me,
        *near(arrived, beside),
        *far(
            w_qkv,
            w_fc1,
            w_fc2,
            jnp.swapaxes(qkv_down, 1, 2).reshape(3 * SPAN, feat),
            qkv_up,
        ),
    )
    w_all, w1, w2, downs, up_all = near(w_all, w1, w2, downs, up_all)
    x_far[0], begun = lax.optimization_barrier((x_far[0], begun))
    x_far[0] = second_hop(x_far[0])

    consts = near(
        out_up, fc1_down.T, fc1_up, fc2_down.T, fc2_up, norm1_gain[None], norm1_bias[None]
    )
    sel = begun[2]
    steps = []
    for c in range(count):
        if c:
            x_far[c], w_far, steps[0][0] = lax.optimization_barrier(
                (x_far[c], w_far, steps[0][0])
            )
            x_far[c] = second_hop(x_far[c])
        attended, x_full = pl.pallas_call(
            functools.partial(attn_kernel, n_tp, c),
            out_shape=[pltpu.VMEM((rows, width), BF), pltpu.VMEM((rows, feat), BF)],
            in_specs=[SMEM] + [VM] * (n_tp + 7),
            out_specs=[VM] * 2,
            compiler_params=params(12),
            cost_estimate=work(2 * rows * feat * 3 * width + 4 * rows * width * 2 * CAP, rows),
            name="attend",
        )(me, *near(arrived, beside, *x_far[c], *begun), w_all, downs, up_all)
        y_got = [swap(attended, 2 * y) for y in range(1, half)]
        if c:
            steps[0][1], attended = lax.optimization_barrier((steps[0][1], attended))
        steps.append([attended, y_got, x_full])
    wouts = [w_out, w_near] + second_hop(w_far)

    def finish(earlier, *values):
        blocks_done = step_blocks + sum(e.shape[0] for e in earlier)
        values = near(*earlier, *values, norm2_gain[None], norm2_bias[None])
        return pl.pallas_call(
            functools.partial(last_kernel, n_tp, len(earlier)),
            out_shape=pltpu.VMEM((blocks_done, n_tp, share, width), BF),
            in_specs=[VM] * len(values),
            out_specs=VM,
            compiler_params=params(8),
            name="finish",
        )(*values)

    for c in range(count):
        attended, y_got, x_full = steps[c]
        atts = second_hop([attended] + y_got)
        if c:
            atts, firsts = lax.optimization_barrier((atts, firsts))
            firsts = [swap(piece, 2 * (y + 1)) for y, piece in enumerate(firsts)]
        even, odd, odds, h_own = pl.pallas_call(
            functools.partial(ffn_kernel, n_tp, c),
            out_shape=[
                pltpu.VMEM((half, own, feat), F32),
                pltpu.VMEM((own, feat), BF),
                pltpu.VMEM((half - 1, own, feat), BF),
                pltpu.VMEM((own, feat), BF),
            ],
            in_specs=[SMEM] + [VM] * (3 * n_tp + 4 + len(consts)),
            out_specs=[VM] * 4,
            scratch_shapes=[pltpu.VMEM((step_blocks, n_tp, share, feat), BF)],
            compiler_params=params(16),
            cost_estimate=work(2 * rows * feat * (2 * w_fc1.shape[1] + feat), rows),
            name="feed",
        )(me, *near(*atts, *wouts, *odowns, x_full, sel), *consts, w1, w2)
        gots = swap(odds, 1)
        if c:
            earlier = finish([], *first_ends, *firsts)
            gots, earlier = lax.optimization_barrier((gots, earlier))
        sends = [(even[y] + gots[y - 1].astype(F32)).astype(BF) for y in range(1, half)]
        ends = [even, swap(odd, 1), h_own]
        if c == 0:
            firsts, first_ends = sends, ends
        else:
            sends = [swap(piece, 2 * (y + 1)) for y, piece in enumerate(sends)]
            done = finish([earlier], *ends, *sends)
    back = lax.all_to_all(
        done.reshape(n_req * n_tp, share, width),
        ("req", "tp"),
        split_axis=0,
        concat_axis=0,
        tiled=True,
    )
    result = pl.pallas_call(
        unpack_kernel,
        out_shape=jax.ShapeDtypeStruct((blocks, CAP, width), BF),
        in_specs=[SMEM, VM],
        out_specs=VM,
        compiler_params=params(4),
        name="unpack",
    )(owners, *near(back.reshape(n_req, CAP, width)))
    return result.reshape(blocks * CAP, width)


def solution(mesh):
    placed = (
        P("req", "tp"),
        P("req", None),
        P("req", None),
        P(),
        P(None, None, "tp"),
        P("tp", None),
        P(None, "tp"),
        P("tp", None),
        P(None, None, "req"),
        P(None, "req", "tp"),
        P("tp", "req"),
        P("req", None),
        P(None, "req"),
        P("req", "tp"),
        P("tp", "req"),
        P("req", None),
        P(),
        P(),
        P(),
        P(),
    )
    return jax.shard_map(
        body, mesh=mesh, in_specs=placed, out_specs=P("req", "tp"), check_vma=False
    )
```

```python
import functools

import jax
import jax.numpy as jnp
from jax import lax
from jax.experimental import pallas as pl
from jax.experimental.pallas import tpu as pltpu
from jax.sharding import PartitionSpec as P

HEAD_DIM = 64
RANK = 16
ADAPT_DEV = 2
CAP = 64
SEQ_G = 4
SPAN = ADAPT_DEV * RANK
PAD = 8
NORM_EPS = 1e-05
BF = jnp.bfloat16
F32 = jnp.float32


def dot(a, b):
    return lax.dot_general(a, b, (((1,), (0,)), ((), ())), preferred_element_type=F32)


def dot_t(a, b):
    return lax.dot_general(a, b, (((1,), (1,)), ((), ())), preferred_element_type=F32)


def layer_norm(values, gain, shift):
    mean = jnp.mean(values, axis=-1, keepdims=True)
    centred = values - mean
    variance = jnp.mean(centred * centred, axis=-1, keepdims=True)
    return centred * lax.rsqrt(variance + NORM_EPS) * gain + shift


def split_low(low, sel):
    low = low * sel
    high = low.astype(BF).astype(F32)
    return jnp.concatenate([high, low - high], axis=1).astype(BF)


def fetch(pairs, sems):
    copies = [
        pltpu.make_async_copy(src, dst, sems.at[i]) for i, (src, dst) in enumerate(pairs)
    ]
    for c in copies:
        c.start()
    return copies


def twice(ref):
    return jnp.concatenate([ref[...], ref[...]], axis=0)


def split_two(low, sel):
    low = low * sel
    high = low.astype(BF).astype(F32)
    lane = lax.broadcasted_iota(jnp.int32, low.shape, 1)
    return jnp.where(lane < low.shape[1] // 2, high, low - high).astype(BF)


def pack_kernel(
    lengths_in, ids_in, slots_in, tok_in, out, owners, lengths, ids, slots, tok, sems
):
    copies = fetch(
        [(lengths_in, lengths), (ids_in, ids), (slots_in, slots), (tok_in, tok)], sems
    )
    blocks = tok.shape[0]
    if out.shape[0] > blocks:
        out[...] = jnp.zeros(out.shape, out.dtype)
    width = out.shape[2]
    pos = lax.broadcasted_iota(jnp.int32, (PAD, width), 1) % CAP
    for c in copies:
        c.wait()
    for g in range(blocks):
        slot = [slots[ids[k, g]] for k in range(SEQ_G)]
        owner = slot[0] // ADAPT_DEV
        owners[g] = owner
        code = jnp.full((PAD, width), 1 + slot[0] % ADAPT_DEV, jnp.int32)
        end = jnp.int32(0)
        for k in range(1, SEQ_G):
            end = end + lengths[k - 1, g]
            code = jnp.where(pos >= end, 1 + k * ADAPT_DEV + slot[k] % ADAPT_DEV, code)
        out[owner, :CAP, :] = tok[g]
        out[owner, CAP:, :] = code.astype(F32).astype(BF)


def tiles(count, step):
    step(0)
    if count == 2:
        step(1)
    elif count > 2:
        lax.fori_loop(1, count, lambda t, c: (step(t), c)[1], 0)


def span(start, size):
    return pl.ds(start if isinstance(start, int) else pl.multiple_of(start, size), size)


def begin_kernel(
    me, own, beside, w_in, w1_in, w2_in, down_in, up_in, *refs
):
    acc, low, sel_out, bias_out, w, w1, w2, down, up_all, up, sems = refs
    pairs = [(up_in, up), (down_in, down)] + [(w_in.at[k], w.at[k]) for k in range(3)]
    for src, dst in ((w1_in, w1), (w2_in, w2)):
        half = src.shape[0] // 2
        pairs += [(src.at[:half], dst.at[:half]), (src.at[half:], dst.at[half:])]
    copies = fetch(pairs, sems)
    up_all[...] = jnp.zeros(up_all.shape, BF)
    copies[0].wait()
    for k in range(3):
        for part in range(2):
            first_row = (3 * part + k) * SPAN
            up_all[first_row : first_row + SPAN, k * up.shape[2] : (k + 1) * up.shape[2]] = up[k]
    for c in copies[1:5]:
        c.wait()
    blocks = own.shape[0]
    width = own.shape[2]
    tp = me[0]
    spans = [span(tp * width, width), span((tp ^ 1) * width, width)]
    pair_lane = lax.broadcasted_iota(jnp.int32, (2 * CAP, 2 * CAP), 1)
    pair_row = lax.broadcasted_iota(jnp.int32, (2 * CAP, 2 * CAP), 0)
    eye = pair_lane == pair_row
    lane_sel = ((pair_lane // RANK) % ADAPT_DEV).astype(F32)
    tile = min(4, blocks)

    def step(t):
        rs = span(t * (tile * CAP), tile * CAP)
        bs = pl.ds(t * tile, tile)
        xs = [part[bs, :CAP, :].reshape(tile * CAP, width) for part in (own, beside)]
        for k in range(3):
            acc[k, rs] = dot(xs[0], w[k, spans[0]]) + dot(xs[1], w[k, spans[1]])
        low[rs] = dot_t(xs[0], down[:, spans[0]]) + dot_t(xs[1], down[:, spans[1]])
        for p in range(tile // 2):
            b0 = t * tile + 2 * p
            c0 = own[b0, CAP : CAP + 1, : 2 * CAP].astype(F32)
            c1 = own[b0 + 1, CAP : CAP + 1, : 2 * CAP].astype(F32) + 64.0
            idr = jnp.where(pair_lane < CAP, c0, c1)
            idc = jnp.sum(jnp.where(eye, idr, 0.0), axis=1, keepdims=True)
            ps = span(t * (tile * CAP) + p * 2 * CAP, 2 * CAP)
            bias_out[ps] = jnp.where(idr == idc, 0.0, -1e30)
            pick = idc - 1.0
            pick = pick - 2.0 * jnp.floor(pick * 0.5)
            sel_out[ps] = (lane_sel == pick).astype(BF)

    tiles(blocks // tile, step)
    for c in copies[5:]:
        c.wait()


def attn_kernel(n_tp, chunk, me, *refs):
    parts = refs[:n_tp]
    acc, low_in, sel_in, bias, w, down, up_all, att, x_full = refs[n_tp:]
    blocks = att.shape[0] // CAP
    width = parts[0].shape[2]
    rows = blocks * CAP
    tp = me[0]
    spans = [span((tp ^ r) * width, width) for r in range(n_tp)]
    for r in range(n_tp):
        offset = chunk * blocks if part_of(parts[r], blocks) else 0
        x_full[:, spans[r]] = parts[r][offset : offset + blocks, :CAP, :].reshape(rows, width)
    first = lax.broadcasted_iota(jnp.int32, (2 * CAP, 2 * CAP), 1) < HEAD_DIM
    zero = jnp.zeros((), BF)
    tile = min(4, blocks)

    def step(t):
        start = t * (tile * CAP)
        rs = span(start, tile * CAP)
        whole = span(chunk * rows + start, tile * CAP)
        bs = pl.ds(t * tile, tile)
        xs = [parts[r][bs, :CAP, :].reshape(tile * CAP, width) for r in range(2, n_tp)]
        low = low_in[whole]
        for r in range(2, n_tp):
            low = low + dot_t(xs[r - 2], down[:, spans[r]])
        low = split_low(low, sel_in[whole].astype(F32)[:, : 3 * SPAN])
        qkv = []
        for k in range(3):
            total = acc[k, whole] + dot(low, up_all[:, k * width : (k + 1) * width])
            for r in range(2, n_tp):
                total = total + dot(xs[r - 2], w[k, spans[r]])
            qkv.append(total.astype(BF))
        q, k_, v = qkv
        q = (q.astype(F32) * HEAD_DIM**-0.5).astype(BF)
        for p in range(tile // 2):
            prs = slice(p * 2 * CAP, (p + 1) * 2 * CAP)
            out_rows = span(start + p * 2 * CAP, 2 * CAP)
            mask = bias[span(chunk * rows + start + p * 2 * CAP, 2 * CAP)]
            for h in range(width // (2 * HEAD_DIM)):
                cs = slice(h * 2 * HEAD_DIM, (h + 1) * 2 * HEAD_DIM)
                both = []
                for half in (first, ~first):
                    s = dot_t(jnp.where(half, q[prs, cs], zero), k_[prs, cs]) + mask
                    e = jnp.exp(s - jnp.max(s, axis=-1, keepdims=True))
                    inv = 1.0 / jnp.sum(e, axis=-1, keepdims=True)
                    both.append(dot((e * inv).astype(BF), v[prs, cs]))
                att[out_rows, cs] = jnp.where(first, *both).astype(BF)

    tiles(blocks // tile, step)


def part_of(array, blocks):
    return array.shape[0] > blocks


def ffn_kernel(n_tp, chunk, me, *refs):
    atts, wouts, odowns = refs[:n_tp], refs[n_tp : 2 * n_tp], refs[2 * n_tp : 3 * n_tp]
    x, sel_in, oup, d1, u1, d2, u2, g1, b1, w1, w2 = refs[3 * n_tp : 3 * n_tp + 11]
    even, odd, odds, h_own, h_scr = refs[3 * n_tp + 11 :]
    rows, feat = x.shape
    blocks = rows // CAP
    share = CAP // n_tp
    tp = me[0]
    size = min(rows, 256)
    nb = size // CAP
    ups = [jnp.concatenate([u[...], u[...]], axis=0) for u in (oup, u1, u2)]

    def step(t):
        rs = span(t * size, size)
        sel = sel_in[span(chunk * rows + t * size, size)].astype(F32)[:, : 2 * SPAN]
        low = None
        for r in range(n_tp):
            part = dot_t(atts[r][rs], twice(odowns[r]))
            low = part if low is None else low + part
        low = split_two(low, sel)
        total = x[rs].astype(F32)
        for r in range(n_tp):
            total = total + dot(atts[r][rs], wouts[r][...])
        total = total + dot(low, ups[0])
        h1 = layer_norm(total, g1[...], b1[...]).astype(BF)
        h_scr[span(t * nb, nb)] = h1.reshape(nb, n_tp, share, feat)
        low = split_two(dot_t(h1, twice(d1)), sel)
        pieces = []
        for n in range(4):
            ns = slice(n * w1.shape[1] // 4, (n + 1) * w1.shape[1] // 4)
            gate = dot(h1, w1[:, ns]) + dot(low, ups[1][:, ns])
            pieces.append((0.5 * gate * (1.0 + lax.erf(gate * 0.7071067811865476))).astype(BF))
        hidden = jnp.concatenate(pieces, axis=1)
        low = split_two(dot_t(hidden, twice(d2)), sel)
        term = dot(hidden, w2[...]) + dot(low, ups[2])
        term = term.reshape(nb, n_tp, share, feat)
        own_rows = span(t * (size // n_tp), size // n_tp)
        for j in range(n_tp):
            rel = tp ^ j
            piece = term[:, j].reshape(nb * share, feat)

            @pl.when(rel % 2 == 0)
            def _():
                even[rel // 2, own_rows, :] = piece

            @pl.when(rel == 1)
            def _():
                odd[own_rows, :] = piece.astype(BF)

            @pl.when((rel % 2 == 1) & (rel > 1))
            def _():
                odds[rel // 2 - 1, own_rows, :] = piece.astype(BF)

    tiles(rows // size, step)
    h_own[...] = h_scr[:, tp].reshape(blocks * share, feat)


def last_kernel(n_tp, earlier, *refs):
    g2, b2, out = refs[-3:]
    even, got, h_own = refs[earlier : earlier + 3]
    _, share, width = out.shape[1:]
    step = h_own.shape[0] // share
    total = h_own[...].astype(F32) + (even[0] + got[...].astype(F32))
    for arrived in refs[earlier + 3 : -3]:
        total = total + arrived[...].astype(F32)
    done = layer_norm(total, g2[...], b2[...]).astype(BF)
    if earlier:
        out[: refs[0].shape[0]] = refs[0][...]
    for f in range(n_tp):
        piece = done[:, f * width : (f + 1) * width].reshape(step, share, width)
        out[out.shape[0] - step :, f] = piece


def unpack_kernel(owners, arrived, out, sems):
    pairs = [(arrived.at[owners[g]], out.at[g]) for g in range(out.shape[0])]
    for c in fetch(pairs, sems):
        c.wait()


VM = pl.BlockSpec(memory_space=pltpu.VMEM)
HBM = pl.BlockSpec(memory_space=pltpu.HBM)
SMEM = pl.BlockSpec(memory_space=pltpu.SMEM)


def near(*arrays):
    return [pltpu.with_memory_space_constraint(a, pltpu.VMEM) for a in arrays]


def far(*arrays):
    return [pltpu.with_memory_space_constraint(a, pltpu.HBM) for a in arrays]


def work(flops, rows):
    return pl.CostEstimate(flops=5 * flops, transcendentals=rows * 1024, bytes_accessed=rows * 8192)


def params(mib=20):
    return pltpu.CompilerParams(vmem_limit_bytes=mib * 1024 * 1024)


def body(
    tokens,
    prompt_lengths,
    adapter_ids,
    adapter_slot,
    w_qkv,
    w_out,
    w_fc1,
    w_fc2,
    qkv_down,
    qkv_up,
    out_down,
    out_up,
    fc1_down,
    fc1_up,
    fc2_down,
    fc2_up,
    norm1_gain,
    norm1_bias,
    norm2_gain,
    norm2_bias,
):
    n_req = lax.axis_size("req")
    n_tp = lax.axis_size("tp")
    feat = w_qkv.shape[1]
    width = tokens.shape[1]
    blocks = tokens.shape[0] // CAP
    share = CAP // n_tp
    half = n_tp // 2
    me = jnp.reshape(lax.axis_index("tp"), (1,)).astype(jnp.int32)

    def swap(value, r):
        return lax.ppermute(value, "tp", [(i, i ^ r) for i in range(n_tp)])

    def second_hop(pieces):
        return [hop for piece in pieces for hop in (piece, swap(piece, 1))]

    packed, owners = pl.pallas_call(
        pack_kernel,
        out_shape=(
            pltpu.VMEM((n_req, CAP + PAD, width), BF),
            jax.ShapeDtypeStruct((blocks,), jnp.int32),
        ),
        in_specs=[HBM] * 4,
        out_specs=(VM, SMEM),
        scratch_shapes=[
            pltpu.SMEM((SEQ_G, blocks), jnp.int32),
            pltpu.SMEM((SEQ_G, blocks), jnp.int32),
            pltpu.SMEM(adapter_slot.shape, jnp.int32),
            pltpu.VMEM((blocks, CAP, width), BF),
            pltpu.SemaphoreType.DMA((4,)),
        ],
        compiler_params=params(4),
        name="pack",
    )(
        *far(
            prompt_lengths.T,
            adapter_ids.T,
            adapter_slot,
            tokens.reshape(blocks, CAP, width),
        )
    )
    packed, me, w_first, o_first = lax.optimization_barrier(
        (packed, me, w_out, out_down.T)
    )
    arrived = lax.all_to_all(packed, "req", split_axis=0, concat_axis=0, tiled=True)
    w_far = [swap(w_first, 2 * y) for y in range(1, half)]
    w_near = swap(w_first, 1)
    odowns = [out_down.T] + [swap(o_first, r) for r in range(1, n_tp)]
    arrived, w_far, w_near, odowns = lax.optimization_barrier((arrived, w_far, w_near, odowns))
    count = 2
    step_blocks = n_req // count
    rows = step_blocks * CAP
    own = rows // n_tp
    beside = swap(arrived, 1)
    x_far = []
    for c in range(count):
        piece = arrived[c * step_blocks : (c + 1) * step_blocks]
        x_far.append([swap(piece, 2 * y) for y in range(1, half)])
    *begun, w_all, w1, w2, downs, up_all = pl.pallas_call(
        begin_kernel,
        out_shape=[
            pltpu.VMEM((3, count * rows, width), F32),
            pltpu.VMEM((count * rows, 3 * SPAN), F32),
            pltpu.VMEM((count * rows, 4 * SPAN), BF),
            pltpu.VMEM((count * rows, 2 * CAP), F32),
            pltpu.VMEM((3, feat, width), BF),
            pltpu.VMEM(w_fc1.shape, BF),
            pltpu.VMEM(w_fc2.shape, BF),
            pltpu.VMEM((3 * SPAN, feat), BF),
            pltpu.VMEM((6 * SPAN, 3 * width), BF),
        ],
        in_specs=[SMEM] + [VM] * 2 + [HBM] * 5,
        out_specs=[VM] * 9,
        scratch_shapes=[
            pltpu.VMEM((3, SPAN, width), BF),
            pltpu.SemaphoreType.DMA((9,)),
        ],
        compiler_params=params(8),
        cost_estimate=work(rows * feat * 3 * width, rows),
        name="begin",
    )(
        me,
        *near(arrived, beside),
        *far(
            w_qkv,
            w_fc1,
            w_fc2,
            jnp.swapaxes(qkv_down, 1, 2).reshape(3 * SPAN, feat),
            qkv_up,
        ),
    )
    w_all, w1, w2, downs, up_all = near(w_all, w1, w2, downs, up_all)
    x_far[0], begun = lax.optimization_barrier((x_far[0], begun))
    x_far[0] = second_hop(x_far[0])
    x_far = lax.optimization_barrier(x_far)
    x_far[1:] = [second_hop(pieces) for pieces in x_far[1:]]

    consts = near(
        out_up, fc1_down.T, fc1_up, fc2_down.T, fc2_up, norm1_gain[None], norm1_bias[None]
    )
    sel = begun[2]
    steps = []
    for c in range(count):
        if c:
            w_far, steps[0][0] = lax.optimization_barrier((w_far, steps[0][0]))
        attended, x_full = pl.pallas_call(
            functools.partial(attn_kernel, n_tp, c),
            out_shape=[pltpu.VMEM((rows, width), BF), pltpu.VMEM((rows, feat), BF)],
            in_specs=[SMEM] + [VM] * (n_tp + 7),
            out_specs=[VM] * 2,
            compiler_params=params(12),
            cost_estimate=work(8 * rows * feat * 3 * width + 16 * rows * width * 2 * CAP, rows),
            name="attend",
        )(me, *near(arrived, beside, *x_far[c], *begun), w_all, downs, up_all)
        y_got = [swap(attended, 2 * y) for y in range(1, half)]
        if c:
            steps[0][1], attended = lax.optimization_barrier((steps[0][1], attended))
        steps.append([attended, y_got, x_full])
    wouts = [w_out, w_near] + second_hop(w_far)

    def finish(earlier, *values):
        blocks_done = step_blocks + sum(e.shape[0] for e in earlier)
        values = near(*earlier, *values, norm2_gain[None], norm2_bias[None])
        return pl.pallas_call(
            functools.partial(last_kernel, n_tp, len(earlier)),
            out_shape=pltpu.VMEM((blocks_done, n_tp, share, width), BF),
            in_specs=[VM] * len(values),
            out_specs=VM,
            compiler_params=params(8),
            name="finish",
        )(*values)

    for c in range(count):
        attended, y_got, x_full = steps[c]
        atts = second_hop([attended] + y_got)
        if c:
            atts, firsts = lax.optimization_barrier((atts, firsts))
            firsts = [swap(piece, 2 * (y + 1)) for y, piece in enumerate(firsts)]
        even, odd, odds, h_own = pl.pallas_call(
            functools.partial(ffn_kernel, n_tp, c),
            out_shape=[
                pltpu.VMEM((half, own, feat), F32),
                pltpu.VMEM((own, feat), BF),
                pltpu.VMEM((half - 1, own, feat), BF),
                pltpu.VMEM((own, feat), BF),
            ],
            in_specs=[SMEM] + [VM] * (3 * n_tp + 4 + len(consts)),
            out_specs=[VM] * 4,
            scratch_shapes=[pltpu.VMEM((step_blocks, n_tp, share, feat), BF)],
            compiler_params=params(16),
            cost_estimate=work(2 * rows * feat * (2 * w_fc1.shape[1] + feat), rows),
            name="feed",
        )(me, *near(*atts, *wouts, *odowns, x_full, sel), *consts, w1, w2)
        gots = swap(odds, 1)
        if c:
            earlier = finish([], *first_ends, *firsts)
            gots, earlier = lax.optimization_barrier((gots, earlier))
        sends = [(even[y] + gots[y - 1].astype(F32)).astype(BF) for y in range(1, half)]
        ends = [even, swap(odd, 1), h_own]
        if c == 0:
            firsts, first_ends = sends, ends
        else:
            sends = [swap(piece, 2 * (y + 1)) for y, piece in enumerate(sends)]
            done = finish([earlier], *ends, *sends)
    back = lax.all_to_all(
        done.reshape(n_req * n_tp, share, width),
        ("req", "tp"),
        split_axis=0,
        concat_axis=0,
        tiled=True,
    )
    result = pl.pallas_call(
        unpack_kernel,
        out_shape=jax.ShapeDtypeStruct((blocks, CAP, width), BF),
        in_specs=[SMEM, VM],
        out_specs=HBM,
        scratch_shapes=[pltpu.SemaphoreType.DMA((blocks,))],
        compiler_params=params(4),
        name="unpack",
    )(owners, *near(back.reshape(n_req, CAP, width)))
    return result.reshape(blocks * CAP, width)


def solution(mesh):
    placed = (
        P("req", "tp"),
        P("req", None),
        P("req", None),
        P(),
        P(None, None, "tp"),
        P("tp", None),
        P(None, "tp"),
        P("tp", None),
        P(None, None, "req"),
        P(None, "req", "tp"),
        P("tp", "req"),
        P("req", None),
        P(None, "req"),
        P("req", "tp"),
        P("tp", "req"),
        P("req", None),
        P(),
        P(),
        P(),
        P(),
    )
    return jax.shard_map(
        body, mesh=mesh, in_specs=placed, out_specs=P("req", "tp"), check_vma=False
    )
```

```python
import functools

import jax
import jax.numpy as jnp
from jax import lax
from jax.experimental import pallas as pl
from jax.experimental.pallas import tpu as pltpu
from jax.sharding import PartitionSpec as P

HEAD_DIM = 64
RANK = 16
ADAPT_DEV = 2
CAP = 64
SEQ_G = 4
SPAN = ADAPT_DEV * RANK
PAD = 8
NORM_EPS = 1e-05
BF = jnp.bfloat16
F32 = jnp.float32


def dot(a, b):
    return lax.dot_general(a, b, (((1,), (0,)), ((), ())), preferred_element_type=F32)


def dot_t(a, b):
    return lax.dot_general(a, b, (((1,), (1,)), ((), ())), preferred_element_type=F32)


def layer_norm(values, gain, shift):
    mean = jnp.mean(values, axis=-1, keepdims=True)
    centred = values - mean
    variance = jnp.mean(centred * centred, axis=-1, keepdims=True)
    return centred * lax.rsqrt(variance + NORM_EPS) * gain + shift


def split_low(low, sel):
    low = low * sel
    high = low.astype(BF).astype(F32)
    return jnp.concatenate([high, low - high], axis=1).astype(BF)


def fetch(pairs, sems):
    copies = [
        pltpu.make_async_copy(src, dst, sems.at[i]) for i, (src, dst) in enumerate(pairs)
    ]
    for c in copies:
        c.start()
    return copies


def twice(ref):
    return jnp.concatenate([ref[...], ref[...]], axis=0)


def split_two(low, sel):
    low = low * sel
    high = low.astype(BF).astype(F32)
    lane = lax.broadcasted_iota(jnp.int32, low.shape, 1)
    return jnp.where(lane < low.shape[1] // 2, high, low - high).astype(BF)


def pack_kernel(
    lengths_in, ids_in, slots_in, tok_in, out, owners, lengths, ids, slots, tok, sems
):
    copies = fetch(
        [(lengths_in, lengths), (ids_in, ids), (slots_in, slots), (tok_in, tok)], sems
    )
    blocks = tok.shape[0]
    if out.shape[0] > blocks:
        out[...] = jnp.zeros(out.shape, out.dtype)
    width = out.shape[2]
    pos = lax.broadcasted_iota(jnp.int32, (PAD, width), 1) % CAP
    for c in copies:
        c.wait()
    for g in range(blocks):
        slot = [slots[ids[k, g]] for k in range(SEQ_G)]
        owner = slot[0] // ADAPT_DEV
        owners[g] = owner
        code = jnp.full((PAD, width), 1 + slot[0] % ADAPT_DEV, jnp.int32)
        end = jnp.int32(0)
        for k in range(1, SEQ_G):
            end = end + lengths[k - 1, g]
            code = jnp.where(pos >= end, 1 + k * ADAPT_DEV + slot[k] % ADAPT_DEV, code)
        out[owner, :CAP, :] = tok[g]
        out[owner, CAP:, :] = code.astype(F32).astype(BF)


def tiles(count, step):
    step(0)
    if count == 2:
        step(1)
    elif count > 2:
        lax.fori_loop(1, count, lambda t, c: (step(t), c)[1], 0)


def span(start, size):
    return pl.ds(start if isinstance(start, int) else pl.multiple_of(start, size), size)


def begin_kernel(
    me, own, beside, w_in, w1_in, w2_in, down_in, up_in, *refs
):
    acc, low, sel_out, bias_out, w, w1, w2, down, up_all, up, sems = refs
    pairs = [(up_in, up), (down_in, down)] + [(w_in.at[k], w.at[k]) for k in range(3)]
    for src, dst in ((w1_in, w1), (w2_in, w2)):
        half = src.shape[0] // 2
        pairs += [(src.at[:half], dst.at[:half]), (src.at[half:], dst.at[half:])]
    copies = fetch(pairs, sems)
    up_all[...] = jnp.zeros(up_all.shape, BF)
    copies[0].wait()
    for k in range(3):
        for part in range(2):
            first_row = (3 * part + k) * SPAN
            up_all[first_row : first_row + SPAN, k * up.shape[2] : (k + 1) * up.shape[2]] = up[k]
    for c in copies[1:5]:
        c.wait()
    blocks = own.shape[0]
    width = own.shape[2]
    tp = me[0]
    spans = [span(tp * width, width), span((tp ^ 1) * width, width)]
    pair_lane = lax.broadcasted_iota(jnp.int32, (2 * CAP, 2 * CAP), 1)
    pair_row = lax.broadcasted_iota(jnp.int32, (2 * CAP, 2 * CAP), 0)
    eye = pair_lane == pair_row
    lane_sel = ((pair_lane // RANK) % ADAPT_DEV).astype(F32)
    tile = min(4, blocks)

    def step(t):
        rs = span(t * (tile * CAP), tile * CAP)
        bs = pl.ds(t * tile, tile)
        xs = [part[bs, :CAP, :].reshape(tile * CAP, width) for part in (own, beside)]
        for k in range(3):
            acc[k, rs] = dot(xs[0], w[k, spans[0]]) + dot(xs[1], w[k, spans[1]])
        low[rs] = dot_t(xs[0], down[:, spans[0]]) + dot_t(xs[1], down[:, spans[1]])
        for p in range(tile // 2):
            b0 = t * tile + 2 * p
            c0 = own[b0, CAP : CAP + 1, : 2 * CAP].astype(F32)
            c1 = own[b0 + 1, CAP : CAP + 1, : 2 * CAP].astype(F32) + 64.0
            idr = jnp.where(pair_lane < CAP, c0, c1)
            idc = jnp.sum(jnp.where(eye, idr, 0.0), axis=1, keepdims=True)
            ps = span(t * (tile * CAP) + p * 2 * CAP, 2 * CAP)
            bias_out[ps] = jnp.where(idr == idc, 0.0, -1e30)
            pick = idc - 1.0
            pick = pick - 2.0 * jnp.floor(pick * 0.5)
            sel_out[ps] = (lane_sel == pick).astype(BF)

    tiles(blocks // tile, step)
    for c in copies[5:]:
        c.wait()


def attn_kernel(n_tp, chunk, me, *refs):
    parts = refs[:n_tp]
    acc, low_in, sel_in, bias, w, down, up_all, att, x_full = refs[n_tp:]
    blocks = att.shape[0] // CAP
    width = parts[0].shape[2]
    rows = blocks * CAP
    tp = me[0]
    spans = [span((tp ^ r) * width, width) for r in range(n_tp)]
    for r in range(n_tp):
        offset = chunk * blocks if part_of(parts[r], blocks) else 0
        x_full[:, spans[r]] = parts[r][offset : offset + blocks, :CAP, :].reshape(rows, width)
    first = lax.broadcasted_iota(jnp.int32, (2 * CAP, 2 * CAP), 1) < HEAD_DIM
    zero = jnp.zeros((), BF)
    tile = min(4, blocks)

    def step(t):
        start = t * (tile * CAP)
        rs = span(start, tile * CAP)
        whole = span(chunk * rows + start, tile * CAP)
        bs = pl.ds(t * tile, tile)
        xs = [parts[r][bs, :CAP, :].reshape(tile * CAP, width) for r in range(2, n_tp)]
        low = low_in[whole]
        for r in range(2, n_tp):
            low = low + dot_t(xs[r - 2], down[:, spans[r]])
        low = split_low(low, sel_in[whole].astype(F32)[:, : 3 * SPAN])
        qkv = []
        for k in range(3):
            total = acc[k, whole] + dot(low, up_all[:, k * width : (k + 1) * width])
            for r in range(2, n_tp):
                total = total + dot(xs[r - 2], w[k, spans[r]])
            qkv.append(total.astype(BF))
        q, k_, v = qkv
        q = (q.astype(F32) * HEAD_DIM**-0.5).astype(BF)
        for p in range(tile // 2):
            prs = slice(p * 2 * CAP, (p + 1) * 2 * CAP)
            out_rows = span(start + p * 2 * CAP, 2 * CAP)
            mask = bias[span(chunk * rows + start + p * 2 * CAP, 2 * CAP)]
            for h in range(width // (2 * HEAD_DIM)):
                cs = slice(h * 2 * HEAD_DIM, (h + 1) * 2 * HEAD_DIM)
                both = []
                for half in (first, ~first):
                    s = dot_t(jnp.where(half, q[prs, cs], zero), k_[prs, cs]) + mask
                    e = jnp.exp(s - jnp.max(s, axis=-1, keepdims=True))
                    inv = 1.0 / jnp.sum(e, axis=-1, keepdims=True)
                    both.append(dot((e * inv).astype(BF), v[prs, cs]))
                att[out_rows, cs] = jnp.where(first, *both).astype(BF)

    tiles(blocks // tile, step)


def part_of(array, blocks):
    return array.shape[0] > blocks


def ffn_kernel(n_tp, chunk, me, *refs):
    n_w = 2 * n_tp - 2
    atts, pieces, odowns = refs[:n_tp], refs[n_tp : n_tp + n_w], refs[n_tp + n_w : 2 * n_tp + n_w]
    x, sel_in, oup, d1, u1, d2, u2, g1, b1, w1, w2 = refs[2 * n_tp + n_w : 2 * n_tp + n_w + 11]
    even, odd, odds, h_own, h_scr = refs[2 * n_tp + n_w + 11 :]
    wouts = [pieces[0][...], pieces[1][...]]
    for r in range(2, n_w, 2):
        wouts.append(jnp.concatenate([pieces[r][...], pieces[r + 1][...]], axis=0))
    rows, feat = x.shape
    blocks = rows // CAP
    share = CAP // n_tp
    tp = me[0]
    size = min(rows, 256)
    nb = size // CAP
    ups = [jnp.concatenate([u[...], u[...]], axis=0) for u in (oup, u1, u2)]

    def step(t):
        rs = span(t * size, size)
        sel = sel_in[span(chunk * rows + t * size, size)].astype(F32)[:, : 2 * SPAN]
        low = None
        for r in range(n_tp):
            part = dot_t(atts[r][rs], twice(odowns[r]))
            low = part if low is None else low + part
        low = split_two(low, sel)
        total = x[rs].astype(F32)
        for r in range(n_tp):
            total = total + dot(atts[r][rs], wouts[r])
        total = total + dot(low, ups[0])
        h1 = layer_norm(total, g1[...], b1[...]).astype(BF)
        h_scr[span(t * nb, nb)] = h1.reshape(nb, n_tp, share, feat)
        low = split_two(dot_t(h1, twice(d1)), sel)
        pieces = []
        for n in range(4):
            ns = slice(n * w1.shape[1] // 4, (n + 1) * w1.shape[1] // 4)
            gate = dot(h1, w1[:, ns]) + dot(low, ups[1][:, ns])
            pieces.append((0.5 * gate * (1.0 + lax.erf(gate * 0.7071067811865476))).astype(BF))
        hidden = jnp.concatenate(pieces, axis=1)
        low = split_two(dot_t(hidden, twice(d2)), sel)
        term = dot(hidden, w2[...]) + dot(low, ups[2])
        term = term.reshape(nb, n_tp, share, feat)
        own_rows = span(t * (size // n_tp), size // n_tp)
        for j in range(n_tp):
            rel = tp ^ j
            piece = term[:, j].reshape(nb * share, feat)

            @pl.when(rel % 2 == 0)
            def _():
                even[rel // 2, own_rows, :] = piece

            @pl.when(rel == 1)
            def _():
                odd[own_rows, :] = piece.astype(BF)

            @pl.when((rel % 2 == 1) & (rel > 1))
            def _():
                odds[rel // 2 - 1, own_rows, :] = piece.astype(BF)

    tiles(rows // size, step)
    h_own[...] = h_scr[:, tp].reshape(blocks * share, feat)


def last_kernel(n_tp, earlier, *refs):
    g2, b2, out = refs[-3:]
    even, got, h_own = refs[earlier : earlier + 3]
    _, share, width = out.shape[1:]
    step = h_own.shape[0] // share
    total = h_own[...].astype(F32) + (even[0] + got[...].astype(F32))
    for arrived in refs[earlier + 3 : -3]:
        total = total + arrived[...].astype(F32)
    done = layer_norm(total, g2[...], b2[...]).astype(BF)
    if earlier:
        out[: refs[0].shape[0]] = refs[0][...]
    for f in range(n_tp):
        piece = done[:, f * width : (f + 1) * width].reshape(step, share, width)
        out[out.shape[0] - step :, f] = piece


def unpack_kernel(owners, arrived, out):
    for g in range(out.shape[0]):
        out[g] = arrived[owners[g]]


VM = pl.BlockSpec(memory_space=pltpu.VMEM)
HBM = pl.BlockSpec(memory_space=pltpu.HBM)
SMEM = pl.BlockSpec(memory_space=pltpu.SMEM)


def near(*arrays):
    return [pltpu.with_memory_space_constraint(a, pltpu.VMEM) for a in arrays]


def far(*arrays):
    return [pltpu.with_memory_space_constraint(a, pltpu.HBM) for a in arrays]


def work(flops, rows):
    return pl.CostEstimate(flops=5 * flops, transcendentals=rows * 1024, bytes_accessed=rows * 8192)


def params(mib=20):
    return pltpu.CompilerParams(vmem_limit_bytes=mib * 1024 * 1024)


def body(
    tokens,
    prompt_lengths,
    adapter_ids,
    adapter_slot,
    w_qkv,
    w_out,
    w_fc1,
    w_fc2,
    qkv_down,
    qkv_up,
    out_down,
    out_up,
    fc1_down,
    fc1_up,
    fc2_down,
    fc2_up,
    norm1_gain,
    norm1_bias,
    norm2_gain,
    norm2_bias,
):
    n_req = lax.axis_size("req")
    n_tp = lax.axis_size("tp")
    feat = w_qkv.shape[1]
    width = tokens.shape[1]
    blocks = tokens.shape[0] // CAP
    share = CAP // n_tp
    half = n_tp // 2
    me = jnp.reshape(lax.axis_index("tp"), (1,)).astype(jnp.int32)

    def swap(value, r):
        return lax.ppermute(value, "tp", [(i, i ^ r) for i in range(n_tp)])

    def second_hop(pieces):
        return [hop for piece in pieces for hop in (piece, swap(piece, 1))]

    packed, owners = pl.pallas_call(
        pack_kernel,
        out_shape=(
            pltpu.VMEM((n_req, CAP + PAD, width), BF),
            jax.ShapeDtypeStruct((blocks,), jnp.int32),
        ),
        in_specs=[HBM] * 4,
        out_specs=(VM, SMEM),
        scratch_shapes=[
            pltpu.SMEM((SEQ_G, blocks), jnp.int32),
            pltpu.SMEM((SEQ_G, blocks), jnp.int32),
            pltpu.SMEM(adapter_slot.shape, jnp.int32),
            pltpu.VMEM((blocks, CAP, width), BF),
            pltpu.SemaphoreType.DMA((4,)),
        ],
        compiler_params=params(4),
        name="pack",
    )(
        *far(
            prompt_lengths.T,
            adapter_ids.T,
            adapter_slot,
            tokens.reshape(blocks, CAP, width),
        )
    )
    packed, me, w_first, o_first = lax.optimization_barrier(
        (packed, me, w_out, out_down.T)
    )
    arrived = lax.all_to_all(packed, "req", split_axis=0, concat_axis=0, tiled=True)
    w_half = w_out.shape[0] // 2
    w_far = [
        [swap(w_first[:w_half], 2 * y), swap(w_first[w_half:], 2 * y)] for y in range(1, half)
    ]
    odowns = [out_down.T] + [swap(o_first, r) for r in range(1, n_tp)]
    arrived, w_far, odowns = lax.optimization_barrier((arrived, w_far, odowns))
    count = 2
    step_blocks = n_req // count
    rows = step_blocks * CAP
    own = rows // n_tp
    beside = swap(arrived, 1)
    x_far = []
    for c in range(count):
        piece = arrived[c * step_blocks : (c + 1) * step_blocks]
        x_far.append([swap(piece, 2 * y) for y in range(1, half)])
    *begun, w_all, w1, w2, downs, up_all = pl.pallas_call(
        begin_kernel,
        out_shape=[
            pltpu.VMEM((3, count * rows, width), F32),
            pltpu.VMEM((count * rows, 3 * SPAN), F32),
            pltpu.VMEM((count * rows, 4 * SPAN), BF),
            pltpu.VMEM((count * rows, 2 * CAP), F32),
            pltpu.VMEM((3, feat, width), BF),
            pltpu.VMEM(w_fc1.shape, BF),
            pltpu.VMEM(w_fc2.shape, BF),
            pltpu.VMEM((3 * SPAN, feat), BF),
            pltpu.VMEM((6 * SPAN, 3 * width), BF),
        ],
        in_specs=[SMEM] + [VM] * 2 + [HBM] * 5,
        out_specs=[VM] * 9,
        scratch_shapes=[
            pltpu.VMEM((3, SPAN, width), BF),
            pltpu.SemaphoreType.DMA((9,)),
        ],
        compiler_params=params(8),
        cost_estimate=work(rows * feat * 3 * width, rows),
        name="begin",
    )(
        me,
        *near(arrived, beside),
        *far(
            w_qkv,
            w_fc1,
            w_fc2,
            jnp.swapaxes(qkv_down, 1, 2).reshape(3 * SPAN, feat),
            qkv_up,
        ),
    )
    w_all, w1, w2, downs, up_all = near(w_all, w1, w2, downs, up_all)
    x_far[0], begun = lax.optimization_barrier((x_far[0], begun))
    x_far[0] = second_hop(x_far[0])
    x_far = lax.optimization_barrier(x_far)
    x_far[1:] = [second_hop(pieces) for pieces in x_far[1:]]

    consts = near(
        out_up, fc1_down.T, fc1_up, fc2_down.T, fc2_up, norm1_gain[None], norm1_bias[None]
    )
    sel = begun[2]
    steps = []
    for c in range(count):
        if c:
            w_far, w_first, steps[0][0] = lax.optimization_barrier(
                (w_far, w_first, steps[0][0])
            )
        attended, x_full = pl.pallas_call(
            functools.partial(attn_kernel, n_tp, c),
            out_shape=[pltpu.VMEM((rows, width), BF), pltpu.VMEM((rows, feat), BF)],
            in_specs=[SMEM] + [VM] * (n_tp + 7),
            out_specs=[VM] * 2,
            compiler_params=params(12),
            cost_estimate=work(8 * rows * feat * 3 * width + 16 * rows * width * 2 * CAP, rows),
            name="attend",
        )(me, *near(arrived, beside, *x_far[c], *begun), w_all, downs, up_all)
        y_got = [swap(attended, 2 * y) for y in range(1, half)]
        if c:
            steps[0][1], attended = lax.optimization_barrier((steps[0][1], attended))
        steps.append([attended, y_got, x_full])
    w_near = swap(w_first, 1)
    wouts = [w_out, w_near]
    for first_half, second_half in w_far:
        wouts += [first_half, second_half, swap(first_half, 1), swap(second_half, 1)]

    def finish(earlier, *values):
        blocks_done = step_blocks + sum(e.shape[0] for e in earlier)
        values = near(*earlier, *values, norm2_gain[None], norm2_bias[None])
        return pl.pallas_call(
            functools.partial(last_kernel, n_tp, len(earlier)),
            out_shape=pltpu.VMEM((blocks_done, n_tp, share, width), BF),
            in_specs=[VM] * len(values),
            out_specs=VM,
            compiler_params=params(8),
            name="finish",
        )(*values)

    for c in range(count):
        attended, y_got, x_full = steps[c]
        atts = second_hop([attended] + y_got)
        if c:
            atts, firsts = lax.optimization_barrier((atts, firsts))
            firsts = [swap(piece, 2 * (y + 1)) for y, piece in enumerate(firsts)]
        even, odd, odds, h_own = pl.pallas_call(
            functools.partial(ffn_kernel, n_tp, c),
            out_shape=[
                pltpu.VMEM((half, own, feat), F32),
                pltpu.VMEM((own, feat), BF),
                pltpu.VMEM((half - 1, own, feat), BF),
                pltpu.VMEM((own, feat), BF),
            ],
            in_specs=[SMEM] + [VM] * (2 * n_tp + len(wouts) + 4 + len(consts)),
            out_specs=[VM] * 4,
            scratch_shapes=[pltpu.VMEM((step_blocks, n_tp, share, feat), BF)],
            compiler_params=params(16),
            cost_estimate=work(2 * rows * feat * (2 * w_fc1.shape[1] + feat), rows),
            name="feed",
        )(me, *near(*atts, *wouts, *odowns, x_full, sel), *consts, w1, w2)
        gots = swap(odds, 1)
        if c:
            earlier = finish([], *first_ends, *firsts)
            gots, earlier = lax.optimization_barrier((gots, earlier))
        sends = [(even[y] + gots[y - 1].astype(F32)).astype(BF) for y in range(1, half)]
        ends = [even, swap(odd, 1), h_own]
        if c == 0:
            firsts, first_ends = sends, ends
        else:
            sends = [swap(piece, 2 * (y + 1)) for y, piece in enumerate(sends)]
            done = finish([earlier], *ends, *sends)
    back = lax.all_to_all(
        done.reshape(n_req * n_tp, share, width),
        ("req", "tp"),
        split_axis=0,
        concat_axis=0,
        tiled=True,
    )
    result = pl.pallas_call(
        unpack_kernel,
        out_shape=jax.ShapeDtypeStruct((blocks, CAP, width), BF),
        in_specs=[SMEM, VM],
        out_specs=VM,
        compiler_params=params(4),
        name="unpack",
    )(owners, *near(back.reshape(n_req, CAP, width)))
    return result.reshape(blocks * CAP, width)


def solution(mesh):
    placed = (
        P("req", "tp"),
        P("req", None),
        P("req", None),
        P(),
        P(None, None, "tp"),
        P("tp", None),
        P(None, "tp"),
        P("tp", None),
        P(None, None, "req"),
        P(None, "req", "tp"),
        P("tp", "req"),
        P("req", None),
        P(None, "req"),
        P("req", "tp"),
        P("tp", "req"),
        P("req", None),
        P(),
        P(),
        P(),
        P(),
    )
    return jax.shard_map(
        body, mesh=mesh, in_specs=placed, out_specs=P("req", "tp"), check_vma=False
    )
```

```python
import functools

import jax
import jax.numpy as jnp
from jax import lax
from jax.experimental import pallas as pl
from jax.experimental.pallas import tpu as pltpu
from jax.sharding import PartitionSpec as P

HEAD_DIM = 64
RANK = 16
ADAPT_DEV = 2
CAP = 64
SEQ_G = 4
SPAN = ADAPT_DEV * RANK
PAD = 8
NORM_EPS = 1e-05
BF = jnp.bfloat16
F32 = jnp.float32


def dot(a, b):
    return lax.dot_general(a, b, (((1,), (0,)), ((), ())), preferred_element_type=F32)


def dot_t(a, b):
    return lax.dot_general(a, b, (((1,), (1,)), ((), ())), preferred_element_type=F32)


def layer_norm(values, gain, shift):
    mean = jnp.mean(values, axis=-1, keepdims=True)
    centred = values - mean
    variance = jnp.mean(centred * centred, axis=-1, keepdims=True)
    return centred * lax.rsqrt(variance + NORM_EPS) * gain + shift


def split_low(low, sel):
    low = low * sel
    high = low.astype(BF).astype(F32)
    return jnp.concatenate([high, low - high], axis=1).astype(BF)


def fetch(pairs, sems):
    copies = [
        pltpu.make_async_copy(src, dst, sems.at[i]) for i, (src, dst) in enumerate(pairs)
    ]
    for c in copies:
        c.start()
    return copies


def twice(ref):
    return jnp.concatenate([ref[...], ref[...]], axis=0)


def split_two(low, sel):
    low = low * sel
    high = low.astype(BF).astype(F32)
    lane = lax.broadcasted_iota(jnp.int32, low.shape, 1)
    return jnp.where(lane < low.shape[1] // 2, high, low - high).astype(BF)


def pack_kernel(
    lengths_in, ids_in, slots_in, tok_in, out, owners, lengths, ids, slots, tok, sems
):
    copies = fetch(
        [(lengths_in, lengths), (ids_in, ids), (slots_in, slots), (tok_in, tok)], sems
    )
    blocks = tok.shape[0]
    if out.shape[0] > blocks:
        out[...] = jnp.zeros(out.shape, out.dtype)
    width = out.shape[2]
    pos = lax.broadcasted_iota(jnp.int32, (PAD, width), 1) % CAP
    for c in copies:
        c.wait()
    for g in range(blocks):
        slot = [slots[ids[k, g]] for k in range(SEQ_G)]
        owner = slot[0] // ADAPT_DEV
        owners[g] = owner
        code = jnp.full((PAD, width), 1 + slot[0] % ADAPT_DEV, jnp.int32)
        end = jnp.int32(0)
        for k in range(1, SEQ_G):
            end = end + lengths[k - 1, g]
            code = jnp.where(pos >= end, 1 + k * ADAPT_DEV + slot[k] % ADAPT_DEV, code)
        out[owner, :CAP, :] = tok[g]
        out[owner, CAP:, :] = code.astype(F32).astype(BF)


def tiles(count, step):
    step(0)
    if count == 2:
        step(1)
    elif count > 2:
        lax.fori_loop(1, count, lambda t, c: (step(t), c)[1], 0)


def span(start, size):
    return pl.ds(start if isinstance(start, int) else pl.multiple_of(start, size), size)


def begin_kernel(
    me, own, beside, w_in, w1_in, w2_in, down_in, up_in, *refs
):
    acc, low, sel_out, bias_out, w, w1, w2, down, up_all, up, sems = refs
    pairs = [(up_in, up), (down_in, down)] + [(w_in.at[k], w.at[k]) for k in range(3)]
    for src, dst in ((w1_in, w1), (w2_in, w2)):
        half = src.shape[0] // 2
        pairs += [(src.at[:half], dst.at[:half]), (src.at[half:], dst.at[half:])]
    copies = fetch(pairs, sems)
    up_all[...] = jnp.zeros(up_all.shape, BF)
    copies[0].wait()
    for k in range(3):
        for part in range(2):
            first_row = (3 * part + k) * SPAN
            up_all[first_row : first_row + SPAN, k * up.shape[2] : (k + 1) * up.shape[2]] = up[k]
    for c in copies[1:5]:
        c.wait()
    blocks = own.shape[0]
    width = own.shape[2]
    tp = me[0]
    spans = [span(tp * width, width), span((tp ^ 1) * width, width)]
    pair_lane = lax.broadcasted_iota(jnp.int32, (2 * CAP, 2 * CAP), 1)
    pair_row = lax.broadcasted_iota(jnp.int32, (2 * CAP, 2 * CAP), 0)
    eye = pair_lane == pair_row
    lane_sel = ((pair_lane // RANK) % ADAPT_DEV).astype(F32)
    tile = min(4, blocks)

    def step(t):
        rs = span(t * (tile * CAP), tile * CAP)
        bs = pl.ds(t * tile, tile)
        xs = [part[bs, :CAP, :].reshape(tile * CAP, width) for part in (own, beside)]
        for k in range(3):
            acc[k, rs] = dot(xs[0], w[k, spans[0]]) + dot(xs[1], w[k, spans[1]])
        low[rs] = dot_t(xs[0], down[:, spans[0]]) + dot_t(xs[1], down[:, spans[1]])
        for p in range(tile // 2):
            b0 = t * tile + 2 * p
            c0 = own[b0, CAP : CAP + 1, : 2 * CAP].astype(F32)
            c1 = own[b0 + 1, CAP : CAP + 1, : 2 * CAP].astype(F32) + 64.0
            idr = jnp.where(pair_lane < CAP, c0, c1)
            idc = jnp.sum(jnp.where(eye, idr, 0.0), axis=1, keepdims=True)
            ps = span(t * (tile * CAP) + p * 2 * CAP, 2 * CAP)
            bias_out[ps] = jnp.where(idr == idc, 0.0, -1e30)
            pick = idc - 1.0
            pick = pick - 2.0 * jnp.floor(pick * 0.5)
            sel_out[ps] = (lane_sel == pick).astype(BF)

    tiles(blocks // tile, step)
    for c in copies[5:]:
        c.wait()


def attn_kernel(n_tp, chunk, me, *refs):
    parts = refs[:n_tp]
    acc, low_in, sel_in, bias, w, down, up_all, att, x_full = refs[n_tp:]
    blocks = att.shape[0] // CAP
    width = parts[0].shape[2]
    rows = blocks * CAP
    tp = me[0]
    spans = [span((tp ^ r) * width, width) for r in range(n_tp)]
    for r in range(n_tp):
        offset = chunk * blocks if part_of(parts[r], blocks) else 0
        x_full[:, spans[r]] = parts[r][offset : offset + blocks, :CAP, :].reshape(rows, width)
    first = lax.broadcasted_iota(jnp.int32, (2 * CAP, 2 * CAP), 1) < HEAD_DIM
    zero = jnp.zeros((), BF)
    tile = min(4, blocks)

    def step(t):
        start = t * (tile * CAP)
        rs = span(start, tile * CAP)
        whole = span(chunk * rows + start, tile * CAP)
        bs = pl.ds(t * tile, tile)
        xs = [parts[r][bs, :CAP, :].reshape(tile * CAP, width) for r in range(2, n_tp)]
        low = low_in[whole]
        for r in range(2, n_tp):
            low = low + dot_t(xs[r - 2], down[:, spans[r]])
        low = split_low(low, sel_in[whole].astype(F32)[:, : 3 * SPAN])
        qkv = []
        for k in range(3):
            total = acc[k, whole] + dot(low, up_all[:, k * width : (k + 1) * width])
            for r in range(2, n_tp):
                total = total + dot(xs[r - 2], w[k, spans[r]])
            qkv.append(total.astype(BF))
        q, k_, v = qkv
        q = (q.astype(F32) * HEAD_DIM**-0.5).astype(BF)
        for p in range(tile // 2):
            prs = slice(p * 2 * CAP, (p + 1) * 2 * CAP)
            out_rows = span(start + p * 2 * CAP, 2 * CAP)
            mask = bias[span(chunk * rows + start + p * 2 * CAP, 2 * CAP)]
            for h in range(width // (2 * HEAD_DIM)):
                cs = slice(h * 2 * HEAD_DIM, (h + 1) * 2 * HEAD_DIM)
                both = []
                for half in (first, ~first):
                    s = dot_t(jnp.where(half, q[prs, cs], zero), k_[prs, cs]) + mask
                    e = jnp.exp(s - jnp.max(s, axis=-1, keepdims=True))
                    inv = 1.0 / jnp.sum(e, axis=-1, keepdims=True)
                    both.append(dot((e * inv).astype(BF), v[prs, cs]))
                att[out_rows, cs] = jnp.where(first, *both).astype(BF)

    tiles(blocks // tile, step)


def part_of(array, blocks):
    return array.shape[0] > blocks


def ffn_kernel(n_tp, chunk, me, *refs):
    n_w = 2 * n_tp - 2
    atts, pieces, odowns = refs[:n_tp], refs[n_tp : n_tp + n_w], refs[n_tp + n_w : 2 * n_tp + n_w]
    x, sel_in, oup, d1, u1, d2, u2, g1, b1, w1, w2 = refs[2 * n_tp + n_w : 2 * n_tp + n_w + 11]
    even, odd, odds, h_own, h_scr = refs[2 * n_tp + n_w + 11 :]
    wouts = [pieces[0][...], pieces[1][...]]
    for r in range(2, n_w, 2):
        wouts.append(jnp.concatenate([pieces[r][...], pieces[r + 1][...]], axis=0))
    rows, feat = x.shape
    blocks = rows // CAP
    share = CAP // n_tp
    tp = me[0]
    size = min(rows, 256)
    nb = size // CAP
    ups = [jnp.concatenate([u[...], u[...]], axis=0) for u in (oup, u1, u2)]

    def step(t):
        rs = span(t * size, size)
        sel = sel_in[span(chunk * rows + t * size, size)].astype(F32)[:, : 2 * SPAN]
        low = None
        for r in range(n_tp):
            part = dot_t(atts[r][rs], twice(odowns[r]))
            low = part if low is None else low + part
        low = split_two(low, sel)
        total = x[rs].astype(F32)
        for r in range(n_tp):
            total = total + dot(atts[r][rs], wouts[r])
        total = total + dot(low, ups[0])
        h1 = layer_norm(total, g1[...], b1[...]).astype(BF)
        h_scr[span(t * nb, nb)] = h1.reshape(nb, n_tp, share, feat)
        low = split_two(dot_t(h1, twice(d1)), sel)
        pieces = []
        for n in range(4):
            ns = slice(n * w1.shape[1] // 4, (n + 1) * w1.shape[1] // 4)
            gate = dot(h1, w1[:, ns]) + dot(low, ups[1][:, ns])
            pieces.append((0.5 * gate * (1.0 + lax.erf(gate * 0.7071067811865476))).astype(BF))
        hidden = jnp.concatenate(pieces, axis=1)
        low = split_two(dot_t(hidden, twice(d2)), sel)
        term = dot(hidden, w2[...]) + dot(low, ups[2])
        term = term.reshape(nb, n_tp, share, feat)
        own_rows = span(t * (size // n_tp), size // n_tp)
        for j in range(n_tp):
            rel = tp ^ j
            piece = term[:, j].reshape(nb * share, feat)

            @pl.when(rel % 2 == 0)
            def _():
                even[rel // 2, own_rows, :] = piece

            @pl.when(rel == 1)
            def _():
                odd[own_rows, :] = piece.astype(BF)

            @pl.when((rel % 2 == 1) & (rel > 1))
            def _():
                odds[rel // 2 - 1, own_rows, :] = piece.astype(BF)

    tiles(rows // size, step)
    h_own[...] = h_scr[:, tp].reshape(blocks * share, feat)


def last_kernel(n_tp, earlier, *refs):
    g2, b2, out = refs[-3:]
    even, got, h_own = refs[earlier : earlier + 3]
    _, share, width = out.shape[1:]
    step = h_own.shape[0] // share
    total = h_own[...].astype(F32) + (even[0] + got[...].astype(F32))
    for arrived in refs[earlier + 3 : -3]:
        total = total + arrived[...].astype(F32)
    done = layer_norm(total, g2[...], b2[...]).astype(BF)
    if earlier:
        out[: refs[0].shape[0]] = refs[0][...]
    for f in range(n_tp):
        piece = done[:, f * width : (f + 1) * width].reshape(step, share, width)
        out[out.shape[0] - step :, f] = piece


def unpack_kernel(owners, arrived, out):
    for g in range(out.shape[0]):
        out[g] = arrived[owners[g]]


VM = pl.BlockSpec(memory_space=pltpu.VMEM)
HBM = pl.BlockSpec(memory_space=pltpu.HBM)
SMEM = pl.BlockSpec(memory_space=pltpu.SMEM)


def near(*arrays):
    return [pltpu.with_memory_space_constraint(a, pltpu.VMEM) for a in arrays]


def far(*arrays):
    return [pltpu.with_memory_space_constraint(a, pltpu.HBM) for a in arrays]


def work(flops, rows):
    return pl.CostEstimate(flops=5 * flops, transcendentals=rows * 1024, bytes_accessed=rows * 8192)


def params(mib=20):
    return pltpu.CompilerParams(vmem_limit_bytes=mib * 1024 * 1024)


def body(
    tokens,
    prompt_lengths,
    adapter_ids,
    adapter_slot,
    w_qkv,
    w_out,
    w_fc1,
    w_fc2,
    qkv_down,
    qkv_up,
    out_down,
    out_up,
    fc1_down,
    fc1_up,
    fc2_down,
    fc2_up,
    norm1_gain,
    norm1_bias,
    norm2_gain,
    norm2_bias,
):
    n_req = lax.axis_size("req")
    n_tp = lax.axis_size("tp")
    feat = w_qkv.shape[1]
    width = tokens.shape[1]
    blocks = tokens.shape[0] // CAP
    share = CAP // n_tp
    half = n_tp // 2
    me = jnp.reshape(lax.axis_index("tp"), (1,)).astype(jnp.int32)

    def swap(value, r):
        return lax.ppermute(value, "tp", [(i, i ^ r) for i in range(n_tp)])

    def second_hop(pieces):
        return [hop for piece in pieces for hop in (piece, swap(piece, 1))]

    packed, owners = pl.pallas_call(
        pack_kernel,
        out_shape=(
            pltpu.VMEM((n_req, CAP + PAD, width), BF),
            jax.ShapeDtypeStruct((blocks,), jnp.int32),
        ),
        in_specs=[HBM] * 4,
        out_specs=(VM, SMEM),
        scratch_shapes=[
            pltpu.SMEM((SEQ_G, blocks), jnp.int32),
            pltpu.SMEM((SEQ_G, blocks), jnp.int32),
            pltpu.SMEM(adapter_slot.shape, jnp.int32),
            pltpu.VMEM((blocks, CAP, width), BF),
            pltpu.SemaphoreType.DMA((4,)),
        ],
        compiler_params=params(4),
        name="pack",
    )(
        *far(
            prompt_lengths.T,
            adapter_ids.T,
            adapter_slot,
            tokens.reshape(blocks, CAP, width),
        )
    )
    packed, me, w_first, o_first = lax.optimization_barrier(
        (packed, me, w_out, out_down.T)
    )
    arrived = lax.all_to_all(packed, "req", split_axis=0, concat_axis=0, tiled=True)
    w_half = w_out.shape[0] * 3 // 8
    w_far = [
        [swap(w_first[:w_half], 2 * y), swap(w_first[w_half:], 2 * y)] for y in range(1, half)
    ]
    odowns = [out_down.T] + [swap(o_first, r) for r in range(1, n_tp)]
    w_small, w_large = [pair[0] for pair in w_far], [pair[1] for pair in w_far]
    arrived, w_small = lax.optimization_barrier((arrived, w_small))
    count = 2
    step_blocks = n_req // count
    rows = step_blocks * CAP
    own = rows // n_tp
    beside, w_large = lax.optimization_barrier((swap(arrived, 1), w_large))
    w_far = list(zip(w_small, w_large))
    x_far = []
    for c in range(count):
        piece = arrived[c * step_blocks : (c + 1) * step_blocks]
        x_far.append([swap(piece, 2 * y) for y in range(1, half)])
    *begun, w_all, w1, w2, downs, up_all = pl.pallas_call(
        begin_kernel,
        out_shape=[
            pltpu.VMEM((3, count * rows, width), F32),
            pltpu.VMEM((count * rows, 3 * SPAN), F32),
            pltpu.VMEM((count * rows, 4 * SPAN), BF),
            pltpu.VMEM((count * rows, 2 * CAP), F32),
            pltpu.VMEM((3, feat, width), BF),
            pltpu.VMEM(w_fc1.shape, BF),
            pltpu.VMEM(w_fc2.shape, BF),
            pltpu.VMEM((3 * SPAN, feat), BF),
            pltpu.VMEM((6 * SPAN, 3 * width), BF),
        ],
        in_specs=[SMEM] + [VM] * 2 + [HBM] * 5,
        out_specs=[VM] * 9,
        scratch_shapes=[
            pltpu.VMEM((3, SPAN, width), BF),
            pltpu.SemaphoreType.DMA((9,)),
        ],
        compiler_params=params(8),
        cost_estimate=work(rows * feat * 3 * width, rows),
        name="begin",
    )(
        me,
        *near(arrived, beside),
        *far(
            w_qkv,
            w_fc1,
            w_fc2,
            jnp.swapaxes(qkv_down, 1, 2).reshape(3 * SPAN, feat),
            qkv_up,
        ),
    )
    w_all, w1, w2, downs, up_all = near(w_all, w1, w2, downs, up_all)
    x_far[0], begun = lax.optimization_barrier((x_far[0], begun))
    x_far[0] = second_hop(x_far[0])
    x_far, odowns = lax.optimization_barrier((x_far, odowns))
    x_far[1:] = [second_hop(pieces) for pieces in x_far[1:]]

    consts = near(
        out_up, fc1_down.T, fc1_up, fc2_down.T, fc2_up, norm1_gain[None], norm1_bias[None]
    )
    sel = begun[2]
    steps = []
    for c in range(count):
        if c:
            w_far, w_first, steps[0][0] = lax.optimization_barrier(
                (w_far, w_first, steps[0][0])
            )
        attended, x_full = pl.pallas_call(
            functools.partial(attn_kernel, n_tp, c),
            out_shape=[pltpu.VMEM((rows, width), BF), pltpu.VMEM((rows, feat), BF)],
            in_specs=[SMEM] + [VM] * (n_tp + 7),
            out_specs=[VM] * 2,
            compiler_params=params(12),
            cost_estimate=work(8 * rows * feat * 3 * width + 16 * rows * width * 2 * CAP, rows),
            name="attend",
        )(me, *near(arrived, beside, *x_far[c], *begun), w_all, downs, up_all)
        y_got = [swap(attended, 2 * y) for y in range(1, half)]
        if c:
            steps[0][1], attended = lax.optimization_barrier((steps[0][1], attended))
        steps.append([attended, y_got, x_full])
    w_near = swap(w_first, 1)
    wouts = [w_out, w_near]
    for first_half, second_half in w_far:
        wouts += [first_half, second_half, swap(first_half, 1), swap(second_half, 1)]

    def finish(earlier, *values):
        blocks_done = step_blocks + sum(e.shape[0] for e in earlier)
        values = near(*earlier, *values, norm2_gain[None], norm2_bias[None])
        return pl.pallas_call(
            functools.partial(last_kernel, n_tp, len(earlier)),
            out_shape=pltpu.VMEM((blocks_done, n_tp, share, width), BF),
            in_specs=[VM] * len(values),
            out_specs=VM,
            compiler_params=params(8),
            name="finish",
        )(*values)

    for c in range(count):
        attended, y_got, x_full = steps[c]
        atts = second_hop([attended] + y_got)
        if c:
            atts, firsts = lax.optimization_barrier((atts, firsts))
            firsts = [swap(piece, 2 * (y + 1)) for y, piece in enumerate(firsts)]
        even, odd, odds, h_own = pl.pallas_call(
            functools.partial(ffn_kernel, n_tp, c),
            out_shape=[
                pltpu.VMEM((half, own, feat), F32),
                pltpu.VMEM((own, feat), BF),
                pltpu.VMEM((half - 1, own, feat), BF),
                pltpu.VMEM((own, feat), BF),
            ],
            in_specs=[SMEM] + [VM] * (2 * n_tp + len(wouts) + 4 + len(consts)),
            out_specs=[VM] * 4,
            scratch_shapes=[pltpu.VMEM((step_blocks, n_tp, share, feat), BF)],
            compiler_params=params(16),
            cost_estimate=work(2 * rows * feat * (2 * w_fc1.shape[1] + feat), rows),
            name="feed",
        )(me, *near(*atts, *wouts, *odowns, x_full, sel), *consts, w1, w2)
        gots = swap(odds, 1)
        if c:
            earlier = finish([], *first_ends, *firsts)
            gots, earlier = lax.optimization_barrier((gots, earlier))
        sends = [(even[y] + gots[y - 1].astype(F32)).astype(BF) for y in range(1, half)]
        ends = [even, swap(odd, 1), h_own]
        if c == 0:
            firsts, first_ends = sends, ends
        else:
            sends = [swap(piece, 2 * (y + 1)) for y, piece in enumerate(sends)]
            done = finish([earlier], *ends, *sends)
    back = lax.all_to_all(
        done.reshape(n_req * n_tp, share, width),
        ("req", "tp"),
        split_axis=0,
        concat_axis=0,
        tiled=True,
    )
    result = pl.pallas_call(
        unpack_kernel,
        out_shape=jax.ShapeDtypeStruct((blocks, CAP, width), BF),
        in_specs=[SMEM, VM],
        out_specs=VM,
        compiler_params=params(4),
        name="unpack",
    )(owners, *near(back.reshape(n_req, CAP, width)))
    return result.reshape(blocks * CAP, width)


def solution(mesh):
    placed = (
        P("req", "tp"),
        P("req", None),
        P("req", None),
        P(),
        P(None, None, "tp"),
        P("tp", None),
        P(None, "tp"),
        P("tp", None),
        P(None, None, "req"),
        P(None, "req", "tp"),
        P("tp", "req"),
        P("req", None),
        P(None, "req"),
        P("req", "tp"),
        P("tp", "req"),
        P("req", None),
        P(),
        P(),
        P(),
        P(),
    )
    return jax.shard_map(
        body, mesh=mesh, in_specs=placed, out_specs=P("req", "tp"), check_vma=False
    )
```

```python
import functools

import jax
import jax.numpy as jnp
from jax import lax
from jax.experimental import pallas as pl
from jax.experimental.pallas import tpu as pltpu
from jax.sharding import PartitionSpec as P

HEAD_DIM = 64
RANK = 16
ADAPT_DEV = 2
CAP = 64
SEQ_G = 4
SPAN = ADAPT_DEV * RANK
PAD = 8
NORM_EPS = 1e-05
BF = jnp.bfloat16
F32 = jnp.float32


def dot(a, b):
    return lax.dot_general(a, b, (((1,), (0,)), ((), ())), preferred_element_type=F32)


def dot_t(a, b):
    return lax.dot_general(a, b, (((1,), (1,)), ((), ())), preferred_element_type=F32)


def layer_norm(values, gain, shift):
    mean = jnp.mean(values, axis=-1, keepdims=True)
    centred = values - mean
    variance = jnp.mean(centred * centred, axis=-1, keepdims=True)
    return centred * lax.rsqrt(variance + NORM_EPS) * gain + shift


def fetch(pairs, sems):
    copies = [
        pltpu.make_async_copy(src, dst, sems.at[i]) for i, (src, dst) in enumerate(pairs)
    ]
    for c in copies:
        c.start()
    return copies


def twice(ref):
    return jnp.concatenate([ref[...], ref[...]], axis=0)


def split_two(low, sel):
    low = low * sel
    high = low.astype(BF).astype(F32)
    lane = lax.broadcasted_iota(jnp.int32, low.shape, 1)
    return jnp.where(lane < low.shape[1] // 2, high, low - high).astype(BF)


def pack_kernel(
    lengths_in, ids_in, slots_in, tok_in, out, owners, lengths, ids, slots, tok, sems
):
    copies = fetch(
        [(lengths_in, lengths), (ids_in, ids), (slots_in, slots), (tok_in, tok)], sems
    )
    blocks = tok.shape[0]
    if out.shape[0] > blocks:
        out[...] = jnp.zeros(out.shape, out.dtype)
    width = out.shape[2]
    pos = lax.broadcasted_iota(jnp.int32, (PAD, width), 1) % CAP
    for c in copies:
        c.wait()
    for g in range(blocks):
        slot = [slots[ids[k, g]] for k in range(SEQ_G)]
        owner = slot[0] // ADAPT_DEV
        owners[g] = owner
        code = jnp.full((PAD, width), 1 + slot[0] % ADAPT_DEV, jnp.int32)
        end = jnp.int32(0)
        for k in range(1, SEQ_G):
            end = end + lengths[k - 1, g]
            code = jnp.where(pos >= end, 1 + k * ADAPT_DEV + slot[k] % ADAPT_DEV, code)
        out[owner, :CAP, :] = tok[g]
        out[owner, CAP:, :] = code.astype(F32).astype(BF)


def tiles(count, step):
    step(0)
    if count == 2:
        step(1)
    elif count > 2:
        lax.fori_loop(1, count, lambda t, c: (step(t), c)[1], 0)


def span(start, size):
    return pl.ds(start if isinstance(start, int) else pl.multiple_of(start, size), size)


def begin_kernel(
    me, own, beside, w_in, w1_in, w2_in, down_in, up_in, *refs
):
    acc, low, sel_out, bias_out, w, w1, w2, down, up_all, up, sems = refs
    low_rows = down_in.shape[0]
    pairs = [(up_in, up), (down_in, down.at[:low_rows]), (down_in, down.at[low_rows:])] + [(w_in.at[k], w.at[k]) for k in range(3)]
    for src, dst in ((w1_in, w1), (w2_in, w2)):
        half = src.shape[0] // 2
        pairs += [(src.at[:half], dst.at[:half]), (src.at[half:], dst.at[half:])]
    copies = fetch(pairs, sems)
    up_all[...] = jnp.zeros(up_all.shape, BF)
    copies[0].wait()
    for k in range(3):
        for part in range(2):
            first_row = (3 * part + k) * SPAN
            up_all[first_row : first_row + SPAN, k * up.shape[2] : (k + 1) * up.shape[2]] = up[k]
    for c in copies[1:6]:
        c.wait()
    blocks = own.shape[0]
    width = own.shape[2]
    tp = me[0]
    spans = [span(tp * width, width), span((tp ^ 1) * width, width)]
    pair_lane = lax.broadcasted_iota(jnp.int32, (2 * CAP, 2 * CAP), 1)
    pair_row = lax.broadcasted_iota(jnp.int32, (2 * CAP, 2 * CAP), 0)
    eye = pair_lane == pair_row
    lane_sel = ((pair_lane // RANK) % ADAPT_DEV).astype(F32)
    tile = min(4, blocks)

    def step(t):
        rs = span(t * (tile * CAP), tile * CAP)
        bs = pl.ds(t * tile, tile)
        xs = [part[bs, :CAP, :].reshape(tile * CAP, width) for part in (own, beside)]
        for k in range(3):
            acc[k, rs] = dot(xs[0], w[k, spans[0]]) + dot(xs[1], w[k, spans[1]])
        low[rs] = dot_t(xs[0], down[:, spans[0]]) + dot_t(xs[1], down[:, spans[1]])
        for p in range(tile // 2):
            b0 = t * tile + 2 * p
            c0 = own[b0, CAP : CAP + 1, : 2 * CAP].astype(F32)
            c1 = own[b0 + 1, CAP : CAP + 1, : 2 * CAP].astype(F32) + 64.0
            idr = jnp.where(pair_lane < CAP, c0, c1)
            idc = jnp.sum(jnp.where(eye, idr, 0.0), axis=1, keepdims=True)
            ps = span(t * (tile * CAP) + p * 2 * CAP, 2 * CAP)
            bias_out[ps] = jnp.where(idr == idc, 0.0, -1e30)
            pick = idc - 1.0
            pick = pick - 2.0 * jnp.floor(pick * 0.5)
            sel_out[ps] = (lane_sel == pick).astype(BF)

    tiles(blocks // tile, step)
    for c in copies[6:]:
        c.wait()


def attn_kernel(n_tp, chunk, me, *refs):
    parts = refs[:n_tp]
    acc, low_in, sel_in, bias, w, down, up_all, att, x_full = refs[n_tp:]
    blocks = att.shape[0] // CAP
    width = parts[0].shape[2]
    rows = blocks * CAP
    tp = me[0]
    spans = [span((tp ^ r) * width, width) for r in range(n_tp)]
    for r in range(n_tp):
        offset = chunk * blocks if part_of(parts[r], blocks) else 0
        x_full[:, spans[r]] = parts[r][offset : offset + blocks, :CAP, :].reshape(rows, width)
    first = lax.broadcasted_iota(jnp.int32, (2 * CAP, 2 * CAP), 1) < HEAD_DIM
    zero = jnp.zeros((), BF)
    tile = min(4, blocks)

    def step(t):
        start = t * (tile * CAP)
        rs = span(start, tile * CAP)
        whole = span(chunk * rows + start, tile * CAP)
        bs = pl.ds(t * tile, tile)
        xs = [parts[r][bs, :CAP, :].reshape(tile * CAP, width) for r in range(2, n_tp)]
        low = low_in[whole]
        for r in range(2, n_tp):
            low = low + dot_t(xs[r - 2], down[:, spans[r]])
        sel = sel_in[whole].astype(F32)
        low = split_two(low, jnp.concatenate([sel, sel[:, : 2 * SPAN]], axis=1))
        qkv = []
        for k in range(3):
            total = acc[k, whole] + dot(low, up_all[:, k * width : (k + 1) * width])
            for r in range(2, n_tp):
                total = total + dot(xs[r - 2], w[k, spans[r]])
            qkv.append(total.astype(BF))
        q, k_, v = qkv
        q = (q.astype(F32) * HEAD_DIM**-0.5).astype(BF)
        for p in range(tile // 2):
            prs = slice(p * 2 * CAP, (p + 1) * 2 * CAP)
            out_rows = span(start + p * 2 * CAP, 2 * CAP)
            mask = bias[span(chunk * rows + start + p * 2 * CAP, 2 * CAP)]
            for h in range(width // (2 * HEAD_DIM)):
                cs = slice(h * 2 * HEAD_DIM, (h + 1) * 2 * HEAD_DIM)
                both = []
                for half in (first, ~first):
                    s = dot_t(jnp.where(half, q[prs, cs], zero), k_[prs, cs]) + mask
                    e = jnp.exp(s - jnp.max(s, axis=-1, keepdims=True))
                    inv = 1.0 / jnp.sum(e, axis=-1, keepdims=True)
                    both.append(dot((e * inv).astype(BF), v[prs, cs]))
                att[out_rows, cs] = jnp.where(first, *both).astype(BF)

    tiles(blocks // tile, step)


def part_of(array, blocks):
    return array.shape[0] > blocks


def ffn_kernel(n_tp, chunk, me, *refs):
    atts, wouts, odowns = refs[:n_tp], refs[n_tp : 2 * n_tp], refs[2 * n_tp : 3 * n_tp]
    x, sel_in, oup, d1, u1, d2, u2, g1, b1, w1, w2 = refs[3 * n_tp : 3 * n_tp + 11]
    even, odd, odds, h_own, h_scr = refs[3 * n_tp + 11 :]
    rows, feat = x.shape
    blocks = rows // CAP
    share = CAP // n_tp
    tp = me[0]
    size = min(rows, 256)
    nb = size // CAP
    ups = [jnp.concatenate([u[...], u[...]], axis=0) for u in (oup, u1, u2)]

    def step(t):
        rs = span(t * size, size)
        sel = sel_in[span(chunk * rows + t * size, size)].astype(F32)[:, : 2 * SPAN]
        low = None
        for r in range(n_tp):
            part = dot_t(atts[r][rs], twice(odowns[r]))
            low = part if low is None else low + part
        low = split_two(low, sel)
        total = x[rs].astype(F32)
        for r in range(n_tp):
            total = total + dot(atts[r][rs], wouts[r][...])
        total = total + dot(low, ups[0])
        h1 = layer_norm(total, g1[...], b1[...]).astype(BF)
        h_scr[span(t * nb, nb)] = h1.reshape(nb, n_tp, share, feat)
        low = split_two(dot_t(h1, twice(d1)), sel)
        pieces = []
        for n in range(4):
            ns = slice(n * w1.shape[1] // 4, (n + 1) * w1.shape[1] // 4)
            gate = dot(h1, w1[:, ns]) + dot(low, ups[1][:, ns])
            pieces.append((0.5 * gate * (1.0 + lax.erf(gate * 0.7071067811865476))).astype(BF))
        hidden = jnp.concatenate(pieces, axis=1)
        low = split_two(dot_t(hidden, twice(d2)), sel)
        term = dot(hidden, w2[...]) + dot(low, ups[2])
        term = term.reshape(nb, n_tp, share, feat)
        own_rows = span(t * (size // n_tp), size // n_tp)
        for j in range(n_tp):
            rel = tp ^ j
            piece = term[:, j].reshape(nb * share, feat)

            @pl.when(rel % 2 == 0)
            def _():
                even[rel // 2, own_rows, :] = piece

            @pl.when(rel == 1)
            def _():
                odd[own_rows, :] = piece.astype(BF)

            @pl.when((rel % 2 == 1) & (rel > 1))
            def _():
                odds[rel // 2 - 1, own_rows, :] = piece.astype(BF)

    tiles(rows // size, step)
    h_own[...] = h_scr[:, tp].reshape(blocks * share, feat)


def last_kernel(n_tp, earlier, *refs):
    g2, b2, out = refs[-3:]
    even, got, h_own = refs[earlier : earlier + 3]
    _, share, width = out.shape[1:]
    step = h_own.shape[0] // share
    total = h_own[...].astype(F32) + (even[0] + got[...].astype(F32))
    for arrived in refs[earlier + 3 : -3]:
        total = total + arrived[...].astype(F32)
    done = layer_norm(total, g2[...], b2[...]).astype(BF)
    if earlier:
        out[: refs[0].shape[0]] = refs[0][...]
    for f in range(n_tp):
        piece = done[:, f * width : (f + 1) * width].reshape(step, share, width)
        out[out.shape[0] - step :, f] = piece


def unpack_kernel(owners, arrived, out, sems):
    pairs = [(arrived.at[owners[g]], out.at[g]) for g in range(out.shape[0])]
    for c in fetch(pairs, sems):
        c.wait()


VM = pl.BlockSpec(memory_space=pltpu.VMEM)
HBM = pl.BlockSpec(memory_space=pltpu.HBM)
SMEM = pl.BlockSpec(memory_space=pltpu.SMEM)


def near(*arrays):
    return [pltpu.with_memory_space_constraint(a, pltpu.VMEM) for a in arrays]


def far(*arrays):
    return [pltpu.with_memory_space_constraint(a, pltpu.HBM) for a in arrays]


def work(flops, rows):
    return pl.CostEstimate(flops=5 * flops, transcendentals=rows * 1024, bytes_accessed=rows * 8192)


def params(mib=20):
    return pltpu.CompilerParams(vmem_limit_bytes=mib * 1024 * 1024)


def body(
    tokens,
    prompt_lengths,
    adapter_ids,
    adapter_slot,
    w_qkv,
    w_out,
    w_fc1,
    w_fc2,
    qkv_down,
    qkv_up,
    out_down,
    out_up,
    fc1_down,
    fc1_up,
    fc2_down,
    fc2_up,
    norm1_gain,
    norm1_bias,
    norm2_gain,
    norm2_bias,
):
    n_req = lax.axis_size("req")
    n_tp = lax.axis_size("tp")
    feat = w_qkv.shape[1]
    width = tokens.shape[1]
    blocks = tokens.shape[0] // CAP
    share = CAP // n_tp
    half = n_tp // 2
    me = jnp.reshape(lax.axis_index("tp"), (1,)).astype(jnp.int32)

    def swap(value, r):
        return lax.ppermute(value, "tp", [(i, i ^ r) for i in range(n_tp)])

    def second_hop(pieces):
        return [hop for piece in pieces for hop in (piece, swap(piece, 1))]

    packed, owners = pl.pallas_call(
        pack_kernel,
        out_shape=(
            pltpu.VMEM((n_req, CAP + PAD, width), BF),
            jax.ShapeDtypeStruct((blocks,), jnp.int32),
        ),
        in_specs=[HBM] * 4,
        out_specs=(VM, SMEM),
        scratch_shapes=[
            pltpu.SMEM((SEQ_G, blocks), jnp.int32),
            pltpu.SMEM((SEQ_G, blocks), jnp.int32),
            pltpu.SMEM(adapter_slot.shape, jnp.int32),
            pltpu.VMEM((blocks, CAP, width), BF),
            pltpu.SemaphoreType.DMA((4,)),
        ],
        compiler_params=params(4),
        name="pack",
    )(
        *far(
            prompt_lengths.T,
            adapter_ids.T,
            adapter_slot,
            tokens.reshape(blocks, CAP, width),
        )
    )
    packed, me, w_first, o_first = lax.optimization_barrier(
        (packed, me, w_out, out_down.T)
    )
    arrived = lax.all_to_all(packed, "req", split_axis=0, concat_axis=0, tiled=True)
    w_far = [swap(w_first, 2 * y) for y in range(1, half)]
    w_near = swap(w_first, 1)
    odowns = [out_down.T] + [swap(o_first, r) for r in range(1, n_tp)]
    arrived, w_far, w_near, odowns = lax.optimization_barrier((arrived, w_far, w_near, odowns))
    count = 2
    step_blocks = n_req // count
    rows = step_blocks * CAP
    own = rows // n_tp
    beside = swap(arrived, 1)
    x_far = []
    for c in range(count):
        piece = arrived[c * step_blocks : (c + 1) * step_blocks]
        x_far.append([swap(piece, 2 * y) for y in range(1, half)])
    *begun, w_all, w1, w2, downs, up_all = pl.pallas_call(
        begin_kernel,
        out_shape=[
            pltpu.VMEM((3, count * rows, width), F32),
            pltpu.VMEM((count * rows, 6 * SPAN), F32),
            pltpu.VMEM((count * rows, 4 * SPAN), BF),
            pltpu.VMEM((count * rows, 2 * CAP), F32),
            pltpu.VMEM((3, feat, width), BF),
            pltpu.VMEM(w_fc1.shape, BF),
            pltpu.VMEM(w_fc2.shape, BF),
            pltpu.VMEM((6 * SPAN, feat), BF),
            pltpu.VMEM((6 * SPAN, 3 * width), BF),
        ],
        in_specs=[SMEM] + [VM] * 2 + [HBM] * 5,
        out_specs=[VM] * 9,
        scratch_shapes=[
            pltpu.VMEM((3, SPAN, width), BF),
            pltpu.SemaphoreType.DMA((10,)),
        ],
        compiler_params=params(8),
        cost_estimate=work(rows * feat * 3 * width, rows),
        name="begin",
    )(
        me,
        *near(arrived, beside),
        *far(
            w_qkv,
            w_fc1,
            w_fc2,
            jnp.swapaxes(qkv_down, 1, 2).reshape(3 * SPAN, feat),
            qkv_up,
        ),
    )
    w_all, w1, w2, downs, up_all = near(w_all, w1, w2, downs, up_all)
    x_far[0], begun = lax.optimization_barrier((x_far[0], begun))
    x_far[0] = second_hop(x_far[0])
    x_far = lax.optimization_barrier(x_far)
    x_far[1:] = [second_hop(pieces) for pieces in x_far[1:]]

    consts = near(
        out_up, fc1_down.T, fc1_up, fc2_down.T, fc2_up, norm1_gain[None], norm1_bias[None]
    )
    sel = begun[2]
    steps = []
    for c in range(count):
        if c:
            w_far, steps[0][0] = lax.optimization_barrier((w_far, steps[0][0]))
        attended, x_full = pl.pallas_call(
            functools.partial(attn_kernel, n_tp, c),
            out_shape=[pltpu.VMEM((rows, width), BF), pltpu.VMEM((rows, feat), BF)],
            in_specs=[SMEM] + [VM] * (n_tp + 7),
            out_specs=[VM] * 2,
            compiler_params=params(12),
            cost_estimate=work(8 * rows * feat * 3 * width + 16 * rows * width * 2 * CAP, rows),
            name="attend",
        )(me, *near(arrived, beside, *x_far[c], *begun), w_all, downs, up_all)
        y_got = [swap(attended, 2 * y) for y in range(1, half)]
        if c:
            steps[0][1], attended = lax.optimization_barrier((steps[0][1], attended))
        steps.append([attended, y_got, x_full])
    wouts = [w_out, w_near] + second_hop(w_far)

    def finish(earlier, *values):
        blocks_done = step_blocks + sum(e.shape[0] for e in earlier)
        values = near(*earlier, *values, norm2_gain[None], norm2_bias[None])
        return pl.pallas_call(
            functools.partial(last_kernel, n_tp, len(earlier)),
            out_shape=pltpu.VMEM((blocks_done, n_tp, share, width), BF),
            in_specs=[VM] * len(values),
            out_specs=VM,
            compiler_params=params(8),
            name="finish",
        )(*values)

    for c in range(count):
        attended, y_got, x_full = steps[c]
        atts = second_hop([attended] + y_got)
        if c:
            atts, firsts = lax.optimization_barrier((atts, firsts))
            firsts = [swap(piece, 2 * (y + 1)) for y, piece in enumerate(firsts)]
        even, odd, odds, h_own = pl.pallas_call(
            functools.partial(ffn_kernel, n_tp, c),
            out_shape=[
                pltpu.VMEM((half, own, feat), F32),
                pltpu.VMEM((own, feat), BF),
                pltpu.VMEM((half - 1, own, feat), BF),
                pltpu.VMEM((own, feat), BF),
            ],
            in_specs=[SMEM] + [VM] * (3 * n_tp + 4 + len(consts)),
            out_specs=[VM] * 4,
            scratch_shapes=[pltpu.VMEM((step_blocks, n_tp, share, feat), BF)],
            compiler_params=params(16),
            cost_estimate=work(2 * rows * feat * (2 * w_fc1.shape[1] + feat), rows),
            name="feed",
        )(me, *near(*atts, *wouts, *odowns, x_full, sel), *consts, w1, w2)
        gots = swap(odds, 1)
        if c:
            earlier = finish([], *first_ends, *firsts)
            gots, earlier = lax.optimization_barrier((gots, earlier))
        sends = [(even[y] + gots[y - 1].astype(F32)).astype(BF) for y in range(1, half)]
        ends = [even, swap(odd, 1), h_own]
        if c == 0:
            firsts, first_ends = sends, ends
        else:
            sends = [swap(piece, 2 * (y + 1)) for y, piece in enumerate(sends)]
            done = finish([earlier], *ends, *sends)
    back = lax.all_to_all(
        done.reshape(n_req * n_tp, share, width),
        ("req", "tp"),
        split_axis=0,
        concat_axis=0,
        tiled=True,
    )
    result = pl.pallas_call(
        unpack_kernel,
        out_shape=jax.ShapeDtypeStruct((blocks, CAP, width), BF),
        in_specs=[SMEM, VM],
        out_specs=HBM,
        scratch_shapes=[pltpu.SemaphoreType.DMA((blocks,))],
        compiler_params=params(4),
        name="unpack",
    )(owners, *near(back.reshape(n_req, CAP, width)))
    return result.reshape(blocks * CAP, width)


def solution(mesh):
    placed = (
        P("req", "tp"),
        P("req", None),
        P("req", None),
        P(),
        P(None, None, "tp"),
        P("tp", None),
        P(None, "tp"),
        P("tp", None),
        P(None, None, "req"),
        P(None, "req", "tp"),
        P("tp", "req"),
        P("req", None),
        P(None, "req"),
        P("req", "tp"),
        P("tp", "req"),
        P("req", None),
        P(),
        P(),
        P(),
        P(),
    )
    return jax.shard_map(
        body, mesh=mesh, in_specs=placed, out_specs=P("req", "tp"), check_vma=False
    )
```

```python
import functools

import jax
import jax.numpy as jnp
from jax import lax
from jax.experimental import pallas as pl
from jax.experimental.pallas import tpu as pltpu
from jax.sharding import PartitionSpec as P

HEAD_DIM = 64
RANK = 16
ADAPT_DEV = 2
CAP = 64
SEQ_G = 4
SPAN = ADAPT_DEV * RANK
PAD = 8
NORM_EPS = 1e-05
BF = jnp.bfloat16
F32 = jnp.float32


def dot(a, b):
    return lax.dot_general(a, b, (((1,), (0,)), ((), ())), preferred_element_type=F32)


def dot_t(a, b):
    return lax.dot_general(a, b, (((1,), (1,)), ((), ())), preferred_element_type=F32)


def layer_norm(values, gain, shift):
    mean = jnp.mean(values, axis=-1, keepdims=True)
    centred = values - mean
    variance = jnp.mean(centred * centred, axis=-1, keepdims=True)
    return centred * lax.rsqrt(variance + NORM_EPS) * gain + shift


def split_low(low, sel):
    low = low * sel
    high = low.astype(BF).astype(F32)
    return jnp.concatenate([high, low - high], axis=1).astype(BF)


def fetch(pairs, sems):
    copies = [
        pltpu.make_async_copy(src, dst, sems.at[i]) for i, (src, dst) in enumerate(pairs)
    ]
    for c in copies:
        c.start()
    return copies


def twice(ref):
    return jnp.concatenate([ref[...], ref[...]], axis=0)


def split_two(low, sel):
    low = low * sel
    high = low.astype(BF).astype(F32)
    lane = lax.broadcasted_iota(jnp.int32, low.shape, 1)
    return jnp.where(lane < low.shape[1] // 2, high, low - high).astype(BF)


def pack_kernel(
    lengths_in, ids_in, slots_in, tok_in, out, owners, lengths, ids, slots, tok, sems
):
    copies = fetch(
        [(lengths_in, lengths), (ids_in, ids), (slots_in, slots), (tok_in, tok)], sems
    )
    blocks = tok.shape[0]
    if out.shape[0] > blocks:
        out[...] = jnp.zeros(out.shape, out.dtype)
    width = out.shape[2]
    pos = lax.broadcasted_iota(jnp.int32, (PAD, width), 1) % CAP
    for c in copies:
        c.wait()
    for g in range(blocks):
        slot = [slots[ids[k, g]] for k in range(SEQ_G)]
        owner = slot[0] // ADAPT_DEV
        owners[g] = owner
        code = jnp.full((PAD, width), 1 + slot[0] % ADAPT_DEV, jnp.int32)
        end = jnp.int32(0)
        for k in range(1, SEQ_G):
            end = end + lengths[k - 1, g]
            code = jnp.where(pos >= end, 1 + k * ADAPT_DEV + slot[k] % ADAPT_DEV, code)
        out[owner, :CAP, :] = tok[g]
        out[owner, CAP:, :] = code.astype(F32).astype(BF)


def tiles(count, step):
    step(0)
    if count == 2:
        step(1)
    elif count > 2:
        lax.fori_loop(1, count, lambda t, c: (step(t), c)[1], 0)


def span(start, size):
    return pl.ds(start if isinstance(start, int) else pl.multiple_of(start, size), size)


def begin_kernel(
    me, own, beside, w_in, w1_in, w2_in, down_in, up_in, *refs
):
    acc, low, sel_out, bias_out, w, w1, w2, down, up_all, up, sems = refs
    pairs = [(up_in, up), (down_in, down)] + [(w_in.at[k], w.at[k]) for k in range(3)]
    for src, dst in ((w1_in, w1), (w2_in, w2)):
        half = src.shape[0] // 2
        pairs += [(src.at[:half], dst.at[:half]), (src.at[half:], dst.at[half:])]
    copies = fetch(pairs, sems)
    up_all[...] = jnp.zeros(up_all.shape, BF)
    copies[0].wait()
    for k in range(3):
        for part in range(2):
            first_row = (3 * part + k) * SPAN
            up_all[first_row : first_row + SPAN, k * up.shape[2] : (k + 1) * up.shape[2]] = up[k]
    for c in copies[1:5]:
        c.wait()
    blocks = own.shape[0]
    width = own.shape[2]
    tp = me[0]
    spans = [span(tp * width, width), span((tp ^ 1) * width, width)]
    pair_lane = lax.broadcasted_iota(jnp.int32, (2 * CAP, 2 * CAP), 1)
    pair_row = lax.broadcasted_iota(jnp.int32, (2 * CAP, 2 * CAP), 0)
    eye = pair_lane == pair_row
    lane_sel = ((pair_lane // RANK) % ADAPT_DEV).astype(F32)
    tile = min(4, blocks)

    def step(t):
        rs = span(t * (tile * CAP), tile * CAP)
        bs = pl.ds(t * tile, tile)
        xs = [part[bs, :CAP, :].reshape(tile * CAP, width) for part in (own, beside)]
        for k in range(3):
            acc[k, rs] = dot(xs[0], w[k, spans[0]]) + dot(xs[1], w[k, spans[1]])
        low[rs] = dot_t(xs[0], down[:, spans[0]]) + dot_t(xs[1], down[:, spans[1]])
        for p in range(tile // 2):
            b0 = t * tile + 2 * p
            c0 = own[b0, CAP : CAP + 1, : 2 * CAP].astype(F32)
            c1 = own[b0 + 1, CAP : CAP + 1, : 2 * CAP].astype(F32) + 64.0
            idr = jnp.where(pair_lane < CAP, c0, c1)
            idc = jnp.sum(jnp.where(eye, idr, 0.0), axis=1, keepdims=True)
            ps = span(t * (tile * CAP) + p * 2 * CAP, 2 * CAP)
            bias_out[ps] = jnp.where(idr == idc, 0.0, -1e30)
            pick = idc - 1.0
            pick = pick - 2.0 * jnp.floor(pick * 0.5)
            sel_out[ps] = (lane_sel == pick).astype(BF)

    tiles(blocks // tile, step)
    for c in copies[5:]:
        c.wait()


def attn_kernel(n_tp, chunk, me, *refs):
    parts = refs[:n_tp]
    acc, low_in, sel_in, bias, w, down, up_all, att, x_full = refs[n_tp:]
    blocks = att.shape[0] // CAP
    width = parts[0].shape[2]
    rows = blocks * CAP
    tp = me[0]
    spans = [span((tp ^ r) * width, width) for r in range(n_tp)]
    for r in range(n_tp):
        offset = chunk * blocks if part_of(parts[r], blocks) else 0
        x_full[:, spans[r]] = parts[r][offset : offset + blocks, :CAP, :].reshape(rows, width)
    first = lax.broadcasted_iota(jnp.int32, (2 * CAP, 2 * CAP), 1) < HEAD_DIM
    zero = jnp.zeros((), BF)
    tile = min(4, blocks)

    def step(t):
        start = t * (tile * CAP)
        rs = span(start, tile * CAP)
        whole = span(chunk * rows + start, tile * CAP)
        bs = pl.ds(t * tile, tile)
        xs = [parts[r][bs, :CAP, :].reshape(tile * CAP, width) for r in range(2, n_tp)]
        low = low_in[whole]
        for r in range(2, n_tp):
            low = low + dot_t(xs[r - 2], down[:, spans[r]])
        low = split_low(low, sel_in[whole].astype(F32)[:, : 3 * SPAN])
        qkv = []
        for k in range(3):
            total = acc[k, whole] + dot(low, up_all[:, k * width : (k + 1) * width])
            for r in range(2, n_tp):
                total = total + dot(xs[r - 2], w[k, spans[r]])
            qkv.append(total.astype(BF))
        q, k_, v = qkv
        q = (q.astype(F32) * HEAD_DIM**-0.5).astype(BF)
        for p in range(tile // 2):
            prs = slice(p * 2 * CAP, (p + 1) * 2 * CAP)
            out_rows = span(start + p * 2 * CAP, 2 * CAP)
            mask = bias[span(chunk * rows + start + p * 2 * CAP, 2 * CAP)]
            for h in range(width // (2 * HEAD_DIM)):
                cs = slice(h * 2 * HEAD_DIM, (h + 1) * 2 * HEAD_DIM)
                both = []
                for half in (first, ~first):
                    s = dot_t(jnp.where(half, q[prs, cs], zero), k_[prs, cs]) + mask
                    e = jnp.exp(s - jnp.max(s, axis=-1, keepdims=True))
                    inv = 1.0 / jnp.sum(e, axis=-1, keepdims=True)
                    both.append(dot((e * inv).astype(BF), v[prs, cs]))
                att[out_rows, cs] = jnp.where(first, *both).astype(BF)

    tiles(blocks // tile, step)


def part_of(array, blocks):
    return array.shape[0] > blocks


def ffn_kernel(n_tp, chunk, me, *refs):
    atts, wouts, odowns = refs[:n_tp], refs[n_tp : 2 * n_tp], refs[2 * n_tp : 3 * n_tp]
    x, sel_in, oup, d1, u1, d2, u2, g1, b1, w1, w2 = refs[3 * n_tp : 3 * n_tp + 11]
    even, odd, odds, h_own, h_scr = refs[3 * n_tp + 11 :]
    rows, feat = x.shape
    blocks = rows // CAP
    share = CAP // n_tp
    tp = me[0]
    size = min(rows, 256)
    nb = size // CAP
    ups = [jnp.concatenate([u[...], u[...]], axis=0) for u in (oup, u1, u2)]

    def step(t):
        rs = span(t * size, size)
        sel = sel_in[span(chunk * rows + t * size, size)].astype(F32)[:, : 2 * SPAN]
        low = None
        for r in range(n_tp):
            part = dot_t(atts[r][rs], twice(odowns[r]))
            low = part if low is None else low + part
        low = split_two(low, sel)
        total = x[rs].astype(F32)
        for r in range(n_tp):
            total = total + dot(atts[r][rs], wouts[r][...])
        total = total + dot(low, ups[0])
        h1 = layer_norm(total, g1[...], b1[...]).astype(BF)
        h_scr[span(t * nb, nb)] = h1.reshape(nb, n_tp, share, feat)
        low = split_two(dot_t(h1, twice(d1)), sel)
        pieces = []
        for n in range(4):
            ns = slice(n * w1.shape[1] // 4, (n + 1) * w1.shape[1] // 4)
            gate = dot(h1, w1[:, ns]) + dot(low, ups[1][:, ns])
            pieces.append((0.5 * gate * (1.0 + lax.erf(gate * 0.7071067811865476))).astype(BF))
        hidden = jnp.concatenate(pieces, axis=1)
        low = split_two(dot_t(hidden, twice(d2)), sel)
        term = dot(hidden, w2[...]) + dot(low, ups[2])
        term = term.reshape(nb, n_tp, share, feat)
        own_rows = span(t * (size // n_tp), size // n_tp)
        for j in range(n_tp):
            rel = tp ^ j
            piece = term[:, j].reshape(nb * share, feat)

            @pl.when(rel % 2 == 0)
            def _():
                even[rel // 2, own_rows, :] = piece

            @pl.when(rel == 1)
            def _():
                odd[own_rows, :] = piece.astype(BF)

            @pl.when((rel % 2 == 1) & (rel > 1))
            def _():
                odds[rel // 2 - 1, own_rows, :] = piece.astype(BF)

    tiles(rows // size, step)
    h_own[...] = h_scr[:, tp].reshape(blocks * share, feat)


def last_kernel(n_tp, earlier, *refs):
    g2, b2, out = refs[-3:]
    even, got, h_own = refs[earlier : earlier + 3]
    _, share, width = out.shape[1:]
    step = h_own.shape[0] // share
    total = h_own[...].astype(F32) + (even[0] + got[...].astype(F32))
    for arrived in refs[earlier + 3 : -3]:
        total = total + arrived[...].astype(F32)
    done = layer_norm(total, g2[...], b2[...]).astype(BF)
    if earlier:
        out[: refs[0].shape[0]] = refs[0][...]
    for f in range(n_tp):
        piece = done[:, f * width : (f + 1) * width].reshape(step, share, width)
        out[out.shape[0] - step :, f] = piece


def unpack_kernel(owners, arrived, out):
    for g in range(out.shape[0]):
        out[g] = arrived[owners[g]]


VM = pl.BlockSpec(memory_space=pltpu.VMEM)
HBM = pl.BlockSpec(memory_space=pltpu.HBM)
SMEM = pl.BlockSpec(memory_space=pltpu.SMEM)


def near(*arrays):
    return [pltpu.with_memory_space_constraint(a, pltpu.VMEM) for a in arrays]


def far(*arrays):
    return [pltpu.with_memory_space_constraint(a, pltpu.HBM) for a in arrays]


def work(flops, rows):
    return pl.CostEstimate(flops=5 * flops, transcendentals=rows * 1024, bytes_accessed=rows * 8192)


def params(mib=20):
    return pltpu.CompilerParams(vmem_limit_bytes=mib * 1024 * 1024)


def body(
    tokens,
    prompt_lengths,
    adapter_ids,
    adapter_slot,
    w_qkv,
    w_out,
    w_fc1,
    w_fc2,
    qkv_down,
    qkv_up,
    out_down,
    out_up,
    fc1_down,
    fc1_up,
    fc2_down,
    fc2_up,
    norm1_gain,
    norm1_bias,
    norm2_gain,
    norm2_bias,
):
    n_req = lax.axis_size("req")
    n_tp = lax.axis_size("tp")
    feat = w_qkv.shape[1]
    width = tokens.shape[1]
    blocks = tokens.shape[0] // CAP
    share = CAP // n_tp
    half = n_tp // 2
    me = jnp.reshape(lax.axis_index("tp"), (1,)).astype(jnp.int32)

    def swap(value, r):
        return lax.ppermute(value, "tp", [(i, i ^ r) for i in range(n_tp)])

    def second_hop(pieces):
        return [hop for piece in pieces for hop in (piece, swap(piece, 1))]

    packed, owners = pl.pallas_call(
        pack_kernel,
        out_shape=(
            pltpu.VMEM((n_req, CAP + PAD, width), BF),
            jax.ShapeDtypeStruct((blocks,), jnp.int32),
        ),
        in_specs=[HBM] * 4,
        out_specs=(VM, SMEM),
        scratch_shapes=[
            pltpu.SMEM((SEQ_G, blocks), jnp.int32),
            pltpu.SMEM((SEQ_G, blocks), jnp.int32),
            pltpu.SMEM(adapter_slot.shape, jnp.int32),
            pltpu.VMEM((blocks, CAP, width), BF),
            pltpu.SemaphoreType.DMA((4,)),
        ],
        compiler_params=params(4),
        name="pack",
    )(
        *far(
            prompt_lengths.T,
            adapter_ids.T,
            adapter_slot,
            tokens.reshape(blocks, CAP, width),
        )
    )
    packed, me, w_first, o_first = lax.optimization_barrier(
        (packed, me, w_out, out_down.T)
    )
    arrived = lax.all_to_all(packed, "req", split_axis=0, concat_axis=0, tiled=True)
    w_far = [swap(w_first, 2 * y) for y in range(1, half)]
    w_near = swap(w_first, 1)
    odowns = [out_down.T] + [swap(o_first, r) for r in range(1, n_tp)]
    arrived, w_far, w_near, odowns = lax.optimization_barrier((arrived, w_far, w_near, odowns))
    count = 2
    step_blocks = n_req // count
    rows = step_blocks * CAP
    own = rows // n_tp
    beside = swap(arrived, 1)
    x_far = []
    for c in range(count):
        piece = arrived[c * step_blocks : (c + 1) * step_blocks]
        x_far.append([swap(piece, 2 * y) for y in range(1, half)])
    *begun, w_all, w1, w2, downs, up_all = pl.pallas_call(
        begin_kernel,
        out_shape=[
            pltpu.VMEM((3, count * rows, width), F32),
            pltpu.VMEM((count * rows, 3 * SPAN), F32),
            pltpu.VMEM((count * rows, 4 * SPAN), BF),
            pltpu.VMEM((count * rows, 2 * CAP), F32),
            pltpu.VMEM((3, feat, width), BF),
            pltpu.VMEM(w_fc1.shape, BF),
            pltpu.VMEM(w_fc2.shape, BF),
            pltpu.VMEM((3 * SPAN, feat), BF),
            pltpu.VMEM((6 * SPAN, 3 * width), BF),
        ],
        in_specs=[SMEM] + [VM] * 2 + [HBM] * 5,
        out_specs=[VM] * 9,
        scratch_shapes=[
            pltpu.VMEM((3, SPAN, width), BF),
            pltpu.SemaphoreType.DMA((9,)),
        ],
        compiler_params=params(8),
        cost_estimate=work(rows * feat * 3 * width, rows),
        name="begin",
    )(
        me,
        *near(arrived, beside),
        *far(
            w_qkv,
            w_fc1,
            w_fc2,
            jnp.swapaxes(qkv_down, 1, 2).reshape(3 * SPAN, feat),
            qkv_up,
        ),
    )
    w_all, w1, w2, downs, up_all = near(w_all, w1, w2, downs, up_all)
    x_far[0], begun = lax.optimization_barrier((x_far[0], begun))
    x_far[0] = second_hop(x_far[0])
    x_far = lax.optimization_barrier(x_far)
    x_far[1:] = [second_hop(pieces) for pieces in x_far[1:]]

    consts = near(
        out_up, fc1_down.T, fc1_up, fc2_down.T, fc2_up, norm1_gain[None], norm1_bias[None]
    )
    sel = begun[2]
    steps = []
    for c in range(count):
        if c:
            w_far, steps[0][0] = lax.optimization_barrier((w_far, steps[0][0]))
        attended, x_full = pl.pallas_call(
            functools.partial(attn_kernel, n_tp, c),
            out_shape=[pltpu.VMEM((rows, width), BF), pltpu.VMEM((rows, feat), BF)],
            in_specs=[SMEM] + [VM] * (n_tp + 7),
            out_specs=[VM] * 2,
            compiler_params=params(12),
            cost_estimate=work(8 * rows * feat * 3 * width + 16 * rows * width * 2 * CAP, rows),
            name="attend",
        )(me, *near(arrived, beside, *x_far[c], *begun), w_all, downs, up_all)
        y_got = [swap(attended, 2 * y) for y in range(1, half)]
        if c:
            steps[0][1], attended = lax.optimization_barrier((steps[0][1], attended))
        steps.append([attended, y_got, x_full])
    wouts = [w_out, w_near] + second_hop(w_far)

    def finish(earlier, *values):
        blocks_done = step_blocks + sum(e.shape[0] for e in earlier)
        values = near(*earlier, *values, norm2_gain[None], norm2_bias[None])
        return pl.pallas_call(
            functools.partial(last_kernel, n_tp, len(earlier)),
            out_shape=pltpu.VMEM((blocks_done, n_tp, share, width), BF),
            in_specs=[VM] * len(values),
            out_specs=VM,
            compiler_params=params(8),
            name="finish",
        )(*values)

    for c in range(count):
        attended, y_got, x_full = steps[c]
        atts = second_hop([attended] + y_got)
        if c:
            atts, firsts = lax.optimization_barrier((atts, firsts))
            firsts = [swap(piece, 2 * (y + 1)) for y, piece in enumerate(firsts)]
        even, odd, odds, h_own = pl.pallas_call(
            functools.partial(ffn_kernel, n_tp, c),
            out_shape=[
                pltpu.VMEM((half, own, feat), F32),
                pltpu.VMEM((own, feat), BF),
                pltpu.VMEM((half - 1, own, feat), BF),
                pltpu.VMEM((own, feat), BF),
            ],
            in_specs=[SMEM] + [VM] * (3 * n_tp + 4 + len(consts)),
            out_specs=[VM] * 4,
            scratch_shapes=[pltpu.VMEM((step_blocks, n_tp, share, feat), BF)],
            compiler_params=params(16),
            cost_estimate=work(2 * rows * feat * (2 * w_fc1.shape[1] + feat), rows),
            name="feed",
        )(me, *near(*atts, *wouts, *odowns, x_full, sel), *consts, w1, w2)
        gots = swap(odds, 1)
        if c:
            earlier = finish([], *first_ends, *firsts)
            gots, earlier = lax.optimization_barrier((gots, earlier))
        sends = [(even[y] + gots[y - 1].astype(F32)).astype(BF) for y in range(1, half)]
        ends = [even, swap(odd, 1), h_own]
        if c == 0:
            firsts, first_ends = sends, ends
        else:
            sends = [swap(piece, 2 * (y + 1)) for y, piece in enumerate(sends)]
            done = finish([earlier], *ends, *sends)
    back = lax.all_to_all(
        done.reshape(n_req * n_tp, share, width),
        ("req", "tp"),
        split_axis=0,
        concat_axis=0,
        tiled=True,
    )
    result = pl.pallas_call(
        unpack_kernel,
        out_shape=jax.ShapeDtypeStruct((blocks, CAP, width), BF),
        in_specs=[SMEM, VM],
        out_specs=VM,
        compiler_params=params(4),
        name="unpack",
    )(owners, *near(back.reshape(n_req, CAP, width)))
    return result.reshape(blocks * CAP, width)


def solution(mesh):
    placed = (
        P("req", "tp"),
        P("req", None),
        P("req", None),
        P(),
        P(None, None, "tp"),
        P("tp", None),
        P(None, "tp"),
        P("tp", None),
        P(None, None, "req"),
        P(None, "req", "tp"),
        P("tp", "req"),
        P("req", None),
        P(None, "req"),
        P("req", "tp"),
        P("tp", "req"),
        P("req", None),
        P(),
        P(),
        P(),
        P(),
    )
    return jax.shard_map(
        body, mesh=mesh, in_specs=placed, out_specs=P("req", "tp"), check_vma=False
    )
```
